32 devices in a mesh: seq: 8 (over y, x, core), rep: 4 (over z).
Axes of the slice: x: 2, y: 2, z: 4, core: 2. Of those that a mesh axis runs over, the one named last changes fastest.
Arguments:
- inputs: bfloat16 [4, 8192, 768], P('rep', 'seq'), may hold values from -6 to 6
- item_kind: int32 [4, 8], P('rep'), may hold values from 0 to 2, as said below
- perm_two: int32 [12, 2], replicated, may hold values from 0 to 1, each once within a row
- perm_three: int32 [12, 3], replicated, may hold values from 0 to 2, each once within a row
- qkv_weight: bfloat16 [3, 768, 768], P(None, ('seq', 'rep')), may hold values from -0.21875 to 0.21875
- qv_bias: bfloat16 [2, 768], P(None, ('seq', 'rep')), may hold values from -0.29882812 to 0.29882812
- out_weight: bfloat16 [768, 768], P(('seq', 'rep')), may hold values from -1.75 to 1.75
- out_bias: bfloat16 [768], P(('seq', 'rep')), may hold values from -1.796875 to 1.796875
- up_weight: bfloat16 [768, 3072], P(('seq', 'rep')), may hold values from -0.21875 to 0.21875
- up_bias: bfloat16 [3072], P(('seq', 'rep')), may hold values from -1.796875 to 1.796875
- down_weight: bfloat16 [3072, 768], P(('seq', 'rep')), may hold values from -0.109375 to 0.109375
- down_bias: bfloat16 [768], P(('seq', 'rep')), may hold values from -1.796875 to 1.796875
- norm_gain: bfloat16 [2, 768], P(None, ('seq', 'rep')), may hold values from 0.5 to 1.5
- norm_bias: bfloat16 [2, 768], P(None, ('seq', 'rep')), may hold values from -1.796875 to 1.796875
- cotangent: bfloat16 [4, 4096, 768], P('rep', 'seq'), may hold values from -6 to 6
Outputs:
- output: bfloat16 [4, 4096, 768], P('rep', 'seq')
- input_grad: float32 [4, 8192, 768], P('rep', 'seq')
- qkv_weight_grad: float32 [3, 768, 768], P(None, ('seq', 'rep'))
- qv_bias_grad: float32 [2, 768], P(None, ('seq', 'rep'))
- out_weight_grad: float32 [768, 768], P(('seq', 'rep'))
- out_bias_grad: float32 [768], P(('seq', 'rep'))
- up_weight_grad: float32 [768, 3072], P(('seq', 'rep'))
- up_bias_grad: float32 [3072], P(('seq', 'rep'))
- down_weight_grad: float32 [3072, 768], P(('seq', 'rep'))
- down_bias_grad: float32 [768], P(('seq', 'rep'))
- norm_gain_grad: float32 [2, 768], P(None, ('seq', 'rep'))
- norm_bias_grad: float32 [2, 768], P(None, ('seq', 'rep'))
The draws below stay inside these ranges and needn't reach their ends.
Inputs may be any that keep to these rules, and one draw needn't show every extreme that they name: `item_kind`: in each group exactly 4 devices hold a three-block item of 768 tokens and 1 devices a two-block item of 1024 tokens; the others hold none. `perm_two`: each row is a permutation of the two block numbers. `perm_three`: each row is a permutation of the three block numbers.
All inputs are finite; a program needn't handle non-finite values.
Results may differ from the reference program's by a relative error of at most 0.013.
Values may be sent and summed in bfloat16 or wider, within the bound.
No kernel may reach another device: no remote copies, remote signals or barrier semaphores. Data moves between devices by JAX's collectives and lax.ppermute only.
A program may use at most 192 MiB of HBM per device.

```python
import jax
import jax.numpy as jnp
from jax import lax

D = 768
H = 12
HD = 64
FF = 3072
UNIT = 256
ATT_DEV = 1024
TOK_DEV = 512
SLOTS = 8192
TOKENS = 4096
GROUPS = 4
N_SEQ = 8


def draw_item_kind(key, part):
    three_count = N_SEQ // 2
    two_count = N_SEQ // 8
    pattern = jnp.concatenate([jnp.ones((three_count,), jnp.int32), jnp.full((two_count,), 2, jnp.int32), jnp.zeros((N_SEQ - three_count - two_count,), jnp.int32)])
    group_keys = jax.random.split(key, GROUPS)

    def shuffled(one_key):
        return jax.random.permutation(one_key, pattern)
    return jax.vmap(shuffled)(group_keys)


def steps_of(key, shape, cuts, smallest, high):
    def one(axis_at, parts):
        draws = jax.random.uniform(jax.random.fold_in(jax.random.fold_in(key, 6), axis_at), (parts,), jnp.float32, smallest / len(cuts), high / len(cuts))
        return jnp.repeat(jnp.exp(draws), shape[axis_at] // parts).reshape((-1,) + (1,) * (len(shape) - axis_at - 1))

    gain = one(*cuts[0])
    for cut in cuts[1:]:
        gain = gain * one(*cut)
    return gain


def scatter_about(own_key, extent, scale, limit, cuts=(), kind=jnp.bfloat16):
    level = steps_of(own_key, extent, cuts, -0.22, 0.18) if cuts else 1.0
    entries = jax.random.normal(own_key, extent, jnp.float32) * scale * level
    return jnp.minimum(jnp.maximum(entries, -limit), limit).astype(kind)


def setup_inputs(seed: int = 0) -> dict:
    key_of = jax.random.split(jax.random.key(seed), 16)
    return {
        "inputs": scatter_about(key_of[0], (GROUPS, SLOTS, D), 1.0, 6.0, ((0, 4), (1, 8))),
        "item_kind": draw_item_kind(jax.random.fold_in(key_of[15], 71), 0),
        "perm_two": jax.vmap(lambda own: jax.random.permutation(own, 2))(jax.random.split(key_of[2], H)).reshape((H, 2)).astype(jnp.int32),
        "perm_three": jax.vmap(lambda own: jax.random.permutation(own, 3))(jax.random.split(key_of[3], H)).reshape((H, 3)).astype(jnp.int32),
        "qkv_weight": scatter_about(key_of[4], (3, D, D), D ** -0.5, 0.21875, ((1, 32),)),
        "qv_bias": scatter_about(key_of[5], (2, D), 0.05, 0.29882812, ((1, 32),)),
        "out_weight": scatter_about(key_of[6], (D, D), (D // 64) ** -0.5, 1.75, ((0, 32),)),
        "out_bias": scatter_about(key_of[7], (D,), 0.3, 1.796875, ((0, 32),)),
        "up_weight": scatter_about(key_of[8], (D, FF), D ** -0.5, 0.21875, ((0, 32),)),
        "up_bias": scatter_about(key_of[9], (FF,), 0.3, 1.796875, ((0, 32),)),
        "down_weight": scatter_about(key_of[10], (FF, D), FF ** -0.5, 0.109375, ((0, 32),)),
        "down_bias": scatter_about(key_of[11], (D,), 0.3, 1.796875, ((0, 32),)),
        "norm_gain": jnp.clip(1.0 + 0.1 * jax.random.normal(key_of[12], (2, D), jnp.float32), 0.5, 1.5).astype(jnp.bfloat16),
        "norm_bias": scatter_about(key_of[13], (2, D), 0.3, 1.796875, ((1, 32),)),
        "cotangent": scatter_about(key_of[14], (GROUPS, TOKENS, D), 1.0, 6.0, ((0, 4), (1, 8))),
    }


@jax.custom_vjp
def low(v):
    return lax.optimization_barrier(v.astype(jnp.bfloat16)).astype(jnp.float32)

@jax.custom_vjp
def low_back(v):
    return v

def low_keep(v):
    return (low(v), None)

def low_pass(kept, grad):
    return (grad,)

def back_keep(v):
    return (v, None)

def back_low(kept, grad):
    return (low(grad),)
low.defvjp(low_keep, low_pass)
low_back.defvjp(back_keep, back_low)
EPSILON = 1e-05
MASKED = -1000000000.0

def norm_rows(values, gain_row, shift_row):
    center = values - lax.optimization_barrier(jnp.mean(values, axis=-1, keepdims=True))
    spread = lax.optimization_barrier(jnp.mean(center * center, axis=-1, keepdims=True))
    return center * lax.rsqrt(spread + EPSILON) * gain_row + shift_row

def key_tables(kind, perm_two, perm_three):
    quarters = jnp.arange(4)
    halves = quarters // 2
    pick_two = lax.optimization_barrier(jnp.sum(jnp.where(halves[None, :, None] == jnp.arange(2)[None, None, :], perm_two[:, None, :], 0), axis=-1))
    pick_three = lax.optimization_barrier(jnp.sum(jnp.where(jnp.minimum(quarters, 2)[None, :, None] == jnp.arange(3)[None, None, :], perm_three[:, None, :], 0), axis=-1))
    first_unit = jnp.where(kind == 2, 2 * pick_two, pick_three)
    second_unit = jnp.where(kind == 2, 2 * pick_two + 1, pick_three)
    first_pick = first_unit[:, :, None] == quarters[None, None, :]
    second_pick = second_unit[:, :, None] == quarters[None, None, :]
    return (first_pick, second_pick, kind == 2)

def attend(proj, kind, perm_two, perm_three):
    slot_count = proj.shape[0]
    quarter = slot_count // 4
    pieces = proj.reshape(4, quarter, 3, H, HD)
    first_pick, second_pick, both_live = key_tables(kind, perm_two, perm_three)
    first_pick = first_pick.astype(jnp.float32)
    second_pick = second_pick.astype(jnp.float32)
    key_live = (jnp.arange(2 * quarter) < quarter) | both_live
    score_scale = HD ** (-0.5)
    highest = lax.Precision.HIGHEST

    def one_block(which):
        key_block = jnp.concatenate([jnp.einsum('hw,wkhd->hkd', first_pick[:, which], pieces[:, :, 1], precision=highest), jnp.einsum('hw,wkhd->hkd', second_pick[:, which], pieces[:, :, 1], precision=highest)], axis=1)
        value_block = jnp.concatenate([jnp.einsum('hw,wkhd->hkd', first_pick[:, which], pieces[:, :, 2], precision=highest), jnp.einsum('hw,wkhd->hkd', second_pick[:, which], pieces[:, :, 2], precision=highest)], axis=1)
        raw = jnp.einsum('qhd,hkd->hqk', pieces[which, :, 0], key_block, precision=highest)
        scores = jnp.where(key_live[None, None, :], low_back(raw * score_scale), MASKED)
        probs = low(jax.nn.softmax(scores, axis=-1))
        blended = jnp.einsum('hqk,hkd->qhd', probs, value_block, precision=highest)
        return blended.reshape(quarter, H * HD)
    blocks = lax.map(jax.checkpoint(one_block), jnp.arange(4))
    return blocks.reshape(slot_count, H * HD)

def balanced_rows(item_kind):
    group_count = item_kind.shape[0]
    per_pair = jnp.where(item_kind == 2, 4 * UNIT, jnp.where(item_kind == 1, 3 * UNIT, 0)) // N_SEQ
    range_ends = jnp.cumsum(per_pair, axis=1)
    range_starts = range_ends - per_pair
    positions = jnp.arange(TOK_DEV)
    sources = lax.optimization_barrier(jnp.sum((range_ends[:, None, :] <= positions[None, :, None]).astype(jnp.int32), axis=-1))
    opening = lax.optimization_barrier(jnp.sum(jnp.where(jnp.arange(N_SEQ)[None, None, :] == sources[:, :, None], range_starts[:, None, :], 0), axis=-1))
    levels = positions[None, :] - opening
    devices = jnp.arange(N_SEQ)
    rows = jnp.arange(group_count)[:, None, None] * SLOTS + sources[:, None, :] * ATT_DEV + levels[:, None, :] * N_SEQ + devices[None, :, None]
    return rows.reshape(-1).astype(jnp.int32)

def reference(inputs, item_kind, perm_two, perm_three, qkv_weight, qv_bias, out_weight, out_bias, up_weight, up_bias, down_weight, down_bias, norm_gain, norm_bias, cotangent):
    group_count = inputs.shape[0]
    order = balanced_rows(item_kind)
    flat_kind = item_kind.reshape(-1)
    highest = lax.Precision.HIGHEST

    def forward(rows, qkv_w, qv_b, out_w, out_b, up_w, up_b, down_w, down_b, gains, shifts):
        flat_rows = rows.reshape(-1, D)
        bias_rows = jnp.stack([qv_b[0], jnp.zeros((D,), jnp.float32), qv_b[1]])
        proj = jnp.einsum('nd,kde->nke', flat_rows, qkv_w, precision=highest) + bias_rows
        proj = low_back(low(proj))
        per_device = proj.reshape(group_count * N_SEQ, ATT_DEV, 3, D)

        def device_heads(pack):
            return attend(pack[0], pack[1], perm_two, perm_three)
        heads = lax.map(device_heads, (per_device, flat_kind)).reshape(-1, D)
        heads = low_back(low(heads))
        branch = low_back(jnp.dot(heads, out_w, precision=highest) + out_b)
        normed = norm_rows(flat_rows + branch, gains[0], shifts[0])
        moved = normed[order]
        pre = low_back(jnp.dot(low(moved), up_w, precision=highest) + up_b)
        active = low(jax.nn.gelu(pre, approximate=False))
        ffn_out = low_back(jnp.dot(active, down_w, precision=highest) + down_b)
        result = norm_rows(moved + ffn_out, gains[1], shifts[1])
        return result.reshape(group_count, TOKENS, D)
    result, pull_back = jax.vjp(forward, inputs.astype(jnp.float32), qkv_weight.astype(jnp.float32), qv_bias.astype(jnp.float32), out_weight.astype(jnp.float32), out_bias.astype(jnp.float32), up_weight.astype(jnp.float32), up_bias.astype(jnp.float32), down_weight.astype(jnp.float32), down_bias.astype(jnp.float32), norm_gain.astype(jnp.float32), norm_bias.astype(jnp.float32))
    grads = pull_back(cotangent.astype(jnp.float32))
    return (result.astype(jnp.bfloat16), grads[0], grads[1], grads[2], grads[3], grads[4], grads[5], grads[6], grads[7], grads[8], grads[9], grads[10])
```

```python
import jax
import jax.numpy as jnp
from jax import lax
from jax.experimental import pallas as pl
from jax.experimental.pallas import tpu as pltpu
from jax.sharding import PartitionSpec as P

HD = 64
UNIT = 256
EPSILON = 1e-05
BF = jnp.bfloat16
F32 = jnp.float32
AXES = ("seq", "rep")
MIB = 1 << 20

ERFC_P = 0.43
ERFC_C = (
    0.24253869020822919,
    0.24398891668429604,
    0.20746674190096287,
    0.23821815491943954,
    -0.06883736466334416,
    0.3647550688015456,
    -0.29904310037103493,
    0.0709127131994358,
)
RSQRT2 = 0.7071067811865476
RSQRT2PI = 0.3989422804014327


def nn(a, b):
    return lax.dot_general(a, b, (((1,), (0,)), ((), ())), preferred_element_type=F32)


def nt(a, b):
    return lax.dot_general(a, b, (((1,), (1,)), ((), ())), preferred_element_type=F32)


def tn(a, b):
    return lax.dot_general(a, b, (((0,), (0,)), ((), ())), preferred_element_type=F32)


def gelu_parts(x):
    u = jnp.abs(x) * RSQRT2
    t = 1.0 / (1.0 + ERFC_P * u)
    poly = jnp.full_like(t, ERFC_C[-1])
    for c in ERFC_C[-2::-1]:
        poly = poly * t + c
    bell = jnp.exp(-0.5 * x * x)
    tail = 0.5 * poly * t * bell
    phi = jnp.where(x >= 0, 1.0 - tail, tail)
    return x * phi, phi + x * (bell * RSQRT2PI)


def attend_forward_kernel(tab_ref, x_ref, w_ref, b_ref, qkv_ref, heads_ref):
    group = pl.program_id(0)
    kind = tab_ref[0]
    width = w_ref.shape[2]
    slots = x_ref.shape[0]
    low = lax.broadcasted_iota(jnp.int32, (UNIT, 2 * HD), 1) < HD

    def project(n, bias, scale):
        for r in range(0, slots, UNIT):
            acc = nn(x_ref[r : r + UNIT, :], w_ref[n])
            if bias is not None:
                acc = acc + bias
            acc = acc.astype(BF)
            if scale is not None:
                acc = acc * jnp.asarray(scale, BF)
            qkv_ref[n, r : r + UNIT, :] = acc

    project(0, b_ref[0:1, :], HD**-0.5)
    project(1, None, None)
    project(2, b_ref[1:2, :], None)

    def units(which, keys):
        for pair in range(width // (2 * HD)):
            lanes = slice(pair * 2 * HD, (pair + 1) * 2 * HD)
            rows = pl.ds(pl.multiple_of(which * UNIT, UNIT), UNIT)
            query = qkv_ref[0, rows, lanes]
            blended = []
            for side in range(2):
                head = group * (width // HD) + pair * 2 + side
                first = tab_ref[1 + head * 4 + which]
                key_rows = pl.ds(pl.multiple_of(first * UNIT, UNIT), keys)
                own = jnp.where(low if side == 0 else ~low, query, jnp.zeros((), BF))
                scores = nt(own, qkv_ref[1, key_rows, lanes])
                largest = jnp.max(scores, axis=-1, keepdims=True)
                expon = jnp.exp(scores - largest)
                total = jnp.sum(expon, axis=-1, keepdims=True)
                probs = (expon * (1.0 / total)).astype(BF)
                blended.append(nn(probs, qkv_ref[2, key_rows, lanes]))
            heads_ref[rows, lanes] = jnp.where(low, blended[0], blended[1]).astype(BF)

    @pl.when(kind == 2)
    def _():
        lax.fori_loop(0, 4, lambda w, c: (units(w, 2 * UNIT), c)[1], 0)

    @pl.when(kind == 1)
    def _():
        lax.fori_loop(0, 3, lambda w, c: (units(w, UNIT), c)[1], 0)
        heads_ref[3 * UNIT :, :] = jnp.zeros((slots - 3 * UNIT, width), BF)

    @pl.when(kind == 0)
    def _():
        heads_ref[...] = jnp.zeros_like(heads_ref)


def attend_forward(table, x, qkv_w, vectors):
    slots, features = x.shape
    width = 4 * HD
    grid_spec = pltpu.PrefetchScalarGridSpec(
        num_scalar_prefetch=1,
        grid=(features // width,),
        in_specs=[
            pl.BlockSpec((slots, features), lambda g, t: (0, 0)),
            pl.BlockSpec((3, features, width), lambda g, t: (0, 0, g)),
            pl.BlockSpec((16, width), lambda g, t: (0, g)),
        ],
        out_specs=[
            pl.BlockSpec((3, slots, width), lambda g, t: (0, 0, g)),
            pl.BlockSpec((slots, width), lambda g, t: (0, g)),
        ],
    )
    return pl.pallas_call(
        attend_forward_kernel,
        out_shape=(
            jax.ShapeDtypeStruct((3, slots, features), BF),
            jax.ShapeDtypeStruct((slots, features), BF),
        ),
        grid_spec=grid_spec,
        name="attend_forward",
        compiler_params=pltpu.CompilerParams(
            dimension_semantics=("arbitrary",), vmem_limit_bytes=48 * MIB
        ),
    )(table, x, qkv_w, vectors)


def norm_forward(z):
    center = z - jnp.mean(z, axis=-1, keepdims=True)
    spread = jnp.mean(center * center, axis=-1, keepdims=True)
    scale = lax.rsqrt(spread + EPSILON)
    return center * scale, scale


def norm_backward(gx, xhat, scale):
    return (
        gx
        - jnp.mean(gx, axis=-1, keepdims=True)
        - xhat * jnp.mean(gx * xhat, axis=-1, keepdims=True)
    ) * scale


def rows_kernel(
    tab_ref,
    heads_ref,
    x_ref,
    cot_ref,
    ow_ref,
    uw_ref,
    dw_ref,
    vec_ref,
    out_ref,
    act_ref,
    gpre_ref,
    nlow_ref,
    gffn_ref,
    gres_ref,
    gbranch_ref,
    gheads_ref,
    terms_ref,
    slope_ref,
):
    tile = pl.program_id(0)
    kind = tab_ref[0]
    live = jnp.where(kind == 2, 4, jnp.where(kind == 1, 3, 0))
    features = x_ref.shape[1]
    hidden = uw_ref.shape[1]
    chunks = [slice(c, c + features) for c in range(0, hidden, features)]

    @pl.when(tile == 0)
    def _():
        terms_ref[...] = jnp.zeros_like(terms_ref)

    @pl.when(tile >= live)
    def _():
        for ref in (out_ref, act_ref, gpre_ref, nlow_ref, gffn_ref, gres_ref, gbranch_ref, gheads_ref):
            ref[...] = jnp.zeros_like(ref)

    @pl.when(tile < live)
    def _():
        def vec(i):
            return vec_ref[i : i + 1, :]

        def add(i, value):
            terms_ref[i : i + 1, :] += jnp.sum(value, axis=0, keepdims=True)

        z1 = x_ref[...].astype(F32) + nn(heads_ref[...], ow_ref[...]) + vec(2)
        xhat1, scale1 = norm_forward(z1)
        normed = xhat1 * vec(8) + vec(10)
        nlow = normed.astype(BF)
        nlow_ref[...] = nlow
        ffn = jnp.zeros_like(normed)
        for i, c in enumerate(chunks):
            pre = nn(nlow, uw_ref[:, c]) + vec(3 + i)
            active, slope = gelu_parts(pre)
            active = active.astype(BF)
            act_ref[:, c] = active
            slope_ref[:, c] = slope
            ffn = ffn + nn(active, dw_ref[c, :])
        z2 = normed + ffn + vec(7)
        xhat2, scale2 = norm_forward(z2)
        out_ref[...] = (xhat2 * vec(9) + vec(11)).astype(BF)
        cot = cot_ref[...].astype(F32)
        add(9, cot * xhat2)
        add(11, cot)
        gres2 = norm_backward(cot * vec(9), xhat2, scale2)
        gffn = gres2.astype(BF)
        gffn_ref[...] = gffn
        add(7, gffn.astype(F32))
        gmoved = gres2
        for i, c in enumerate(chunks):
            gactive = nt(gffn, dw_ref[c, :])
            gpre = (gactive * slope_ref[:, c]).astype(BF)
            gpre_ref[:, c] = gpre
            add(3 + i, gpre.astype(F32))
            gmoved = gmoved + nt(gpre, uw_ref[:, c])
        add(8, gmoved * xhat1)
        add(10, gmoved)
        gres1 = norm_backward(gmoved * vec(8), xhat1, scale1)
        gres_ref[...] = gres1
        gbranch = gres1.astype(BF)
        gbranch_ref[...] = gbranch
        add(2, gbranch.astype(F32))
        gheads_ref[...] = nt(gbranch, ow_ref[...]).astype(BF)


def rows_both_ways(table, heads, x, cot, out_w, up_w, down_w, vectors):
    slots, features = x.shape
    hidden = up_w.shape[1]

    def tile(width):
        return pl.BlockSpec((UNIT, width), lambda i, t: (i, 0))

    def whole(shape):
        return pl.BlockSpec(shape, lambda i, t: (0, 0), pipeline_mode=pl.Buffered(1))

    narrow = jax.ShapeDtypeStruct((slots, features), BF)
    wide = jax.ShapeDtypeStruct((slots, hidden), BF)
    grid_spec = pltpu.PrefetchScalarGridSpec(
        num_scalar_prefetch=1,
        grid=(slots // UNIT,),
        in_specs=[
            tile(features),
            tile(features),
            tile(features),
            whole(out_w.shape),
            whole(up_w.shape),
            whole(down_w.shape),
            whole(vectors.shape),
        ],
        out_specs=[
            tile(features),
            tile(hidden),
            tile(hidden),
            tile(features),
            tile(features),
            tile(features),
            tile(features),
            tile(features),
            pl.BlockSpec((16, features), lambda i, t: (0, 0)),
        ],
        scratch_shapes=[pltpu.VMEM((UNIT, hidden), F32)],
    )
    return pl.pallas_call(
        rows_kernel,
        out_shape=(
            narrow,
            wide,
            wide,
            narrow,
            narrow,
            jax.ShapeDtypeStruct((slots, features), F32),
            narrow,
            narrow,
            jax.ShapeDtypeStruct((16, features), F32),
        ),
        grid_spec=grid_spec,
        name="rows_both_ways",
        compiler_params=pltpu.CompilerParams(
            dimension_semantics=("arbitrary",), vmem_limit_bytes=56 * MIB
        ),
    )(table, heads, x, cot, out_w, up_w, down_w, vectors)


def attend_backward_kernel(tab_ref, qkv_ref, gh_ref, xt_ref, g_ref, gw_ref, gb_ref, dk_ref, dv_ref):
    group = pl.program_id(0)
    kind = tab_ref[0]
    slots, width = gh_ref.shape
    low = lax.broadcasted_iota(jnp.int32, (UNIT, 2 * HD), 1) < HD

    dk_ref[...] = jnp.zeros_like(dk_ref)
    dv_ref[...] = jnp.zeros_like(dv_ref)

    def units(which, keys):
        for pair in range(width // (2 * HD)):
            lanes = slice(pair * 2 * HD, (pair + 1) * 2 * HD)
            rows = pl.ds(pl.multiple_of(which * UNIT, UNIT), UNIT)
            query = qkv_ref[0, rows, lanes]
            gout = gh_ref[rows, lanes]
            gquery = []
            for side in range(2):
                head = group * (width // HD) + pair * 2 + side
                first = tab_ref[1 + head * 4 + which]
                key_rows = pl.ds(pl.multiple_of(first * UNIT, UNIT), keys)
                mine = low if side == 0 else ~low
                own = jnp.where(mine, query, jnp.zeros((), BF))
                gown = jnp.where(mine, gout, jnp.zeros((), BF))
                key = qkv_ref[1, key_rows, lanes]
                value = qkv_ref[2, key_rows, lanes]
                scores = nt(key, own)
                expon = jnp.exp(scores - jnp.max(scores, axis=0, keepdims=True))
                probs = expon * (1.0 / jnp.sum(expon, axis=0, keepdims=True))
                gprobs = nt(value, gown)
                inner = jnp.sum(gprobs * probs, axis=0, keepdims=True)
                gscores = (probs * (gprobs - inner)).astype(BF)
                dv_ref[key_rows, lanes] += nn(probs.astype(BF), gown)
                dk_ref[key_rows, lanes] += nn(gscores, own)
                gquery.append(tn(gscores, key))
            g_ref[0, rows, lanes] = (jnp.where(low, gquery[0], gquery[1]) * HD**-0.5).astype(BF)

    @pl.when(kind == 2)
    def _():
        lax.fori_loop(0, 4, lambda w, c: (units(w, 2 * UNIT), c)[1], 0)

    @pl.when(kind == 1)
    def _():
        lax.fori_loop(0, 3, lambda w, c: (units(w, UNIT), c)[1], 0)
        g_ref[0, 3 * UNIT :, :] = jnp.zeros((slots - 3 * UNIT, width), BF)

    @pl.when(kind == 0)
    def _():
        g_ref[0] = jnp.zeros((slots, width), BF)

    g_ref[1] = dk_ref[...].astype(BF)
    g_ref[2] = dv_ref[...].astype(BF)
    gb_ref[...] = jnp.zeros_like(gb_ref)
    gb_ref[0:1, :] = jnp.sum(g_ref[0].astype(F32), axis=0, keepdims=True)
    gb_ref[1:2, :] = jnp.sum(g_ref[2].astype(F32), axis=0, keepdims=True)
    for n in range(3):
        gw_ref[n] = nn(xt_ref[...], g_ref[n]).astype(BF)


def attend_backward(table, qkv, gheads, xt):
    _, slots, features = qkv.shape
    width = 4 * HD
    grid_spec = pltpu.PrefetchScalarGridSpec(
        num_scalar_prefetch=1,
        grid=(features // width,),
        in_specs=[
            pl.BlockSpec((3, slots, width), lambda g, t: (0, 0, g)),
            pl.BlockSpec((slots, width), lambda g, t: (0, g)),
            pl.BlockSpec((features, slots), lambda g, t: (0, 0)),
        ],
        out_specs=[
            pl.BlockSpec((3, slots, width), lambda g, t: (0, 0, g)),
            pl.BlockSpec((3, features, width), lambda g, t: (0, 0, g)),
            pl.BlockSpec((8, width), lambda g, t: (0, g)),
        ],
        scratch_shapes=[pltpu.VMEM((slots, width), F32), pltpu.VMEM((slots, width), F32)],
    )
    return pl.pallas_call(
        attend_backward_kernel,
        out_shape=(
            jax.ShapeDtypeStruct((3, slots, features), BF),
            jax.ShapeDtypeStruct((3, features, features), BF),
            jax.ShapeDtypeStruct((8, features), F32),
        ),
        grid_spec=grid_spec,
        name="attend_backward",
        compiler_params=pltpu.CompilerParams(
            dimension_semantics=("arbitrary",), vmem_limit_bytes=48 * MIB
        ),
    )(table, qkv, gheads, xt)


def swapped(parts, index):
    bit = 1
    while bit < len(parts):
        flip = (index & bit) != 0
        parts = [jnp.where(flip, parts[j ^ bit], parts[j]) for j in range(len(parts))]
        bit *= 2
    return parts


def seq_swap(x, k):
    n = lax.axis_size("seq")
    return lax.ppermute(x, "seq", [(i, i ^ k) for i in range(n)])


def rep_swap(x, k):
    n = lax.axis_size("rep")
    return lax.ppermute(x, "rep", [(i, i ^ k) for i in range(n)])


def key_table(own_kind, perm_two, perm_three):
    quarters = jnp.arange(4)
    halves = quarters // 2
    pick_two = jnp.sum(
        jnp.where(halves[None, :, None] == jnp.arange(2)[None, None, :], perm_two[:, None, :], 0),
        axis=-1,
    )
    pick_three = jnp.sum(
        jnp.where(
            jnp.minimum(quarters, 2)[None, :, None] == jnp.arange(3)[None, None, :],
            perm_three[:, None, :],
            0,
        ),
        axis=-1,
    )
    first = jnp.where(own_kind == 2, 2 * pick_two, pick_three)
    return jnp.concatenate([own_kind.reshape(1), first.reshape(-1)]).astype(jnp.int32)


def placed(vector, rows, offset, features):
    lane = lax.broadcasted_iota(jnp.int32, (vector.shape[-1], features), 1)
    entry = lax.broadcasted_iota(jnp.int32, (vector.shape[-1], features), 0)
    return jnp.dot(vector, (lane == entry + offset).astype(BF), preferred_element_type=F32)


def shards(
    inputs,
    item_kind,
    perm_two,
    perm_three,
    qkv_weight,
    qv_bias,
    out_weight,
    out_bias,
    up_weight,
    up_bias,
    down_weight,
    down_bias,
    norm_gain,
    norm_bias,
    cotangent,
):
    peers = lax.axis_size("seq")
    copies = lax.axis_size("rep")
    seq = lax.axis_index("seq")
    rep = lax.axis_index("rep")
    x = inputs[0]
    slots, features = x.shape
    tokens = cotangent.shape[1]
    hidden = up_weight.shape[1]
    quarter = slots // 4
    per_peer = slots // peers
    staged = peers == 8 and copies == 4
    own = out_weight.shape[0]

    kind_row = item_kind[0]
    own_kind = jnp.sum(jnp.where(jnp.arange(peers) == seq, kind_row, 0))
    table = key_table(own_kind, perm_two, perm_three)

    per_pair = (
        jnp.where(kind_row == 2, 4 * quarter, jnp.where(kind_row == 1, 3 * quarter, 0)) // peers
    )
    earlier = jnp.arange(peers)[:, None] <= jnp.arange(peers)[None, :]
    range_ends = jnp.sum(jnp.where(earlier, per_pair[:, None], 0), axis=0)
    range_starts = range_ends - per_pair
    positions = jnp.arange(tokens)
    sources = jnp.sum((range_ends[None, :] <= positions[:, None]).astype(jnp.int32), axis=1)
    opening = jnp.sum(
        jnp.where(jnp.arange(peers)[None, :] == sources[:, None], range_starts[None, :], 0), axis=1
    )
    arrivals = (positions - opening) * peers + sources
    levels = jnp.arange(per_peer)[:, None]
    filled = levels < per_pair[None, :]
    targets = jnp.minimum(range_starts[None, :] + levels, tokens - 1)

    if staged:
        core, plane = seq & 1, seq >> 1

        def along_rep(piece):
            return jnp.stack(swapped([piece] + [rep_swap(piece, k) for k in (1, 2, 3)], rep))

        def along_plane(piece):
            return swapped([piece] + [seq_swap(piece, 2 * k) for k in (1, 2, 3)], plane)

        def along_core(piece):
            return swapped([piece, seq_swap(piece, 1)], core)

        index = seq * copies + rep
        small = jnp.concatenate([qv_bias, out_bias[None], down_bias[None], norm_gain, norm_bias])
        small = placed(small, 8, index * own, features)
        fan = 4 * own
        up_row = (index * fan) // features
        spread = placed(up_bias[None], 1, index * fan - up_row * features, features)
        spread = jnp.where(jnp.arange(4)[:, None] == up_row, spread, 0.0)
        vectors = jnp.concatenate(
            [small[0:3], spread, small[3:8], jnp.zeros((4, features), F32)]
        ).astype(BF)

        qkv_z = along_rep(qkv_weight.reshape(3 * own, features))
        vec_z = vectors.astype(F32)
        for k in (1, 2, 3):
            vec_z = vec_z + rep_swap(vectors, k).astype(F32)
        first = jnp.concatenate([qkv_z.reshape(-1, features), vec_z.astype(BF)])
        planes = along_plane(first)
        vec_xy = sum(p[-16:].astype(F32) for p in planes).astype(BF)
        body = jnp.stack([p[:-16] for p in planes])
        cores = along_core(body)
        vectors = vec_xy.astype(F32) + seq_swap(vec_xy, 1).astype(F32)

        def whole(cores, rows):
            both = jnp.stack([c.reshape(4, 4, rows, features) for c in cores], axis=1)
            return both

        qkv_all = whole(cores, 3 * own).reshape(4, 2, 4, 3, own, features)
        qkv_w = qkv_all.transpose(3, 0, 1, 2, 4, 5).reshape(3, features, features)

        second = jnp.concatenate(
            [out_weight] + [up_weight[:, c : c + features] for c in range(0, hidden, features)]
        )
        second = jnp.stack(along_plane(along_rep(second)))
        second = whole(along_core(second), 5 * own).reshape(4, 2, 4, 5, own, features)
        out_w = second[:, :, :, 0].reshape(features, features)
        up_w = jnp.concatenate(
            [second[:, :, :, 1 + j].reshape(features, features) for j in range(4)], axis=1
        )
        third = jnp.stack(along_plane(along_rep(down_weight)))
        down_w = whole(along_core(third), fan).reshape(hidden, features)
    else:
        def gathered(v, axis):
            return lax.all_gather(v, AXES, axis=axis, tiled=True)

        qkv_w = gathered(qkv_weight, 1)
        out_w = gathered(out_weight, 0)
        up_w = gathered(up_weight, 0)
        down_w = gathered(down_weight, 0)
        qv_b = gathered(qv_bias, 1)
        vectors = jnp.concatenate(
            [
                qv_b,
                gathered(out_bias, 0)[None],
                gathered(up_bias, 0).reshape(4, features),
                gathered(down_bias, 0)[None],
                gathered(norm_gain, 1),
                gathered(norm_bias, 1),
                jnp.zeros((4, features), BF),
            ]
        ).astype(F32)

    picked = jnp.where(filled[:, :, None], cotangent[0][targets], jnp.zeros((), BF))
    cot = lax.all_to_all(picked, "seq", split_axis=1, concat_axis=1, tiled=True)
    cot = cot.reshape(slots, features)

    qkv, heads = attend_forward(table, x, qkv_w, vectors)
    out, act, gpre, nlow, gffn, gres, gbranch, gheads, terms = rows_both_ways(
        table, heads, x, cot, out_w, up_w, down_w, vectors
    )

    moved = lax.all_to_all(
        out.reshape(per_peer, peers, features), "seq", split_axis=1, concat_axis=1, tiled=True
    )
    output = moved.reshape(slots, features)[arrivals]

    down_grad = tn(act, gffn).astype(BF)
    up_grad = tn(nlow, gpre).astype(BF)
    out_grad = tn(heads, gbranch).astype(BF)
    grads, qkv_grad, bias_terms = attend_backward(table, qkv, gheads, x.T)
    terms = jnp.concatenate([bias_terms[0:2], terms[2:]])

    if staged:
        def scattered(grad, rows, extra=None):
            grad = grad.reshape(4, 2, 4, rows, features)
            mine = jnp.where(core == 0, grad[:, 0], grad[:, 1]).astype(BF)
            other = jnp.where(core == 0, grad[:, 1], grad[:, 0]).astype(BF)
            got = seq_swap(other, 1)
            half = (mine.astype(F32) + got.astype(F32)).astype(BF)
            if extra is not None:
                extra = extra + seq_swap(extra.astype(BF), 1).astype(F32)
            parts = swapped([half[j] for j in range(4)], plane)
            parts = [p.reshape(-1, features) for p in parts]
            if extra is not None:
                low = extra.astype(BF)
                parts = [jnp.concatenate([p, low]) for p in parts]
            total = parts[0].astype(F32)
            for k in (1, 2, 3):
                total = total + seq_swap(parts[k], 2 * k).astype(F32)
            total = total.astype(BF)
            body = total[: 4 * rows].reshape(4, rows, features)
            parts = swapped([body[j] for j in range(4)], rep)
            if extra is not None:
                parts = [jnp.concatenate([p, total[4 * rows :]]) for p in parts]
            total = parts[0].astype(F32)
            for k in (1, 2, 3):
                total = total + rep_swap(parts[k], k).astype(F32)
            return total

        down_out = scattered(down_grad, fan)
        up_out = scattered(
            jnp.stack(
                [
                    up_grad[:, c : c + features].reshape(4, 2, 4, own, features)
                    for c in range(0, hidden, features)
                ],
                axis=3,
            ),
            4 * own,
        )
        up_out = jnp.concatenate([up_out[j * own : (j + 1) * own] for j in range(4)], axis=1)
        out_out = scattered(out_grad, own)
        last = scattered(
            qkv_grad.reshape(3, 4, 2, 4, own, features).transpose(1, 2, 3, 0, 4, 5), 3 * own, terms
        )
        qkv_out = last[: 3 * own].reshape(3, own, features)
        sums = last[3 * own :]
        mine = lax.dynamic_slice(sums, (0, index * own), (16, own))
        up_bias_out = lax.dynamic_slice(
            sums, (3 + up_row, index * fan - up_row * features), (1, fan)
        )[0]
        qv_out, out_bias_out, down_bias_out = mine[0:2], mine[2], mine[7]
        gain_out, shift_out = mine[8:10], mine[10:12]
    else:
        def reduced(v, axis):
            return lax.psum_scatter(v.astype(F32), AXES, scatter_dimension=axis, tiled=True)

        down_out = reduced(down_grad, 0)
        up_out = reduced(up_grad, 0)
        out_out = reduced(out_grad, 0)
        qkv_out = reduced(qkv_grad, 1)
        qv_out = reduced(terms[0:2], 1)
        out_bias_out = reduced(terms[2], 0)
        up_bias_out = reduced(terms[3:7].reshape(hidden), 0)
        down_bias_out = reduced(terms[7], 0)
        gain_out = reduced(terms[8:10], 1)
        shift_out = reduced(terms[10:12], 1)

    input_grad = gres
    for n in range(3):
        input_grad = input_grad + nt(grads[n], qkv_w[n])
    return (
        output[None],
        input_grad[None],
        qkv_out,
        qv_out,
        out_out,
        out_bias_out,
        up_out,
        up_bias_out,
        down_out,
        down_bias_out,
        gain_out,
        shift_out,
    )


def solution(mesh):
    both = ("seq", "rep")
    in_specs = (
        P("rep", "seq", None),
        P("rep", None),
        P(),
        P(),
        P(None, both, None),
        P(None, both),
        P(both, None),
        P(both),
        P(both, None),
        P(both),
        P(both, None),
        P(both),
        P(None, both),
        P(None, both),
        P("rep", "seq", None),
    )
    out_specs = (
        P("rep", "seq", None),
        P("rep", "seq", None),
        P(None, both, None),
        P(None, both),
        P(both, None),
        P(both),
        P(both, None),
        P(both),
        P(both, None),
        P(both),
        P(None, both),
        P(None, both),
    )
    return jax.shard_map(shards, mesh=mesh, in_specs=in_specs, out_specs=out_specs, check_vma=False)
```

```python
import functools

import jax
import jax.numpy as jnp
from jax import lax
from jax.experimental import pallas as pl
from jax.experimental.pallas import tpu as pltpu
from jax.sharding import PartitionSpec as P

HD = 64
UNIT = 256
EPSILON = 1e-05
BF = jnp.bfloat16
F32 = jnp.float32
AXES = ("seq", "rep")
MIB = 1 << 20
BRIEF = pl.CostEstimate(flops=1000, transcendentals=0, bytes_accessed=1000)


def hbm(x):
    return pltpu.with_memory_space_constraint(x, pltpu.HBM)


def pinned(shape, dtype):
    return pltpu.HBM(shape, dtype)


ERFC_P = 0.43
ERFC_C = (
    0.24253869020822919,
    0.24398891668429604,
    0.20746674190096287,
    0.23821815491943954,
    -0.06883736466334416,
    0.3647550688015456,
    -0.29904310037103493,
    0.0709127131994358,
)
RSQRT2 = 0.7071067811865476
RSQRT2PI = 0.3989422804014327


def nn(a, b):
    return lax.dot_general(a, b, (((1,), (0,)), ((), ())), preferred_element_type=F32)


def nt(a, b):
    return lax.dot_general(a, b, (((1,), (1,)), ((), ())), preferred_element_type=F32)


def tn(a, b):
    return lax.dot_general(a, b, (((0,), (0,)), ((), ())), preferred_element_type=F32)


def gelu_parts(x):
    u = jnp.abs(x) * RSQRT2
    t = 1.0 / (1.0 + ERFC_P * u)
    poly = jnp.full_like(t, ERFC_C[-1])
    for c in ERFC_C[-2::-1]:
        poly = poly * t + c
    bell = jnp.exp(-0.5 * x * x)
    tail = 0.5 * poly * t * bell
    phi = jnp.where(x >= 0, 1.0 - tail, tail)
    return x * phi, phi + x * (bell * RSQRT2PI)


def start_pieces(place_ref, refs, copies, sem):
    for swap in range(2):
        for plane in range(4):
            device = (place_ref[0] >> 2) ^ (plane * 2 + swap)
            for first, rows, target in copies:
                pltpu.make_async_copy(
                    refs[swap * 4 + plane].at[pl.ds(first, rows), :], target(device), sem
                ).start()


def wait_whole(ref, sem):
    pltpu.make_async_copy(ref, ref, sem).wait()


def attend_forward_kernel(
    staged, place_ref, tab_ref, x_ref, b_ref, *refs
):
    count = 8 if staged else 1
    pieces = refs[:count]
    qkv_ref, heads_ref, keep_ref, w_ref, sem, keep_sem = refs[count:]
    group = pl.program_id(0)
    kind = tab_ref[0]
    slots, width = heads_ref.shape
    features = x_ref.shape[1]
    low = lax.broadcasted_iota(jnp.int32, (UNIT, 2 * HD), 1) < HD
    keep = pltpu.make_async_copy(w_ref, keep_ref, keep_sem)

    @pl.when(group == 0)
    def _():
        if staged:
            rows = features // 8

            def target(n):
                return lambda d: w_ref.at[n, pl.ds(pl.multiple_of(d * rows, 32), rows), :]

            start_pieces(
                place_ref, pieces, [(n * rows, rows, target(n)) for n in range(3)], sem
            )
        else:
            pltpu.make_async_copy(pieces[0], w_ref, sem).start()
        wait_whole(w_ref, sem)
        keep.start()

    @pl.when(group == pl.num_programs(0) - 1)
    def _():
        keep.wait()

    cols = pl.ds(pl.multiple_of(group * width, width), width)

    def project(n, bias, scale):
        weight = w_ref[n, :, cols]
        for r in range(0, slots, UNIT):
            acc = nn(x_ref[r : r + UNIT, :], weight)
            if bias is not None:
                acc = acc + bias
            acc = acc.astype(BF)
            if scale is not None:
                acc = acc * jnp.asarray(scale, BF)
            qkv_ref[n, r : r + UNIT, :] = acc

    project(0, b_ref[0:1, :], HD**-0.5)
    project(1, None, None)
    project(2, b_ref[1:2, :], None)

    def units(which, keys):
        for pair in range(width // (2 * HD)):
            lanes = slice(pair * 2 * HD, (pair + 1) * 2 * HD)
            rows = pl.ds(pl.multiple_of(which * UNIT, UNIT), UNIT)
            query = qkv_ref[0, rows, lanes]
            blended = []
            for side in range(2):
                head = group * (width // HD) + pair * 2 + side
                first = tab_ref[1 + head * 4 + which]
                key_rows = pl.ds(pl.multiple_of(first * UNIT, UNIT), keys)
                own = jnp.where(low if side == 0 else ~low, query, jnp.zeros((), BF))
                scores = nt(own, qkv_ref[1, key_rows, lanes])
                largest = jnp.max(scores, axis=-1, keepdims=True)
                expon = jnp.exp(scores - largest)
                total = jnp.sum(expon, axis=-1, keepdims=True)
                probs = (expon * (1.0 / total)).astype(BF)
                blended.append(nn(probs, qkv_ref[2, key_rows, lanes]))
            heads_ref[rows, lanes] = jnp.where(low, blended[0], blended[1]).astype(BF)

    @pl.when(kind == 2)
    def _():
        lax.fori_loop(0, 4, lambda w, c: (units(w, 2 * UNIT), c)[1], 0)

    @pl.when(kind == 1)
    def _():
        lax.fori_loop(0, 3, lambda w, c: (units(w, UNIT), c)[1], 0)
        heads_ref[3 * UNIT :, :] = jnp.zeros((slots - 3 * UNIT, width), BF)

    @pl.when(kind == 0)
    def _():
        heads_ref[...] = jnp.zeros_like(heads_ref)


def attend_forward(place, table, x, pieces, vectors):
    slots, features = x.shape
    width = 4 * HD
    staged = len(pieces) == 8
    grid_spec = pltpu.PrefetchScalarGridSpec(
        num_scalar_prefetch=2,
        grid=(features // width,),
        in_specs=[
            pl.BlockSpec((slots, features), lambda g, *_: (0, 0)),
            pl.BlockSpec((16, width), lambda g, *_: (0, g)),
        ]
        + [pl.BlockSpec(memory_space=pl.ANY)] * len(pieces),
        out_specs=[
            pl.BlockSpec((3, slots, width), lambda g, *_: (0, 0, g)),
            pl.BlockSpec((slots, width), lambda g, *_: (0, g)),
            pl.BlockSpec(memory_space=pl.ANY),
        ],
        scratch_shapes=[
            pltpu.VMEM((3, features, features), BF),
            pltpu.SemaphoreType.DMA(()),
            pltpu.SemaphoreType.DMA(()),
        ],
    )
    return pl.pallas_call(
        functools.partial(attend_forward_kernel, staged),
        out_shape=(
            pinned((3, slots, features), BF),
            pinned((slots, features), BF),
            pinned((3, features, features), BF),
        ),
        grid_spec=grid_spec,
        name="attend_forward",
        cost_estimate=pl.CostEstimate(
            flops=20 * 10**9, transcendentals=6 * 10**6, bytes_accessed=20 * MIB
        ),
        compiler_params=pltpu.CompilerParams(
            dimension_semantics=("arbitrary",), vmem_limit_bytes=48 * MIB
        ),
    )(place, table, hbm(x), vectors, *map(hbm, pieces))


def norm_forward(z):
    center = z - jnp.mean(z, axis=-1, keepdims=True)
    spread = jnp.mean(center * center, axis=-1, keepdims=True)
    scale = lax.rsqrt(spread + EPSILON)
    return center * scale, scale


def norm_backward(gx, xhat, scale):
    return (
        gx
        - jnp.mean(gx, axis=-1, keepdims=True)
        - xhat * jnp.mean(gx * xhat, axis=-1, keepdims=True)
    ) * scale


def rows_kernel(
    staged,
    place_ref,
    tab_ref,
    heads_ref,
    x_ref,
    cot_ref,
    vec_ref,
    down_ref,
    *refs,
):
    count = 8 if staged else 2
    pieces = refs[:count]
    written = refs[count : count + 9]
    out_ref, act_ref, gpre_ref, nlow_ref, gffn_ref, gres_ref, gbranch_ref, gheads_ref, ht_ref = written
    terms_ref, slope_ref, mixed_ref, ow_ref, uw_ref, dw_ref, sems = refs[count + 9 :]
    peers = cot_ref.shape[0]
    levels = cot_ref.shape[1]
    tile = pl.program_id(0)
    kind = tab_ref[0]
    live = jnp.where(kind == 2, 4, jnp.where(kind == 1, 3, 0))
    features = x_ref.shape[1]
    hidden = uw_ref.shape[1]
    chunks = [slice(c, c + features) for c in range(0, hidden, features)]

    @pl.when(tile == 0)
    def _():
        terms_ref[...] = jnp.zeros_like(terms_ref)

    @pl.when(tile >= live)
    def _():
        for ref in written:
            ref[...] = jnp.zeros_like(ref)

    @pl.when((tile == 0) & (live > 0))
    def _():
        if staged:
            rows = features // 8

            def out_rows(d):
                return ow_ref.at[pl.ds(pl.multiple_of(d * rows, 32), rows), :]

            def up_rows(j):
                lanes = pl.ds(j * features, features)
                return lambda d: uw_ref.at[pl.ds(pl.multiple_of(d * rows, 32), rows), lanes]

            start_pieces(place_ref, pieces, [(0, rows, out_rows)], sems.at[0])
            start_pieces(
                place_ref, pieces, [((1 + j) * rows, rows, up_rows(j)) for j in range(4)], sems.at[1]
            )
        else:
            pltpu.make_async_copy(pieces[0], ow_ref, sems.at[0]).start()
            pltpu.make_async_copy(pieces[1], uw_ref, sems.at[1]).start()
        pltpu.make_async_copy(down_ref, dw_ref, sems.at[2]).start()
        wait_whole(ow_ref, sems.at[0])
        wait_whole(uw_ref, sems.at[1])
        wait_whole(dw_ref, sems.at[2])

    @pl.when(tile < live)
    def _():
        def vec(i):
            return vec_ref[i : i + 1, :]

        def add(i, value):
            terms_ref[i : i + 1, :] += jnp.sum(value, axis=0, keepdims=True)

        z1 = x_ref[...].astype(F32) + nn(heads_ref[...], ow_ref[...]) + vec(2)
        xhat1, scale1 = norm_forward(z1)
        normed = xhat1 * vec(8) + vec(10)
        nlow = normed.astype(BF)
        nlow_ref[...] = nlow.T
        ht_ref[...] = heads_ref[...].T
        ffn = jnp.zeros_like(normed)
        for i, c in enumerate(chunks):
            pre = nn(nlow, uw_ref[:, c]) + vec(3 + i)
            active, slope = gelu_parts(pre)
            active = active.astype(BF)
            act_ref[:, c] = active
            slope_ref[:, c] = slope
            ffn = ffn + nn(active, dw_ref[c, :])
        z2 = normed + ffn + vec(7)
        xhat2, scale2 = norm_forward(z2)
        result = xhat2 * vec(9) + vec(11)
        for j in range(features // 128):
            lanes = slice(j * 128, (j + 1) * 128)
            mixed_ref[j] = result[:, lanes]
            for peer in range(peers):
                out_ref[peer, :, lanes] = mixed_ref[j, pl.ds(peer, levels, stride=peers), :].astype(BF)
        cot = []
        for j in range(features // 128):
            lanes = slice(j * 128, (j + 1) * 128)
            for peer in range(peers):
                mixed_ref[j, pl.ds(peer, levels, stride=peers), :] = cot_ref[peer, :, lanes].astype(F32)
            cot.append(mixed_ref[j])
        cot = jnp.concatenate(cot, axis=1)
        add(9, cot * xhat2)
        add(11, cot)
        gres2 = norm_backward(cot * vec(9), xhat2, scale2)
        gffn = gres2.astype(BF)
        gffn_ref[...] = gffn
        add(7, gffn.astype(F32))
        gmoved = gres2
        for i, c in enumerate(chunks):
            gactive = nt(gffn, dw_ref[c, :])
            gpre = (gactive * slope_ref[:, c]).astype(BF)
            gpre_ref[:, c] = gpre
            add(3 + i, gpre.astype(F32))
            gmoved = gmoved + nt(gpre, uw_ref[:, c])
        add(8, gmoved * xhat1)
        add(10, gmoved)
        gres1 = norm_backward(gmoved * vec(8), xhat1, scale1)
        gres_ref[...] = gres1
        gbranch = gres1.astype(BF)
        gbranch_ref[...] = gbranch
        add(2, gbranch.astype(F32))
        gheads_ref[...] = nt(gbranch, ow_ref[...]).astype(BF)


def rows_both_ways(place, table, heads, x, cot, pieces, down_w, vectors, staged):
    slots, features = x.shape
    hidden = down_w.shape[0]
    peers, levels = cot.shape[:2]

    def tile(width):
        return pl.BlockSpec((UNIT, width), lambda i, *_: (i, 0))

    peer_tile = pl.BlockSpec((peers, UNIT // peers, features), lambda i, *_: (0, i, 0))
    turned_tile = pl.BlockSpec((features, UNIT), lambda i, *_: (0, i))
    narrow = pinned((slots, features), BF)
    turned = pinned((features, slots), BF)
    wide = pinned((slots, hidden), BF)
    grid_spec = pltpu.PrefetchScalarGridSpec(
        num_scalar_prefetch=2,
        grid=(slots // UNIT,),
        in_specs=[
            tile(features),
            tile(features),
            peer_tile,
            pl.BlockSpec((16, features), lambda i, *_: (0, 0)),
        ]
        + [pl.BlockSpec(memory_space=pl.ANY)] * (1 + len(pieces)),
        out_specs=[
            peer_tile,
            tile(hidden),
            tile(hidden),
            turned_tile,
            tile(features),
            tile(features),
            tile(features),
            tile(features),
            turned_tile,
            pl.BlockSpec((16, features), lambda i, *_: (0, 0)),
        ],
        scratch_shapes=[
            pltpu.VMEM((UNIT, hidden), F32),
            pltpu.VMEM((features // 128, UNIT, 128), F32),
            pltpu.VMEM((features, features), BF),
            pltpu.VMEM((features, hidden), BF),
            pltpu.VMEM((hidden, features), BF),
            pltpu.SemaphoreType.DMA((3,)),
        ],
    )
    return pl.pallas_call(
        functools.partial(rows_kernel, staged),
        out_shape=(
            pinned(cot.shape, BF),
            wide,
            wide,
            turned,
            narrow,
            pinned((slots, features), F32),
            narrow,
            narrow,
            turned,
            pinned((16, features), F32),
        ),
        grid_spec=grid_spec,
        name="rows_both_ways",
        cost_estimate=pl.CostEstimate(
            flops=40 * 10**9, transcendentals=6 * 10**6, bytes_accessed=40 * MIB
        ),
        compiler_params=pltpu.CompilerParams(
            dimension_semantics=("arbitrary",), vmem_limit_bytes=58 * MIB
        ),
    )(place, table, hbm(heads), hbm(x), hbm(cot), vectors, hbm(down_w), *map(hbm, pieces))


def down_grad_kernel(place_ref, cols_ref, g_ref, *refs):
    total = tn(cols_ref[...], g_ref[...])
    if len(refs) == 1:
        refs[0][0] = total.astype(BF)
        return
    total = (total + refs[0][0].astype(F32)).astype(BF)
    for k in range(4):

        @pl.when(pl.program_id(0) == k)
        def _():
            refs[1 + k][...] = total


def down_gradient(place, act, gffn, got=None):
    slots, hidden = act.shape
    features = gffn.shape[1]
    rows = hidden // 8
    swap = 1 if got is None else 0
    piece = pl.BlockSpec((1, rows, features), lambda k, *_: (k, 0, 0))

    def columns(k, place):
        return 0, ((place[0] >> 3) ^ k) * 2 + (((place[0] >> 2) & 1) ^ swap)

    in_specs = [
        pl.BlockSpec((slots, rows), columns),
        pl.BlockSpec((slots, features), lambda k, *_: (0, 0)),
    ]
    if got is None:
        args, out_shape, out_specs = [], pinned((4, rows, features), BF), piece
    else:
        args = [hbm(got)]
        in_specs.append(piece)
        out_shape = [pinned((rows + 5 * (features // 8), features), BF)] * 4
        out_specs = [pl.BlockSpec((rows, features), lambda k, *_: (0, 0))] * 4
    return pl.pallas_call(
        down_grad_kernel,
        out_shape=out_shape,
        grid_spec=pltpu.PrefetchScalarGridSpec(
            num_scalar_prefetch=1, grid=(4,), in_specs=in_specs, out_specs=out_specs
        ),
        name="down_gradient",
        cost_estimate=pl.CostEstimate(
            flops=3 * 10**9, transcendentals=0, bytes_accessed=9 * MIB
        ),
        compiler_params=pltpu.CompilerParams(
            dimension_semantics=("arbitrary",), vmem_limit_bytes=40 * MIB
        ),
    )(place, hbm(act), hbm(gffn), *args)


def up_grad_kernel(swap, place_ref, turned_ref, g_ref, heads_ref, gbranch_ref, *refs):
    step = pl.program_id(0)
    rows = turned_ref.shape[0] // 8

    def emit(left_ref, right_ref):
        core = ((place_ref[0] >> 2) & 1) ^ swap
        left = [
            left_ref[
                pl.ds(pl.multiple_of((((place_ref[0] >> 3) ^ k) * 2 + core) * rows, 32), rows), :
            ]
            for k in range(4)
        ]
        total = nn(jnp.concatenate(left, axis=0), right_ref[...])
        for k in range(4):
            part = total[k * rows : (k + 1) * rows, :]
            if swap:
                refs[0][k, 0] = part.astype(BF)
            else:
                refs[5 + k][...] = (part + refs[0][k, 0].astype(F32)).astype(BF)

    @pl.when(step < 4)
    def _():
        emit(turned_ref, g_ref)

    @pl.when(step == 4)
    def _():
        emit(heads_ref, gbranch_ref)


def up_gradient(place, nlow_t, gpre, heads_t, gbranch, got=None, sums=None):
    features, slots = nlow_t.shape
    rows = features // 8
    swap = 1 if got is None else 0
    piece = pl.BlockSpec((4, 1, rows, features), lambda j, *_: (0, j, 0, 0))

    def whole(shape):
        return pl.BlockSpec(shape, lambda j, *_: (0, 0))

    in_specs = [
        whole((features, slots)),
        pl.BlockSpec((slots, features), lambda j, *_: (0, jnp.minimum(j, 3))),
        whole((features, slots)),
        whole((slots, features)),
    ]
    args = [hbm(nlow_t), hbm(gpre), hbm(heads_t), hbm(gbranch)]
    if got is None:
        out_shape, out_specs, aliases = pinned((4, 5, rows, features), BF), piece, {}
    else:
        args += [hbm(got), *map(hbm, sums)]
        in_specs += [piece] + [pl.BlockSpec(memory_space=pl.ANY)] * 4
        out_shape = [pinned(sums[0].shape, BF)] * 4
        out_specs = [pl.BlockSpec((rows, features), lambda j, *_: (4 + j, 0))] * 4
        aliases = {6 + k: k for k in range(4)}
    return pl.pallas_call(
        functools.partial(up_grad_kernel, swap),
        out_shape=out_shape,
        grid_spec=pltpu.PrefetchScalarGridSpec(
            num_scalar_prefetch=1, grid=(5,), in_specs=in_specs, out_specs=out_specs
        ),
        input_output_aliases=aliases,
        name="up_gradient",
        cost_estimate=pl.CostEstimate(
            flops=4 * 10**9, transcendentals=0, bytes_accessed=14 * MIB
        ),
        compiler_params=pltpu.CompilerParams(
            dimension_semantics=("arbitrary",), vmem_limit_bytes=40 * MIB
        ),
    )(place, *args)


def cut_rows(place_ref, full_ref, keep_ref, send_ref, at):
    rows = full_ref.shape[0] // 8
    for k in range(4):
        plane = (place_ref[0] >> 3) ^ k
        core = (place_ref[0] >> 2) & 1
        for swap, ref in ((0, keep_ref), (1, send_ref)):
            first = (plane * 2 + (core ^ swap)) * rows
            at(ref, k, full_ref[pl.ds(pl.multiple_of(first, 8), rows), :].astype(BF))


def attend_backward_kernel(
    staged,
    place_ref,
    tab_ref,
    qkv_ref,
    gh_ref,
    xt_ref,
    terms_in_ref,
    g_ref,
    keep_ref,
    send_a_ref,
    send_b_ref,
    terms_ref,
    dk_ref,
    dv_ref,
    full_ref,
):
    group = pl.program_id(0)
    kind = tab_ref[0]
    slots, width = gh_ref.shape
    low = lax.broadcasted_iota(jnp.int32, (UNIT, 2 * HD), 1) < HD

    dk_ref[...] = jnp.zeros_like(dk_ref)
    dv_ref[...] = jnp.zeros_like(dv_ref)

    def units(which, keys):
        for pair in range(width // (2 * HD)):
            lanes = slice(pair * 2 * HD, (pair + 1) * 2 * HD)
            rows = pl.ds(pl.multiple_of(which * UNIT, UNIT), UNIT)
            query = qkv_ref[0, rows, lanes]
            gout = gh_ref[rows, lanes]
            gquery = []
            for side in range(2):
                head = group * (width // HD) + pair * 2 + side
                first = tab_ref[1 + head * 4 + which]
                key_rows = pl.ds(pl.multiple_of(first * UNIT, UNIT), keys)
                mine = low if side == 0 else ~low
                own = jnp.where(mine, query, jnp.zeros((), BF))
                gown = jnp.where(mine, gout, jnp.zeros((), BF))
                key = qkv_ref[1, key_rows, lanes]
                value = qkv_ref[2, key_rows, lanes]
                scores = nt(key, own)
                expon = jnp.exp(scores - jnp.max(scores, axis=0, keepdims=True))
                probs = expon * (1.0 / jnp.sum(expon, axis=0, keepdims=True))
                gprobs = nt(value, gown)
                inner = jnp.sum(gprobs * probs, axis=0, keepdims=True)
                gscores = (probs * (gprobs - inner)).astype(BF)
                dv_ref[key_rows, lanes] += nn(probs.astype(BF), gown)
                dk_ref[key_rows, lanes] += nn(gscores, own)
                gquery.append(tn(gscores, key))
            g_ref[0, rows, lanes] = (jnp.where(low, gquery[0], gquery[1]) * HD**-0.5).astype(BF)

    @pl.when(kind == 2)
    def _():
        lax.fori_loop(0, 4, lambda w, c: (units(w, 2 * UNIT), c)[1], 0)

    @pl.when(kind == 1)
    def _():
        lax.fori_loop(0, 3, lambda w, c: (units(w, UNIT), c)[1], 0)
        g_ref[0, 3 * UNIT :, :] = jnp.zeros((slots - 3 * UNIT, width), BF)

    @pl.when(kind == 0)
    def _():
        g_ref[0] = jnp.zeros((slots, width), BF)

    g_ref[1] = dk_ref[...].astype(BF)
    g_ref[2] = dv_ref[...].astype(BF)
    terms_ref[...] = terms_in_ref[...]
    terms_ref[0:1, :] = jnp.sum(g_ref[0].astype(F32), axis=0, keepdims=True)
    terms_ref[1:2, :] = jnp.sum(g_ref[2].astype(F32), axis=0, keepdims=True)
    for n in range(3):
        if not staged:
            keep_ref[n] = nn(xt_ref[...], g_ref[n]).astype(BF)
            continue
        full_ref[...] = nn(xt_ref[...], g_ref[n])
        rows = full_ref.shape[0] // 8

        def put(ref, k, value):
            if ref is keep_ref:
                keep_ref[k, n] = value
            else:
                at = ((k % 2) * 3 + n) * rows
                (send_a_ref if k < 2 else send_b_ref)[at : at + rows, :] = value

        cut_rows(place_ref, full_ref, keep_ref, None, put)
    if staged:
        send_b_ref[6 * rows :, :] = terms_ref[...].astype(BF)


def attend_backward(place, table, qkv, gheads, xt, terms, staged):
    _, slots, features = qkv.shape
    width = 4 * HD
    if staged:
        cut = pinned((4, 3, features // 8, features), BF)
        cut_spec = pl.BlockSpec((4, 3, features // 8, width), lambda g, *_: (0, 0, 0, g))
        heights = (6 * features // 8, 6 * features // 8 + 16)
    else:
        heights = (16, 16)
        cut = pinned((3, features, features), BF)
        cut_spec = pl.BlockSpec((3, features, width), lambda g, *_: (0, 0, g))
    grid_spec = pltpu.PrefetchScalarGridSpec(
        num_scalar_prefetch=2,
        grid=(features // width,),
        in_specs=[
            pl.BlockSpec((3, slots, width), lambda g, *_: (0, 0, g)),
            pl.BlockSpec((slots, width), lambda g, *_: (0, g)),
            pl.BlockSpec((features, slots), lambda g, *_: (0, 0)),
            pl.BlockSpec((16, width), lambda g, *_: (0, g)),
        ],
        out_specs=[
            pl.BlockSpec((3, slots, width), lambda g, *_: (0, 0, g)),
            cut_spec,
            *[pl.BlockSpec((h, width), lambda g, *_: (0, g)) for h in heights],
            pl.BlockSpec((16, width), lambda g, *_: (0, g)),
        ],
        scratch_shapes=[
            pltpu.VMEM((slots, width), F32),
            pltpu.VMEM((slots, width), F32),
            pltpu.VMEM((features, width), F32),
        ],
    )
    return pl.pallas_call(
        functools.partial(attend_backward_kernel, staged),
        out_shape=(
            pinned((3, slots, features), BF),
            cut,
            *[pinned((h, features), BF) for h in heights],
            pinned((16, features), F32),
        ),
        grid_spec=grid_spec,
        name="attend_backward",
        cost_estimate=pl.CostEstimate(
            flops=40 * 10**9, transcendentals=6 * 10**6, bytes_accessed=25 * MIB
        ),
        compiler_params=pltpu.CompilerParams(
            dimension_semantics=("arbitrary",), vmem_limit_bytes=48 * MIB
        ),
    )(place, table, hbm(qkv), hbm(gheads), hbm(xt), hbm(terms))


def chip_sums_q_kernel(keep_ref, got_a_ref, got_b_ref, terms_ref, *out_refs):
    rows = keep_ref.shape[2]
    terms = (terms_ref[...] + got_b_ref[6 * rows :, :].astype(F32)).astype(BF)
    for k in range(4):
        got_ref = got_a_ref if k < 2 else got_b_ref
        for n in range(3):
            at = ((k % 2) * 3 + n) * rows
            out_refs[k][n * rows : (n + 1) * rows, :] = (
                keep_ref[k, n].astype(F32) + got_ref[at : at + rows, :].astype(F32)
            ).astype(BF)
        out_refs[k][3 * rows :, :] = terms


def chip_sums_q(keep, got_a, got_b, terms):
    rows, features = keep.shape[2:]
    return pl.pallas_call(
        chip_sums_q_kernel,
        out_shape=[pinned((3 * rows + 16, features), BF)] * 4,
        grid=(1,),
        in_specs=[
            pl.BlockSpec(v.shape, lambda i, n=v.ndim: (0,) * n) for v in (keep, got_a, got_b, terms)
        ],
        out_specs=[pl.BlockSpec((3 * rows + 16, features), lambda i: (0, 0))] * 4,
        name="chip_sums_q",
        cost_estimate=BRIEF,
        compiler_params=pltpu.CompilerParams(vmem_limit_bytes=32 * MIB),
    )(hbm(keep), hbm(got_a), hbm(got_b), hbm(terms))


def plane_sums_kernel(pieces, place_ref, a_ref, b_ref, c_ref, d_ref, *refs):
    out_refs, full_ref = refs[:-1], refs[-1]
    each = 4 // len(out_refs)
    height = out_refs[0].shape[0] // each
    full_ref[...] = (
        a_ref[...].astype(F32)
        + b_ref[...].astype(F32)
        + c_ref[...].astype(F32)
        + d_ref[...].astype(F32)
    )
    rep = place_ref[0] & 3
    for k in range(4):
        for base, rows, at in pieces:
            first = base + (rep ^ k) * rows if rows else base
            rows = rows or 16
            at = at + (k % each) * height
            out_refs[k // each][at : at + rows, :] = full_ref[
                pl.ds(pl.multiple_of(first, 8), rows), :
            ].astype(BF)


def plane_sums(place, parts, pieces, height, arrays=4):
    rows, features = parts[0].shape
    return pl.pallas_call(
        functools.partial(plane_sums_kernel, pieces),
        out_shape=[pinned((height * 4 // arrays, features), BF)] * arrays,
        grid_spec=pltpu.PrefetchScalarGridSpec(
            num_scalar_prefetch=1,
            grid=(1,),
            in_specs=[pl.BlockSpec((rows, features), lambda i, *_: (0, 0))] * 4,
            out_specs=[pl.BlockSpec((height * 4 // arrays, features), lambda i, *_: (0, 0))] * arrays,
            scratch_shapes=[pltpu.VMEM((rows, features), F32)],
        ),
        name="plane_sums",
        cost_estimate=BRIEF,
        compiler_params=pltpu.CompilerParams(vmem_limit_bytes=32 * MIB),
    )(place, *map(hbm, parts))


def input_grad_kernel(tab_ref, gres_ref, g_ref, w_ref, out_ref):
    kind = tab_ref[0]
    live = jnp.where(kind == 2, 4, jnp.where(kind == 1, 3, 0))
    tile = pl.program_id(0)

    @pl.when(tile < live)
    def _():
        total = gres_ref[...]
        for n in range(3):
            total = total + nt(g_ref[n], w_ref[n])
        out_ref[...] = total

    @pl.when(tile >= live)
    def _():
        out_ref[...] = jnp.zeros_like(out_ref)


def input_gradient(table, gres, grads, qkv_w):
    slots, features = gres.shape
    grid_spec = pltpu.PrefetchScalarGridSpec(
        num_scalar_prefetch=1,
        grid=(slots // UNIT,),
        in_specs=[
            pl.BlockSpec((UNIT, features), lambda i, *_: (i, 0)),
            pl.BlockSpec((3, UNIT, features), lambda i, *_: (0, i, 0)),
            pl.BlockSpec((3, features, features), lambda i, *_: (0, 0, 0)),
        ],
        out_specs=pl.BlockSpec((UNIT, features), lambda i, *_: (i, 0)),
    )
    return pl.pallas_call(
        input_grad_kernel,
        out_shape=pinned((slots, features), F32),
        grid_spec=grid_spec,
        name="input_gradient",
        cost_estimate=BRIEF,
        compiler_params=pltpu.CompilerParams(
            dimension_semantics=("arbitrary",), vmem_limit_bytes=40 * MIB
        ),
    )(table, hbm(gres), hbm(grads), hbm(qkv_w))


def gather_line_kernel(place_ref, *refs, blocks):
    full_ref, out_ref = refs[5], refs[4]
    rep = place_ref[0] & 3
    own = refs[0].shape[0] // blocks if refs[0].shape[0] % blocks == 0 else (refs[0].shape[0] - 16) // blocks
    for k in range(4):
        for n in range(blocks):
            full_ref[pl.ds(pl.multiple_of((n * 4 + (rep ^ k)) * own, 8), own), :] = refs[k][
                n * own : (n + 1) * own, :
            ].astype(F32)
    out_ref[: blocks * 4 * own, :] = full_ref[...].astype(BF)
    if out_ref.shape[0] > blocks * 4 * own:
        total = refs[0][blocks * own :, :].astype(F32)
        for k in (1, 2, 3):
            total = total + refs[k][blocks * own :, :].astype(F32)
        out_ref[blocks * 4 * own :, :] = total.astype(BF)


def gather_line(place, parts, blocks, extra):
    rows, features = parts[0].shape
    height = (rows - extra) * 4
    return pl.pallas_call(
        functools.partial(gather_line_kernel, blocks=blocks),
        out_shape=pinned((height + extra, features), BF),
        grid_spec=pltpu.PrefetchScalarGridSpec(
            num_scalar_prefetch=1,
            grid=(1,),
            in_specs=[pl.BlockSpec((rows, features), lambda i, *_: (0, 0))] * 4,
            out_specs=pl.BlockSpec((height + extra, features), lambda i, *_: (0, 0)),
            scratch_shapes=[pltpu.VMEM((height, features), F32)],
        ),
        name="gather_line",
        cost_estimate=BRIEF,
        compiler_params=pltpu.CompilerParams(vmem_limit_bytes=16 * MIB),
    )(place, *parts)


def to_peers_kernel(spans_ref, rows_ref, out_ref):
    peers, per_peer = out_ref.shape[:2]
    some = per_peer * 3 // 4
    for peer in range(peers):
        start = pl.multiple_of(spans_ref[peer], 32)

        @pl.when(spans_ref[peers + peer] == per_peer)
        def _():
            out_ref[peer] = rows_ref[pl.ds(start, per_peer), :]

        @pl.when(spans_ref[peers + peer] == some)
        def _():
            out_ref[peer, :some, :] = rows_ref[pl.ds(start, some), :]
            out_ref[peer, some:, :] = jnp.zeros_like(out_ref[peer, some:, :])

        @pl.when(spans_ref[peers + peer] == 0)
        def _():
            out_ref[peer] = jnp.zeros_like(out_ref[peer])


def from_peers_kernel(spans_ref, in_ref, rows_ref):
    peers, per_peer = in_ref.shape[:2]
    some = per_peer * 3 // 4
    for peer in range(peers):
        start = pl.multiple_of(spans_ref[peer], 32)

        @pl.when(spans_ref[peers + peer] == per_peer)
        def _():
            rows_ref[pl.ds(start, per_peer), :] = in_ref[peer]

        @pl.when(spans_ref[peers + peer] == some)
        def _():
            rows_ref[pl.ds(start, some), :] = in_ref[peer, :some, :]


def between_layouts(kernel, name, spans, x, shape):
    return pl.pallas_call(
        kernel,
        out_shape=pinned(shape, BF),
        grid_spec=pltpu.PrefetchScalarGridSpec(
            num_scalar_prefetch=1,
            grid=(1,),
            in_specs=[pl.BlockSpec(x.shape, lambda i, *_: (0,) * x.ndim)],
            out_specs=pl.BlockSpec(shape, lambda i, *_: (0,) * len(shape)),
        ),
        name=name,
        cost_estimate=BRIEF,
        compiler_params=pltpu.CompilerParams(vmem_limit_bytes=16 * MIB),
    )(spans, x)


def seq_swap(x, k):
    n = lax.axis_size("seq")
    return lax.ppermute(x, "seq", [(i, i ^ k) for i in range(n)])


def rep_swap(x, k):
    n = lax.axis_size("rep")
    return lax.ppermute(x, "rep", [(i, i ^ k) for i in range(n)])


def key_table(own_kind, perm_two, perm_three):
    quarters = jnp.arange(4)
    halves = quarters // 2
    pick_two = jnp.sum(
        jnp.where(halves[None, :, None] == jnp.arange(2)[None, None, :], perm_two[:, None, :], 0),
        axis=-1,
    )
    pick_three = jnp.sum(
        jnp.where(
            jnp.minimum(quarters, 2)[None, :, None] == jnp.arange(3)[None, None, :],
            perm_three[:, None, :],
            0,
        ),
        axis=-1,
    )
    first = jnp.where(own_kind == 2, 2 * pick_two, pick_three)
    return jnp.concatenate([own_kind.reshape(1), first.reshape(-1)]).astype(jnp.int32)


def placed(vector, rows, offset, features):
    lane = lax.broadcasted_iota(jnp.int32, (vector.shape[-1], features), 1)
    entry = lax.broadcasted_iota(jnp.int32, (vector.shape[-1], features), 0)
    return jnp.dot(vector, (lane == entry + offset).astype(BF), preferred_element_type=F32)


def shards(
    inputs,
    item_kind,
    perm_two,
    perm_three,
    qkv_weight,
    qv_bias,
    out_weight,
    out_bias,
    up_weight,
    up_bias,
    down_weight,
    down_bias,
    norm_gain,
    norm_bias,
    cotangent,
):
    peers = lax.axis_size("seq")
    copies = lax.axis_size("rep")
    seq = lax.axis_index("seq")
    rep = lax.axis_index("rep")
    x = inputs[0]
    slots, features = x.shape
    tokens = cotangent.shape[1]
    hidden = up_weight.shape[1]
    quarter = slots // 4
    per_peer = slots // peers
    staged = peers == 8 and copies == 4
    own = out_weight.shape[0]

    kind_row = item_kind[0]
    own_kind = jnp.sum(jnp.where(jnp.arange(peers) == seq, kind_row, 0))
    table = key_table(own_kind, perm_two, perm_three)

    per_pair = (
        jnp.where(kind_row == 2, 4 * quarter, jnp.where(kind_row == 1, 3 * quarter, 0)) // peers
    )
    earlier = jnp.arange(peers)[:, None] < jnp.arange(peers)[None, :]
    range_starts = jnp.sum(jnp.where(earlier, per_pair[:, None], 0), axis=0)
    spans = jnp.concatenate([range_starts, per_pair]).astype(jnp.int32)

    place = (seq * copies + rep).astype(jnp.int32).reshape(1)
    index = seq * copies + rep
    core, plane = seq & 1, seq >> 1
    fan = 4 * own
    up_row = (index * fan) // features
    together = lax.optimization_barrier

    def swap_rows(rows):
        return lax.all_to_all(rows, "seq", split_axis=0, concat_axis=0, tiled=True)

    turned = x.T
    if staged:
        down_w = lax.all_gather(down_weight, AXES, axis=0, tiled=True)

        def along_rep(piece):
            return [piece] + [rep_swap(piece, k) for k in (1, 2, 3)]

        def along_plane(piece):
            return [piece] + [seq_swap(piece, 2 * k) for k in (1, 2, 3)]

        def both_cores(parts):
            return parts + [seq_swap(p, 1) for p in parts]

        small = jnp.concatenate([qv_bias, out_bias[None], down_bias[None], norm_gain, norm_bias])
        small = placed(small, 8, index * own, features)
        spread = placed(up_bias[None], 1, index * fan - up_row * features, features)
        spread = jnp.where(jnp.arange(4)[:, None] == up_row, spread, 0.0)
        vectors = jnp.concatenate(
            [small[0:3], spread, small[3:8], jnp.zeros((4, features), F32)]
        ).astype(BF)

        first = along_rep(jnp.concatenate([qkv_weight.reshape(3 * own, features), vectors]))
        second = jnp.concatenate(
            [out_weight] + [up_weight[:, c : c + features] for c in range(0, hidden, features)]
        )
        near = rep_swap(second, 1)
        picked = between_layouts(
            to_peers_kernel, "to_peers", spans, cotangent[0], (peers, per_peer, features)
        )
        turned, near, *first = together((turned, near, *first))
        first = gather_line(place, first, 3, 16)
        pair = jnp.concatenate([second, near])
        pair, first = together((pair, first))
        far = rep_swap(pair, 2)
        first = along_plane(first)
        second = gather_line(place, [pair[: 5 * own], pair[5 * own :], far[: 5 * own], far[5 * own :]], 5, 0)
        second, picked, *first = together((second, picked, *first))
        first = both_cores(first)
        second = along_plane(second)
        cot = swap_rows(picked)
        vectors = sum(p[12 * own :].astype(F32) for p in first)
        qkv, heads, qkv_w = attend_forward(place, table, x, first, vectors)
        heads, cot, *second = together((heads, cot, *second))
        pieces = both_cores(second)
    else:

        def gathered(v, axis):
            return lax.all_gather(v, AXES, axis=axis, tiled=True)

        qkv_all = gathered(qkv_weight, 1)
        pieces = [gathered(out_weight, 0), gathered(up_weight, 0)]
        down_w = gathered(down_weight, 0)
        vectors = jnp.concatenate(
            [
                gathered(qv_bias, 1),
                gathered(out_bias, 0)[None],
                gathered(up_bias, 0).reshape(4, features),
                gathered(down_bias, 0)[None],
                gathered(norm_gain, 1),
                gathered(norm_bias, 1),
                jnp.zeros((4, features), BF),
            ]
        ).astype(F32)
        levels = jnp.arange(per_peer)[None, :]
        targets = jnp.minimum(range_starts[:, None] + levels, tokens - 1)
        cot = swap_rows(cotangent[0][targets])
        qkv, heads, qkv_w = attend_forward(place, table, x, [qkv_all], vectors)

    out, act, gpre, nlow_t, gffn, gres, gbranch, gheads, heads_t, terms = rows_both_ways(
        place, table, heads, x, cot, pieces, down_w, vectors, staged
    )

    moved = swap_rows(out)

    if staged:

        def over_plane(parts):
            return [parts[0]] + [seq_swap(parts[k], 2 * k) for k in (1, 2, 3)]

        def over_rep(parts):
            return [parts[0]] + [rep_swap(parts[k], k) for k in (1, 2, 3)]

        def total_of(parts):
            total = parts[0].astype(F32)
            for p in parts[1:]:
                total = total + p.astype(F32)
            return total

        send_d = down_gradient(place, act, gffn)
        got_d = seq_swap(send_d, 1)
        gpre, send_d = together((gpre, send_d))
        send_u = up_gradient(place, nlow_t, gpre, heads_t, gbranch)
        got_d, send_u = together((got_d, send_u))
        got_u = seq_swap(send_u, 1)
        parts = down_gradient(place, act, gffn, got_d)
        got_u, *parts = together((got_u, *parts))
        parts = up_gradient(place, nlow_t, gpre, heads_t, gbranch, got_u, parts)
        moved, *parts = together((moved, *parts))
        output = between_layouts(from_peers_kernel, "from_peers", spans, moved, (tokens, features))
        gheads, output, *parts = together((gheads, output, *parts))
        parts = over_plane(parts)
        grads, keep_q, send_a, send_b, terms = attend_backward(
            place, table, qkv, gheads, turned, terms, staged
        )
        got_a, got_b = seq_swap(send_a, 1), seq_swap(send_b, 1)
        got_a, got_b, *parts = together((got_a, got_b, *parts))
        parts_q = chip_sums_q(keep_q, got_a, got_b, terms)
        merged = together((*parts_q, *parts))
        parts_q, parts = merged[:4], merged[4:]
        parts_q = over_plane(parts_q)
        pieces = [(0, fan, 0)] + [(4 * fan + 4 * own * j, own, fan + own * j) for j in range(5)]
        height = fan + 5 * own
        near, far = plane_sums(place, parts, pieces, height, 2)
        grads, near, far = together((grads, near, far))
        far = rep_swap(far, 2)
        input_grad = input_gradient(table, gres, grads, qkv_w)
        input_grad, far = together((input_grad, far))
        near = near.astype(F32) + far.astype(F32)
        far = rep_swap(near[height:].astype(BF), 1)
        far, *parts_q = together((far, *parts_q))
        pieces = [(4 * own * n, own, own * n) for n in range(3)] + [(12 * own, 0, 3 * own)]
        parts_q = over_rep(plane_sums(place, parts_q, pieces, 3 * own + 16))
        total = near[:height] + far.astype(F32)
        down_out = total[:fan]
        up_out = jnp.concatenate(
            [total[fan + own * j : fan + own * (j + 1)] for j in range(4)], axis=1
        )
        out_out = total[fan + 4 * own :]
        last = total_of(parts_q)
        qkv_out = last[: 3 * own].reshape(3, own, features)
        sums = last[3 * own :]
        mine = lax.dynamic_slice(sums, (0, index * own), (16, own))
        up_bias_out = lax.dynamic_slice(
            sums, (3 + up_row, index * fan - up_row * features), (1, fan)
        )[0]
        qv_out, out_bias_out, down_bias_out = mine[0:2], mine[2], mine[7]
        gain_out, shift_out = mine[8:10], mine[10:12]
    else:

        def reduced(v, axis):
            return lax.psum_scatter(v.astype(F32), AXES, scatter_dimension=axis, tiled=True)

        grads, qkv_grad, _, _, terms = attend_backward(
            place, table, qkv, gheads, turned, terms, staged
        )
        input_grad = input_gradient(table, gres, grads, qkv_w)
        down_out = reduced(tn(act, gffn), 0)
        up_out = reduced(nn(nlow_t, gpre), 0)
        out_out = reduced(nn(heads_t, gbranch), 0)
        qkv_out = reduced(qkv_grad, 1)
        qv_out = reduced(terms[0:2], 1)
        out_bias_out = reduced(terms[2], 0)
        up_bias_out = reduced(terms[3:7].reshape(hidden), 0)
        down_bias_out = reduced(terms[7], 0)
        gain_out = reduced(terms[8:10], 1)
        shift_out = reduced(terms[10:12], 1)
        positions = jnp.arange(tokens)
        ends = range_starts + per_pair
        sources = jnp.sum((ends[None, :] <= positions[:, None]).astype(jnp.int32), axis=1)
        opening = jnp.sum(
            jnp.where(jnp.arange(peers)[None, :] == sources[:, None], range_starts[None, :], 0),
            axis=1,
        )
        arrivals = sources * per_peer + positions - opening
        output = moved.reshape(slots, features)[arrivals]

    return (
        output[None],
        input_grad[None],
        qkv_out,
        qv_out,
        out_out,
        out_bias_out,
        up_out,
        up_bias_out,
        down_out,
        down_bias_out,
        gain_out,
        shift_out,
    )


def solution(mesh):
    both = ("seq", "rep")
    in_specs = (
        P("rep", "seq", None),
        P("rep", None),
        P(),
        P(),
        P(None, both, None),
        P(None, both),
        P(both, None),
        P(both),
        P(both, None),
        P(both),
        P(both, None),
        P(both),
        P(None, both),
        P(None, both),
        P("rep", "seq", None),
    )
    out_specs = (
        P("rep", "seq", None),
        P("rep", "seq", None),
        P(None, both, None),
        P(None, both),
        P(both, None),
        P(both),
        P(both, None),
        P(both),
        P(both, None),
        P(both),
        P(None, both),
        P(None, both),
    )
    return jax.shard_map(shards, mesh=mesh, in_specs=in_specs, out_specs=out_specs, check_vma=False)
```

```python
import functools

import jax
import jax.numpy as jnp
from jax import lax
from jax.experimental import pallas as pl
from jax.experimental.pallas import tpu as pltpu
from jax.sharding import PartitionSpec as P

HD = 64
CHUNK = 768
UNIT = 256
EPSILON = 1e-05
BF = jnp.bfloat16
F32 = jnp.float32
AXES = ("seq", "rep")
MIB = 1 << 20
BRIEF = pl.CostEstimate(flops=1000, transcendentals=0, bytes_accessed=1000)


def hbm(x):
    return pltpu.with_memory_space_constraint(x, pltpu.HBM)


def pinned(shape, dtype):
    return pltpu.HBM(shape, dtype)


TAIL_P = 0.4 * 0.7071067811865476
TAIL_C = tuple(
    0.5 * c
    for c in (
        0.23192178895457838,
        0.16182559848968434,
        0.46826879780965075,
        -0.3709009174795544,
        0.7091427810415396,
        -0.20025807634318435,
    )
)
BELL = -0.7213475204444817
RSQRT2PI = 0.3989422804014327


def nn(a, b):
    return lax.dot_general(a, b, (((1,), (0,)), ((), ())), preferred_element_type=F32)


def nt(a, b):
    return lax.dot_general(a, b, (((1,), (1,)), ((), ())), preferred_element_type=F32)


def tn(a, b):
    return lax.dot_general(a, b, (((0,), (0,)), ((), ())), preferred_element_type=F32)


def gelu_parts(x):
    t = 1.0 / (1.0 + TAIL_P * jnp.abs(x))
    poly = TAIL_C[-1] * t + TAIL_C[-2]
    for c in TAIL_C[-3::-1]:
        poly = poly * t + c
    bell = jnp.exp2(x * x * BELL)
    tail = poly * t * bell
    phi = jnp.where(x >= 0, 1.0 - tail, tail)
    return x * phi, phi + x * bell * RSQRT2PI


def start_pieces(place_ref, refs, copies, sem):
    for swap in range(2):
        for plane in range(4):
            device = (place_ref[0] >> 2) ^ (plane * 2 + swap)
            for first, rows, target in copies:
                pltpu.make_async_copy(
                    refs[swap * 4 + plane].at[pl.ds(first, rows), :], target(device), sem
                ).start()


def wait_whole(ref, sem):
    pltpu.make_async_copy(ref, ref, sem).wait()


def attend_forward_kernel(
    staged, place_ref, tab_ref, x_ref, b_ref, *refs
):
    count = 8 if staged else 1
    pieces = refs[:count]
    qkv_ref, heads_ref, turned_ref, total_ref, keep_ref = refs[count : count + 5]
    w_ref, vt_ref, sem, keep_sem = refs[count + 5 :]
    group = pl.program_id(0)
    kind = tab_ref[0]
    slots, width = heads_ref.shape
    features = x_ref.shape[1]
    low = lax.broadcasted_iota(jnp.int32, (UNIT, 2 * HD), 1) < HD
    keep = pltpu.make_async_copy(w_ref, keep_ref, keep_sem)

    @pl.when(group == 0)
    def _():
        if staged:
            rows = features // 8

            def target(n):
                return lambda d: w_ref.at[n, pl.ds(pl.multiple_of(d * rows, 32), rows), :]

            start_pieces(
                place_ref, pieces, [(n * rows, rows, target(n)) for n in range(3)], sem
            )
        else:
            pltpu.make_async_copy(pieces[0], w_ref, sem).start()
        wait_whole(w_ref, sem)
        keep.start()

    @pl.when(group == pl.num_programs(0) - 1)
    def _():
        keep.wait()

    cols = pl.ds(pl.multiple_of(group * width, width), width)

    def project(n, bias, scale):
        weight = w_ref[n, :, cols]
        for r in range(0, slots, UNIT):
            acc = nn(x_ref[r : r + UNIT, :], weight)
            if bias is not None:
                acc = acc + bias
            acc = acc.astype(BF)
            if scale is not None:
                acc = acc * jnp.asarray(scale, BF)
            qkv_ref[n, r : r + UNIT, :] = acc

    project(0, b_ref[0:1, :], HD**-0.5)
    project(1, None, None)
    project(2, b_ref[1:2, :], None)

    for unit in range(4):
        vt_ref[unit] = qkv_ref[2, unit * UNIT : (unit + 1) * UNIT, :].T

    def units(first_unit, count, keys):
        heads = width // HD
        tasks = [(first_unit + u, side) for u in range(count) for side in range(heads)]

        def rows_of(which):
            return pl.ds(pl.multiple_of(which * UNIT, UNIT), UNIT)

        def start_of(which, side):
            return tab_ref[1 + (group * heads + side) * 4 + which]

        def score(which, side):
            lanes = slice(side // 2 * 2 * HD, (side // 2 + 1) * 2 * HD)
            key_rows = pl.ds(pl.multiple_of(start_of(which, side) * UNIT, UNIT), keys)
            mine = low if side % 2 == 0 else ~low
            own = jnp.where(mine, qkv_ref[0, rows_of(which), lanes], jnp.zeros((), BF))
            return nt(qkv_ref[1, key_rows, lanes], own)

        def soften(which, side, scores):
            largest = jnp.max(scores, axis=0, keepdims=True)
            expon = jnp.exp(scores - largest)
            total = jnp.sum(expon, axis=0, keepdims=True)
            total_ref[side, which] = largest + jnp.log(total)
            return expon.astype(BF), 1.0 / total

        def blend(which, side, expon, inverse):
            part = sum(
                nn(
                    vt_ref[start_of(which, side) + j, side * HD : (side + 1) * HD, :],
                    expon[j * UNIT : (j + 1) * UNIT, :],
                )
                for j in range(keys // UNIT)
            )
            part = (part * inverse).astype(BF)
            turned_ref[side * HD : (side + 1) * HD, rows_of(which)] = part
            if side == heads - 1:
                heads_ref[rows_of(which), :] = turned_ref[:, rows_of(which)].T

        ahead, soft = score(*tasks[0]), None
        for i, task in enumerate(tasks):
            now = ahead
            if i + 1 < len(tasks):
                ahead = score(*tasks[i + 1])
            fresh = soften(*task, now)
            if soft is not None:
                blend(*tasks[i - 1], *soft)
            soft = fresh
        blend(*tasks[-1], *soft)

    @pl.when(kind == 2)
    def _():
        lax.fori_loop(0, 1, lambda w, c: (units(w * 4, 4, 2 * UNIT), c)[1], 0)

    @pl.when(kind == 1)
    def _():
        lax.fori_loop(0, 1, lambda w, c: (units(w * 3, 3, UNIT), c)[1], 0)
        heads_ref[3 * UNIT :, :] = jnp.zeros((slots - 3 * UNIT, width), BF)
        turned_ref[:, 3 * UNIT :] = jnp.zeros((width, slots - 3 * UNIT), BF)

    @pl.when(kind == 0)
    def _():
        heads_ref[...] = jnp.zeros_like(heads_ref)
        turned_ref[...] = jnp.zeros_like(turned_ref)


def attend_forward(place, table, x, pieces, vectors):
    slots, features = x.shape
    width = 4 * HD
    staged = len(pieces) == 8
    grid_spec = pltpu.PrefetchScalarGridSpec(
        num_scalar_prefetch=2,
        grid=(features // width,),
        in_specs=[
            pl.BlockSpec((slots, features), lambda g, *_: (0, 0)),
            pl.BlockSpec((16, width), lambda g, *_: (0, g)),
        ]
        + [pl.BlockSpec(memory_space=pl.ANY)] * len(pieces),
        out_specs=[
            pl.BlockSpec((3, slots, width), lambda g, *_: (0, 0, g)),
            pl.BlockSpec((slots, width), lambda g, *_: (0, g)),
            pl.BlockSpec((width, slots), lambda g, *_: (g, 0)),
            pl.BlockSpec((4, 4, 1, UNIT), lambda g, *_: (g, 0, 0, 0)),
            pl.BlockSpec(memory_space=pl.ANY),
        ],
        scratch_shapes=[
            pltpu.VMEM((3, features, features), BF),
            pltpu.VMEM((4, width, UNIT), BF),
            pltpu.SemaphoreType.DMA(()),
            pltpu.SemaphoreType.DMA(()),
        ],
    )
    return pl.pallas_call(
        functools.partial(attend_forward_kernel, staged),
        out_shape=(
            pinned((3, slots, features), BF),
            pinned((slots, features), BF),
            pinned((features, slots), BF),
            pinned((features // HD, 4, 1, UNIT), F32),
            pinned((3, features, features), BF),
        ),
        grid_spec=grid_spec,
        name="attend_forward",
        cost_estimate=pl.CostEstimate(
            flops=20 * 10**9, transcendentals=6 * 10**6, bytes_accessed=20 * MIB
        ),
        compiler_params=pltpu.CompilerParams(
            dimension_semantics=("arbitrary",), vmem_limit_bytes=48 * MIB
        ),
    )(place, table, hbm(x), vectors, *map(hbm, pieces))


def norm_forward(z):
    center = z - jnp.mean(z, axis=-1, keepdims=True)
    spread = jnp.mean(center * center, axis=-1, keepdims=True)
    scale = lax.rsqrt(spread + EPSILON)
    return center * scale, scale


def norm_backward(gx, xhat, scale):
    return (
        gx
        - jnp.mean(gx, axis=-1, keepdims=True)
        - xhat * jnp.mean(gx * xhat, axis=-1, keepdims=True)
    ) * scale


def live_tiles(tab_ref):
    kind = tab_ref[0]
    return jnp.where(kind == 2, 4, jnp.where(kind == 1, 3, 0))


def start_weights(staged, place_ref, pieces, down_ref, ow_ref, uw_ref, dw_ref, sems):
    features = ow_ref.shape[0]
    if staged:
        rows = features // 8

        def out_rows(d):
            return ow_ref.at[pl.ds(pl.multiple_of(d * rows, 32), rows), :]

        def up_rows(j):
            lanes = pl.ds(j * features, features)
            return lambda d: uw_ref.at[pl.ds(pl.multiple_of(d * rows, 32), rows), lanes]

        start_pieces(place_ref, pieces, [(0, rows, out_rows)], sems.at[0])
        start_pieces(
            place_ref, pieces, [((1 + j) * rows, rows, up_rows(j)) for j in range(4)], sems.at[1]
        )
    else:
        pltpu.make_async_copy(pieces[0], ow_ref, sems.at[0]).start()
        pltpu.make_async_copy(pieces[1], uw_ref, sems.at[1]).start()
    pltpu.make_async_copy(down_ref, dw_ref, sems.at[2]).start()


def rows_forward_kernel(staged, place_ref, tab_ref, heads_ref, x_ref, vec_ref, down_ref, *refs):
    count = 8 if staged else 2
    pieces = refs[:count]
    written = refs[count : count + 6]
    out_ref, act_ref, slope_ref, nlow_ref, z1_ref, z2_ref = written
    mixed_ref, ow_ref, uw_ref, dw_ref, sems = refs[count + 6 :]
    tile = pl.program_id(0)
    live = live_tiles(tab_ref)
    features = x_ref.shape[1]
    hidden = uw_ref.shape[1]
    peers, levels = out_ref.shape[:2]

    @pl.when(tile >= live)
    def _():
        for ref in written:
            ref[...] = jnp.zeros_like(ref)

    @pl.when((tile == 0) & (live > 0))
    def _():
        start_weights(staged, place_ref, pieces, down_ref, ow_ref, uw_ref, dw_ref, sems)

    @pl.when(tile < live)
    def _():
        def vec(i):
            return vec_ref[i : i + 1, :]

        def arrive(ref, i):
            pl.when(tile == 0)(lambda: wait_whole(ref, sems.at[i]))

        arrive(ow_ref, 0)
        z1 = x_ref[...].astype(F32) + nn(heads_ref[...], ow_ref[...]) + vec(2)
        z1_ref[...] = z1
        normed = norm_forward(z1)[0] * vec(8) + vec(10)
        nlow = normed.astype(BF)
        nlow_ref[...] = nlow.T
        chunks = [slice(c, c + CHUNK) for c in range(0, hidden, CHUNK)]

        def lead(c):
            bias = vec_ref[3 + c.start // features, c.start % features : c.start % features + CHUNK]
            return nn(nlow, uw_ref[:, c]) + bias[None, :]

        arrive(uw_ref, 1)
        arrive(dw_ref, 2)
        ahead, ready, ffn = lead(chunks[0]), None, normed + vec(7)
        for i, c in enumerate(chunks):
            now = ahead
            if i + 1 < len(chunks):
                ahead = lead(chunks[i + 1])
            active, slope = gelu_parts(now)
            active = active.astype(BF)
            act_ref[:, c] = active
            slope_ref[:, c] = slope.astype(BF)
            if ready is not None:
                ffn = ffn + nn(ready, dw_ref[chunks[i - 1], :])
            ready = active
        z2 = ffn + nn(ready, dw_ref[chunks[-1], :])
        z2_ref[...] = z2
        result = norm_forward(z2)[0] * vec(9) + vec(11)
        for j in range(features // 128):
            lanes = slice(j * 128, (j + 1) * 128)
            mixed_ref[j] = result[:, lanes]
            for peer in range(peers):
                out_ref[peer, :, lanes] = mixed_ref[j, pl.ds(peer, levels, stride=peers), :].astype(BF)


def rows_backward_kernel(
    staged, place_ref, tab_ref, z1_ref, z2_ref, cot_ref, slope_ref, vec_ref, down_ref, *refs
):
    count = 8 if staged else 2
    pieces = refs[:count]
    written = refs[count : count + 5]
    gpre_ref, gffn_ref, gres_ref, gbranch_ref, gheads_ref = written
    terms_ref, mixed_ref, ow_ref, uw_ref, dw_ref, sems = refs[count + 5 :]
    tile = pl.program_id(0)
    live = live_tiles(tab_ref)
    features = z1_ref.shape[1]
    hidden = uw_ref.shape[1]
    peers, levels = cot_ref.shape[:2]

    @pl.when(tile == 0)
    def _():
        terms_ref[...] = jnp.zeros_like(terms_ref)

    @pl.when(tile >= live)
    def _():
        for ref in written:
            ref[...] = jnp.zeros_like(ref)

    @pl.when((tile == 0) & (live > 0))
    def _():
        start_weights(staged, place_ref, pieces, down_ref, ow_ref, uw_ref, dw_ref, sems)

    @pl.when(tile < live)
    def _():
        def vec(i):
            return vec_ref[i : i + 1, :]

        def arrive(ref, i):
            pl.when(tile == 0)(lambda: wait_whole(ref, sems.at[i]))

        def add(i, value):
            terms_ref[i : i + 1, :] += jnp.sum(value, axis=0, keepdims=True)

        cot = []
        for j in range(features // 128):
            lanes = slice(j * 128, (j + 1) * 128)
            for peer in range(peers):
                mixed_ref[j, pl.ds(peer, levels, stride=peers), :] = cot_ref[peer, :, lanes].astype(F32)
            cot.append(mixed_ref[j])
        cot = jnp.concatenate(cot, axis=1)
        xhat2, scale2 = norm_forward(z2_ref[...])
        add(9, cot * xhat2)
        add(11, cot)
        gres2 = norm_backward(cot * vec(9), xhat2, scale2)
        gffn = gres2.astype(BF)
        gffn_ref[...] = gffn
        add(7, gffn.astype(F32))
        chunks = [slice(c, c + CHUNK) for c in range(0, hidden, CHUNK)]

        def lead(c):
            return nt(gffn, dw_ref[c, :])

        arrive(dw_ref, 2)
        arrive(uw_ref, 1)
        arrive(ow_ref, 0)
        ahead, ready, gmoved = lead(chunks[0]), None, gres2
        for i, c in enumerate(chunks):
            now = ahead
            if i + 1 < len(chunks):
                ahead = lead(chunks[i + 1])
            gpre = (now * slope_ref[:, c].astype(F32)).astype(BF)
            gpre_ref[:, c] = gpre
            row, lanes = 3 + c.start // features, slice(c.start % features, c.start % features + CHUNK)
            terms_ref[row : row + 1, lanes] += jnp.sum(gpre.astype(F32), axis=0, keepdims=True)
            if ready is not None:
                gmoved = gmoved + nt(ready, uw_ref[:, chunks[i - 1]])
            ready = gpre
        gmoved = gmoved + nt(ready, uw_ref[:, chunks[-1]])
        xhat1, scale1 = norm_forward(z1_ref[...])
        add(8, gmoved * xhat1)
        add(10, gmoved)
        gres1 = norm_backward(gmoved * vec(8), xhat1, scale1)
        gres_ref[...] = gres1
        gbranch = gres1.astype(BF)
        gbranch_ref[...] = gbranch
        add(2, gbranch.astype(F32))
        gheads_ref[...] = nt(gbranch, ow_ref[...]).astype(BF)


def over_rows(kernel, name, place, table, tiles, vectors, down_w, pieces, outs, staged):
    features, hidden = down_w.shape[1], down_w.shape[0]

    def spec(shape):
        if len(shape) == 3:
            return pl.BlockSpec((shape[0], UNIT // shape[0], features), lambda i, *_: (0, i, 0))
        if shape[0] == 16:
            return pl.BlockSpec(shape, lambda i, *_: (0, 0))
        if shape[0] == features:
            return pl.BlockSpec((features, UNIT), lambda i, *_: (0, i))
        return pl.BlockSpec((UNIT, shape[1]), lambda i, *_: (i, 0))

    slots = tiles[0].shape[0]
    return pl.pallas_call(
        functools.partial(kernel, staged),
        out_shape=[pinned(*o) for o in outs],
        grid_spec=pltpu.PrefetchScalarGridSpec(
            num_scalar_prefetch=2,
            grid=(slots // UNIT,),
            in_specs=[spec(v.shape) for v in tiles]
            + [pl.BlockSpec((16, features), lambda i, *_: (0, 0))]
            + [pl.BlockSpec(memory_space=pl.ANY)] * (1 + len(pieces)),
            out_specs=[spec(o[0]) for o in outs],
            scratch_shapes=[
                pltpu.VMEM((features // 128, UNIT, 128), F32),
                pltpu.VMEM((features, features), BF),
                pltpu.VMEM((features, hidden), BF),
                pltpu.VMEM((hidden, features), BF),
                pltpu.SemaphoreType.DMA((3,)),
            ],
        ),
        name=name,
        cost_estimate=BRIEF,
        compiler_params=pltpu.CompilerParams(
            dimension_semantics=("arbitrary",), vmem_limit_bytes=56 * MIB
        ),
    )(place, table, *map(hbm, tiles), hbm(vectors), hbm(down_w), *map(hbm, pieces))


def rows_forward(place, table, heads, x, pieces, down_w, vectors, peers, staged):
    slots, features = x.shape
    hidden = down_w.shape[0]
    outs = [
        ((peers, slots // peers, features), BF),
        ((slots, hidden), BF),
        ((slots, hidden), BF),
        ((features, slots), BF),
        ((slots, features), F32),
        ((slots, features), F32),
    ]
    return over_rows(
        rows_forward_kernel, "rows_forward", place, table, [heads, x], vectors, down_w, pieces, outs, staged
    )


def rows_backward(place, table, z1, z2, cot, slope, pieces, down_w, vectors, staged):
    slots, features = z1.shape
    hidden = down_w.shape[0]
    outs = [
        ((slots, hidden), BF),
        ((slots, features), BF),
        ((slots, features), F32),
        ((slots, features), BF),
        ((slots, features), BF),
        ((16, features), F32),
    ]
    return over_rows(
        rows_backward_kernel,
        "rows_backward",
        place,
        table,
        [z1, z2, cot, slope],
        vectors,
        down_w,
        pieces,
        outs,
        staged,
    )


def down_grad_kernel(cols_ref, g_ref, out_ref):
    out_ref[...] = tn(cols_ref[...], g_ref[...]).astype(BF)


def down_gradient(act, gffn):
    slots, hidden = act.shape
    features = gffn.shape[1]
    return pl.pallas_call(
        down_grad_kernel,
        out_shape=pinned((hidden, features), BF),
        grid=(hidden // features,),
        in_specs=[
            pl.BlockSpec((slots, features), lambda k: (0, k)),
            pl.BlockSpec((slots, features), lambda k: (0, 0)),
        ],
        out_specs=pl.BlockSpec((features, features), lambda k: (k, 0)),
        name="down_gradient",
        cost_estimate=pl.CostEstimate(
            flops=3 * 10**9, transcendentals=0, bytes_accessed=9 * MIB
        ),
        compiler_params=pltpu.CompilerParams(
            dimension_semantics=("arbitrary",), vmem_limit_bytes=40 * MIB
        ),
    )(hbm(act), hbm(gffn))


def up_grad_kernel(first, place_ref, turned_ref, g_ref, heads_ref, gbranch_ref, keep_ref, send_ref, full_ref):
    step = pl.program_id(0) + first

    @pl.when(step < 4)
    def _():
        full_ref[...] = nn(turned_ref[...], g_ref[...])

    @pl.when(step == 4)
    def _():
        full_ref[...] = nn(heads_ref[...], gbranch_ref[...])

    def put(ref, k, value):
        ref[k, 0] = value

    cut_rows(place_ref, full_ref, keep_ref, send_ref, put)


def up_gradient(place, nlow_t, gpre, heads_t, gbranch, first, blocks):
    features, slots = nlow_t.shape
    rows = features // 8
    cut = pinned((4, blocks, rows, features), BF)

    def whole(shape):
        return pl.BlockSpec(shape, lambda j, *_: (0, 0))

    return pl.pallas_call(
        functools.partial(up_grad_kernel, first),
        out_shape=[cut, cut],
        grid_spec=pltpu.PrefetchScalarGridSpec(
            num_scalar_prefetch=1,
            grid=(blocks,),
            in_specs=[
                whole((features, slots)),
                pl.BlockSpec((slots, features), lambda j, *_: (0, jnp.minimum(j + first, 3))),
                whole((features, slots)),
                whole((slots, features)),
            ],
            out_specs=[pl.BlockSpec((4, 1, rows, features), lambda j, *_: (0, j, 0, 0))] * 2,
            scratch_shapes=[pltpu.VMEM((features, features), F32)],
        ),
        name="up_gradient",
        cost_estimate=BRIEF,
        compiler_params=pltpu.CompilerParams(
            dimension_semantics=("arbitrary",), vmem_limit_bytes=40 * MIB
        ),
    )(place, *map(hbm, (nlow_t, gpre, heads_t, gbranch)))


def cut_rows(place_ref, full_ref, keep_ref, send_ref, at):
    rows = full_ref.shape[0] // 8
    for k in range(4):
        plane = (place_ref[0] >> 3) ^ k
        core = (place_ref[0] >> 2) & 1
        for swap, ref in ((0, keep_ref), (1, send_ref)):
            first = (plane * 2 + (core ^ swap)) * rows
            at(ref, k, full_ref[pl.ds(pl.multiple_of(first, 8), rows), :].astype(BF))


def attend_backward_kernel(
    staged,
    place_ref,
    tab_ref,
    qkv_ref,
    gh_ref,
    total_ref,
    xt_ref,
    terms_in_ref,
    g_ref,
    keep_ref,
    send_a_ref,
    send_b_ref,
    terms_ref,
    dk_ref,
    dv_ref,
    full_ref,
    kt_ref,
    gq_ref,
):
    group = pl.program_id(0)
    kind = tab_ref[0]
    slots, width = gh_ref.shape
    low = lax.broadcasted_iota(jnp.int32, (UNIT, 2 * HD), 1) < HD

    dk_ref[...] = jnp.zeros_like(dk_ref)
    dv_ref[...] = jnp.zeros_like(dv_ref)

    for unit in range(4):
        kt_ref[unit] = qkv_ref[1, unit * UNIT : (unit + 1) * UNIT, :].T

    def units(first_unit, count, keys):
        heads = width // HD
        tasks = [(first_unit + u, side) for u in range(count) for side in range(heads)]

        def places(which, side):
            first = tab_ref[1 + (group * heads + side) * 4 + which]
            return (
                first,
                slice(side // 2 * 2 * HD, (side // 2 + 1) * 2 * HD),
                pl.ds(pl.multiple_of(which * UNIT, UNIT), UNIT),
                pl.ds(pl.multiple_of(first * UNIT, UNIT), keys),
                low if side % 2 == 0 else ~low,
            )

        def lead(which, side):
            first, lanes, rows, key_rows, mine = places(which, side)
            own = jnp.where(mine, qkv_ref[0, rows, lanes], jnp.zeros((), BF))
            gown = jnp.where(mine, gh_ref[rows, lanes], jnp.zeros((), BF))
            return nt(qkv_ref[1, key_rows, lanes], own), nt(qkv_ref[2, key_rows, lanes], gown)

        def middle(which, side, scores, gprobs):
            probs = jnp.exp(scores - total_ref[side, which])
            inner = jnp.sum(gprobs * probs, axis=0, keepdims=True)
            return probs.astype(BF), (probs * (gprobs - inner)).astype(BF)

        def trail(which, side, probs, gscores):
            first, lanes, rows, key_rows, mine = places(which, side)
            own = jnp.where(mine, qkv_ref[0, rows, lanes], jnp.zeros((), BF))
            gown = jnp.where(mine, gh_ref[rows, lanes], jnp.zeros((), BF))
            dv_ref[key_rows, lanes] += nn(probs, gown)
            dk_ref[key_rows, lanes] += nn(gscores, own)
            part = sum(
                nn(
                    kt_ref[first + j, side * HD : (side + 1) * HD, :],
                    gscores[j * UNIT : (j + 1) * UNIT, :],
                )
                for j in range(keys // UNIT)
            )
            gq_ref[side * HD : (side + 1) * HD, :] = (part * HD**-0.5).astype(BF)
            if side == heads - 1:
                g_ref[0, rows, :] = gq_ref[...].T

        ahead, ready = lead(*tasks[0]), None
        for i, task in enumerate(tasks):
            now = ahead
            if i + 1 < len(tasks):
                ahead = lead(*tasks[i + 1])
            fresh = middle(*task, *now)
            if ready is not None:
                trail(*tasks[i - 1], *ready)
            ready = fresh
        trail(*tasks[-1], *ready)

    @pl.when(kind == 2)
    def _():
        lax.fori_loop(0, 1, lambda w, c: (units(w * 4, 4, 2 * UNIT), c)[1], 0)

    @pl.when(kind == 1)
    def _():
        lax.fori_loop(0, 1, lambda w, c: (units(w * 3, 3, UNIT), c)[1], 0)
        g_ref[0, 3 * UNIT :, :] = jnp.zeros((slots - 3 * UNIT, width), BF)

    @pl.when(kind == 0)
    def _():
        g_ref[0] = jnp.zeros((slots, width), BF)

    g_ref[1] = dk_ref[...].astype(BF)
    g_ref[2] = dv_ref[...].astype(BF)
    terms_ref[...] = terms_in_ref[...]
    terms_ref[0:1, :] = jnp.sum(g_ref[0].astype(F32), axis=0, keepdims=True)
    terms_ref[1:2, :] = jnp.sum(g_ref[2].astype(F32), axis=0, keepdims=True)
    for n in range(3):
        if not staged:
            keep_ref[n] = nn(xt_ref[...], g_ref[n]).astype(BF)
            continue
        full_ref[...] = nn(xt_ref[...], g_ref[n])
        rows = full_ref.shape[0] // 8

        def put(ref, k, value):
            if ref is keep_ref:
                keep_ref[k, n] = value
            else:
                at = ((k % 2) * 3 + n) * rows
                (send_a_ref if k < 2 else send_b_ref)[at : at + rows, :] = value

        cut_rows(place_ref, full_ref, keep_ref, None, put)
    if staged:
        send_b_ref[6 * rows :, :] = terms_ref[...].astype(BF)


def attend_backward(place, table, qkv, gheads, log_total, xt, terms, staged):
    _, slots, features = qkv.shape
    width = 4 * HD
    if staged:
        cut = pinned((4, 3, features // 8, features), BF)
        cut_spec = pl.BlockSpec((4, 3, features // 8, width), lambda g, *_: (0, 0, 0, g))
        heights = (6 * features // 8, 6 * features // 8 + 16)
    else:
        heights = (16, 16)
        cut = pinned((3, features, features), BF)
        cut_spec = pl.BlockSpec((3, features, width), lambda g, *_: (0, 0, g))
    grid_spec = pltpu.PrefetchScalarGridSpec(
        num_scalar_prefetch=2,
        grid=(features // width,),
        in_specs=[
            pl.BlockSpec((3, slots, width), lambda g, *_: (0, 0, g)),
            pl.BlockSpec((slots, width), lambda g, *_: (0, g)),
            pl.BlockSpec((4, 4, 1, UNIT), lambda g, *_: (g, 0, 0, 0)),
            pl.BlockSpec((features, slots), lambda g, *_: (0, 0)),
            pl.BlockSpec((16, width), lambda g, *_: (0, g)),
        ],
        out_specs=[
            pl.BlockSpec((3, slots, width), lambda g, *_: (0, 0, g)),
            cut_spec,
            *[pl.BlockSpec((h, width), lambda g, *_: (0, g)) for h in heights],
            pl.BlockSpec((16, width), lambda g, *_: (0, g)),
        ],
        scratch_shapes=[
            pltpu.VMEM((slots, width), F32),
            pltpu.VMEM((slots, width), F32),
            pltpu.VMEM((features, width), F32),
            pltpu.VMEM((4, width, UNIT), BF),
            pltpu.VMEM((width, UNIT), BF),
        ],
    )
    return pl.pallas_call(
        functools.partial(attend_backward_kernel, staged),
        out_shape=(
            pinned((3, slots, features), BF),
            cut,
            *[pinned((h, features), BF) for h in heights],
            pinned((16, features), F32),
        ),
        grid_spec=grid_spec,
        name="attend_backward",
        cost_estimate=BRIEF,
        compiler_params=pltpu.CompilerParams(
            dimension_semantics=("arbitrary",), vmem_limit_bytes=48 * MIB
        ),
    )(place, table, *map(hbm, (qkv, gheads, log_total, xt, terms)))


def chip_sums_kernel(keep_a_ref, got_a_ref, keep_b_ref, got_b_ref, *out_refs):
    for k in range(4):
        at = 0
        for keep_ref, got_ref in ((keep_a_ref, got_a_ref), (keep_b_ref, got_b_ref)):
            rows = keep_ref.shape[2]
            for j in range(keep_ref.shape[1]):

                @pl.when(pl.program_id(0) == k)
                def _():
                    out_refs[k][at : at + rows, :] = (
                        keep_ref[0, j].astype(F32) + got_ref[0, j].astype(F32)
                    ).astype(BF)

                at += rows


def chip_sums(*parts):
    blocks, rows, features = parts[0].shape[1] + parts[2].shape[1], *parts[0].shape[2:]
    return pl.pallas_call(
        chip_sums_kernel,
        out_shape=[pinned((blocks * rows, features), BF)] * 4,
        grid=(4,),
        in_specs=[pl.BlockSpec((1, *p.shape[1:]), lambda k: (k, 0, 0, 0)) for p in parts],
        out_specs=[pl.BlockSpec((blocks * rows, features), lambda k: (0, 0))] * 4,
        name="chip_sums",
        cost_estimate=BRIEF,
        compiler_params=pltpu.CompilerParams(vmem_limit_bytes=24 * MIB),
    )(*map(hbm, parts))


def chip_sums_q_kernel(keep_ref, got_a_ref, got_b_ref, terms_ref, *out_refs):
    rows = keep_ref.shape[2]
    terms = (terms_ref[...] + got_b_ref[6 * rows :, :].astype(F32)).astype(BF)
    for k in range(4):
        got_ref = got_a_ref if k < 2 else got_b_ref
        for n in range(3):
            at = ((k % 2) * 3 + n) * rows
            out_refs[k][n * rows : (n + 1) * rows, :] = (
                keep_ref[k, n].astype(F32) + got_ref[at : at + rows, :].astype(F32)
            ).astype(BF)
        out_refs[k][3 * rows :, :] = terms


def chip_sums_q(keep, got_a, got_b, terms):
    rows, features = keep.shape[2:]
    return pl.pallas_call(
        chip_sums_q_kernel,
        out_shape=[pinned((3 * rows + 16, features), BF)] * 4,
        grid=(1,),
        in_specs=[
            pl.BlockSpec(v.shape, lambda i, n=v.ndim: (0,) * n) for v in (keep, got_a, got_b, terms)
        ],
        out_specs=[pl.BlockSpec((3 * rows + 16, features), lambda i: (0, 0))] * 4,
        name="chip_sums_q",
        cost_estimate=BRIEF,
        compiler_params=pltpu.CompilerParams(vmem_limit_bytes=32 * MIB),
    )(hbm(keep), hbm(got_a), hbm(got_b), hbm(terms))


def plane_sums_kernel(pieces, place_ref, a_ref, b_ref, c_ref, d_ref, *refs):
    out_refs, full_ref = refs[:-1], refs[-1]
    each = 4 // len(out_refs)
    height = out_refs[0].shape[0] // each
    full_ref[...] = (
        a_ref[...].astype(F32)
        + b_ref[...].astype(F32)
        + c_ref[...].astype(F32)
        + d_ref[...].astype(F32)
    )
    rep = place_ref[0] & 3
    for k in range(4):
        for base, rows, at in pieces:
            first = base + (rep ^ k) * rows if rows else base
            rows = rows or 16
            at = at + (k % each) * height
            out_refs[k // each][at : at + rows, :] = full_ref[
                pl.ds(pl.multiple_of(first, 8), rows), :
            ].astype(BF)


def plane_sums(place, parts, pieces, height, arrays=4):
    rows, features = parts[0].shape
    return pl.pallas_call(
        functools.partial(plane_sums_kernel, pieces),
        out_shape=[pinned((height * 4 // arrays, features), BF)] * arrays,
        grid_spec=pltpu.PrefetchScalarGridSpec(
            num_scalar_prefetch=1,
            grid=(1,),
            in_specs=[pl.BlockSpec((rows, features), lambda i, *_: (0, 0))] * 4,
            out_specs=[pl.BlockSpec((height * 4 // arrays, features), lambda i, *_: (0, 0))] * arrays,
            scratch_shapes=[pltpu.VMEM((rows, features), F32)],
        ),
        name="plane_sums",
        cost_estimate=BRIEF,
        compiler_params=pltpu.CompilerParams(vmem_limit_bytes=32 * MIB),
    )(place, *map(hbm, parts))


def input_grad_kernel(tab_ref, gres_ref, g_ref, w_ref, out_ref):
    kind = tab_ref[0]
    live = jnp.where(kind == 2, 4, jnp.where(kind == 1, 3, 0))
    tile = pl.program_id(0)

    @pl.when(tile < live)
    def _():
        total = gres_ref[...]
        for n in range(3):
            total = total + nt(g_ref[n], w_ref[n])
        out_ref[...] = total

    @pl.when(tile >= live)
    def _():
        out_ref[...] = jnp.zeros_like(out_ref)


def input_gradient(table, gres, grads, qkv_w):
    slots, features = gres.shape
    grid_spec = pltpu.PrefetchScalarGridSpec(
        num_scalar_prefetch=1,
        grid=(slots // UNIT,),
        in_specs=[
            pl.BlockSpec((UNIT, features), lambda i, *_: (i, 0)),
            pl.BlockSpec((3, UNIT, features), lambda i, *_: (0, i, 0)),
            pl.BlockSpec((3, features, features), lambda i, *_: (0, 0, 0)),
        ],
        out_specs=pl.BlockSpec((UNIT, features), lambda i, *_: (i, 0)),
    )
    return pl.pallas_call(
        input_grad_kernel,
        out_shape=pinned((slots, features), F32),
        grid_spec=grid_spec,
        name="input_gradient",
        cost_estimate=BRIEF,
        compiler_params=pltpu.CompilerParams(
            dimension_semantics=("arbitrary",), vmem_limit_bytes=40 * MIB
        ),
    )(table, hbm(gres), hbm(grads), hbm(qkv_w))


def gather_line_kernel(place_ref, *refs, blocks):
    full_ref, out_ref = refs[5], refs[4]
    rep = place_ref[0] & 3
    own = refs[0].shape[0] // blocks if refs[0].shape[0] % blocks == 0 else (refs[0].shape[0] - 16) // blocks
    for k in range(4):
        for n in range(blocks):
            full_ref[pl.ds(pl.multiple_of((n * 4 + (rep ^ k)) * own, 8), own), :] = refs[k][
                n * own : (n + 1) * own, :
            ].astype(F32)
    out_ref[: blocks * 4 * own, :] = full_ref[...].astype(BF)
    if out_ref.shape[0] > blocks * 4 * own:
        total = refs[0][blocks * own :, :].astype(F32)
        for k in (1, 2, 3):
            total = total + refs[k][blocks * own :, :].astype(F32)
        out_ref[blocks * 4 * own :, :] = total.astype(BF)


def gather_line(place, parts, blocks, extra):
    rows, features = parts[0].shape
    height = (rows - extra) * 4
    return pl.pallas_call(
        functools.partial(gather_line_kernel, blocks=blocks),
        out_shape=pinned((height + extra, features), BF),
        grid_spec=pltpu.PrefetchScalarGridSpec(
            num_scalar_prefetch=1,
            grid=(1,),
            in_specs=[pl.BlockSpec((rows, features), lambda i, *_: (0, 0))] * 4,
            out_specs=pl.BlockSpec((height + extra, features), lambda i, *_: (0, 0)),
            scratch_shapes=[pltpu.VMEM((height, features), F32)],
        ),
        name="gather_line",
        cost_estimate=BRIEF,
        compiler_params=pltpu.CompilerParams(vmem_limit_bytes=16 * MIB),
    )(place, *parts)


def to_peers_kernel(spans_ref, rows_ref, out_ref):
    peers, per_peer = out_ref.shape[:2]
    some = per_peer * 3 // 4
    for peer in range(peers):
        start = pl.multiple_of(spans_ref[peer], 32)

        @pl.when(spans_ref[peers + peer] == per_peer)
        def _():
            out_ref[peer] = rows_ref[pl.ds(start, per_peer), :]

        @pl.when(spans_ref[peers + peer] == some)
        def _():
            out_ref[peer, :some, :] = rows_ref[pl.ds(start, some), :]
            out_ref[peer, some:, :] = jnp.zeros_like(out_ref[peer, some:, :])

        @pl.when(spans_ref[peers + peer] == 0)
        def _():
            out_ref[peer] = jnp.zeros_like(out_ref[peer])


def from_peers_kernel(spans_ref, in_ref, rows_ref):
    peers, per_peer = in_ref.shape[:2]
    some = per_peer * 3 // 4
    for peer in range(peers):
        start = pl.multiple_of(spans_ref[peer], 32)

        @pl.when(spans_ref[peers + peer] == per_peer)
        def _():
            rows_ref[pl.ds(start, per_peer), :] = in_ref[peer]

        @pl.when(spans_ref[peers + peer] == some)
        def _():
            rows_ref[pl.ds(start, some), :] = in_ref[peer, :some, :]


def between_layouts(kernel, name, spans, x, shape):
    return pl.pallas_call(
        kernel,
        out_shape=pinned(shape, BF),
        grid_spec=pltpu.PrefetchScalarGridSpec(
            num_scalar_prefetch=1,
            grid=(1,),
            in_specs=[pl.BlockSpec(x.shape, lambda i, *_: (0,) * x.ndim)],
            out_specs=pl.BlockSpec(shape, lambda i, *_: (0,) * len(shape)),
        ),
        name=name,
        cost_estimate=BRIEF,
        compiler_params=pltpu.CompilerParams(vmem_limit_bytes=16 * MIB),
    )(spans, x)


def seq_swap(x, k):
    n = lax.axis_size("seq")
    return lax.ppermute(x, "seq", [(i, i ^ k) for i in range(n)])


def rep_swap(x, k):
    n = lax.axis_size("rep")
    return lax.ppermute(x, "rep", [(i, i ^ k) for i in range(n)])


def key_table(own_kind, perm_two, perm_three):
    quarters = jnp.arange(4)
    halves = quarters // 2
    pick_two = jnp.sum(
        jnp.where(halves[None, :, None] == jnp.arange(2)[None, None, :], perm_two[:, None, :], 0),
        axis=-1,
    )
    pick_three = jnp.sum(
        jnp.where(
            jnp.minimum(quarters, 2)[None, :, None] == jnp.arange(3)[None, None, :],
            perm_three[:, None, :],
            0,
        ),
        axis=-1,
    )
    first = jnp.where(own_kind == 2, 2 * pick_two, pick_three)
    return jnp.concatenate([own_kind.reshape(1), first.reshape(-1)]).astype(jnp.int32)


def placed(vector, rows, offset, features):
    lane = lax.broadcasted_iota(jnp.int32, (vector.shape[-1], features), 1)
    entry = lax.broadcasted_iota(jnp.int32, (vector.shape[-1], features), 0)
    return jnp.dot(vector, (lane == entry + offset).astype(BF), preferred_element_type=F32)


def shards(
    inputs,
    item_kind,
    perm_two,
    perm_three,
    qkv_weight,
    qv_bias,
    out_weight,
    out_bias,
    up_weight,
    up_bias,
    down_weight,
    down_bias,
    norm_gain,
    norm_bias,
    cotangent,
):
    peers = lax.axis_size("seq")
    copies = lax.axis_size("rep")
    seq = lax.axis_index("seq")
    rep = lax.axis_index("rep")
    x = inputs[0]
    slots, features = x.shape
    tokens = cotangent.shape[1]
    hidden = up_weight.shape[1]
    quarter = slots // 4
    per_peer = slots // peers
    staged = peers == 8 and copies == 4
    own = out_weight.shape[0]

    kind_row = item_kind[0]
    own_kind = jnp.sum(jnp.where(jnp.arange(peers) == seq, kind_row, 0))
    table = key_table(own_kind, perm_two, perm_three)

    per_pair = (
        jnp.where(kind_row == 2, 4 * quarter, jnp.where(kind_row == 1, 3 * quarter, 0)) // peers
    )
    earlier = jnp.arange(peers)[:, None] < jnp.arange(peers)[None, :]
    range_starts = jnp.sum(jnp.where(earlier, per_pair[:, None], 0), axis=0)
    spans = jnp.concatenate([range_starts, per_pair]).astype(jnp.int32)

    place = (seq * copies + rep).astype(jnp.int32).reshape(1)
    index = seq * copies + rep
    core, plane = seq & 1, seq >> 1
    fan = 4 * own
    up_row = (index * fan) // features
    together = lax.optimization_barrier

    def swap_rows(rows):
        return lax.all_to_all(rows, "seq", split_axis=0, concat_axis=0, tiled=True)

    turned = x.T
    if staged:
        down_w = lax.all_gather(down_weight, AXES, axis=0, tiled=True)

        def along_rep(piece):
            return [piece] + [rep_swap(piece, k) for k in (1, 2, 3)]

        def along_plane(piece):
            return [piece] + [seq_swap(piece, 2 * k) for k in (1, 2, 3)]

        def both_cores(parts):
            return parts + [seq_swap(p, 1) for p in parts]

        small = jnp.concatenate([qv_bias, out_bias[None], down_bias[None], norm_gain, norm_bias])
        small = placed(small, 8, index * own, features)
        spread = placed(up_bias[None], 1, index * fan - up_row * features, features)
        spread = jnp.where(jnp.arange(4)[:, None] == up_row, spread, 0.0)
        vectors = jnp.concatenate(
            [small[0:3], spread, small[3:8], jnp.zeros((4, features), F32)]
        ).astype(BF)

        first = along_rep(jnp.concatenate([qkv_weight.reshape(3 * own, features), vectors]))
        second = jnp.concatenate(
            [out_weight] + [up_weight[:, c : c + features] for c in range(0, hidden, features)]
        )
        near = rep_swap(second, 1)
        picked = between_layouts(
            to_peers_kernel, "to_peers", spans, cotangent[0], (peers, per_peer, features)
        )
        turned, near, *first = together((turned, near, *first))
        first = gather_line(place, first, 3, 16)
        pair = jnp.concatenate([second, near])
        pair, first = together((pair, first))
        far = rep_swap(pair, 2)
        first = along_plane(first)
        second = gather_line(place, [pair[: 5 * own], pair[5 * own :], far[: 5 * own], far[5 * own :]], 5, 0)
        second, picked, *first = together((second, picked, *first))
        first = both_cores(first)
        second = along_plane(second)
        vectors = sum(p[12 * own :].astype(F32) for p in first)
        qkv, heads, heads_t, log_total, qkv_w = attend_forward(place, table, x, first, vectors)
        heads, picked, *second = together((heads, picked, *second))
        cot = swap_rows(picked)
        pieces = both_cores(second)
    else:

        def gathered(v, axis):
            return lax.all_gather(v, AXES, axis=axis, tiled=True)

        qkv_all = gathered(qkv_weight, 1)
        pieces = [gathered(out_weight, 0), gathered(up_weight, 0)]
        down_w = gathered(down_weight, 0)
        vectors = jnp.concatenate(
            [
                gathered(qv_bias, 1),
                gathered(out_bias, 0)[None],
                gathered(up_bias, 0).reshape(4, features),
                gathered(down_bias, 0)[None],
                gathered(norm_gain, 1),
                gathered(norm_bias, 1),
                jnp.zeros((4, features), BF),
            ]
        ).astype(F32)
        levels = jnp.arange(per_peer)[None, :]
        targets = jnp.minimum(range_starts[:, None] + levels, tokens - 1)
        cot = swap_rows(cotangent[0][targets])
        qkv, heads, heads_t, log_total, qkv_w = attend_forward(place, table, x, [qkv_all], vectors)

    out, act, slope, nlow_t, z1, z2 = rows_forward(
        place, table, heads, x, pieces, down_w, vectors, peers, staged
    )
    moved = swap_rows(out)
    z1, cot = together((z1, cot))
    gpre, gffn, gres, gbranch, gheads, terms = rows_backward(
        place, table, z1, z2, cot, slope, pieces, down_w, vectors, staged
    )
    gffn, moved = together((gffn, moved))

    if staged:

        def over_plane(parts):
            return [parts[0]] + [seq_swap(parts[k], 2 * k) for k in (1, 2, 3)]

        def over_rep(parts):
            return [parts[0]] + [rep_swap(parts[k], k) for k in (1, 2, 3)]

        def total_of(parts):
            total = parts[0].astype(F32)
            for p in parts[1:]:
                total = total + p.astype(F32)
            return total

        down_grad = down_gradient(act, gffn)
        down_out = lax.psum_scatter(down_grad, AXES, scatter_dimension=0, tiled=True).astype(F32)
        gpre, down_grad = together((gpre, down_grad))
        keep_a, send_a = up_gradient(place, nlow_t, gpre, heads_t, gbranch, 0, 3)
        got_a = seq_swap(send_a, 1)
        gbranch, keep_a = together((gbranch, keep_a))
        keep_b, send_b = up_gradient(place, nlow_t, gpre, heads_t, gbranch, 3, 2)
        got_b = seq_swap(send_b, 1)
        output = between_layouts(from_peers_kernel, "from_peers", spans, moved, (tokens, features))
        got_a, got_b, output = together((got_a, got_b, output))
        parts = chip_sums(keep_a, got_a, keep_b, got_b)
        gheads, *parts = together((gheads, *parts))
        parts = over_plane(parts)
        grads, keep_q, send_a, send_b, terms = attend_backward(
            place, table, qkv, gheads, log_total, turned, terms, staged
        )
        send_a, send_b, *parts = together((send_a, send_b, *parts))
        got_a, got_b = seq_swap(send_a, 1), seq_swap(send_b, 1)
        parts_q = chip_sums_q(keep_q, got_a, got_b, terms)
        grads, *parts_q = together((grads, *parts_q))
        parts_q = over_plane(parts_q)
        input_grad = input_gradient(table, gres, grads, qkv_w)
        input_grad, *parts = together((input_grad, *parts))
        pieces = [(4 * own * j, own, own * j) for j in range(5)]
        height = 5 * own
        near, far = plane_sums(place, parts, pieces, height, 2)
        far = rep_swap(far, 2)
        near, *parts_q = together((near, *parts_q))
        pieces = [(4 * own * n, own, own * n) for n in range(3)] + [(12 * own, 0, 3 * own)]
        parts_q = over_rep(plane_sums(place, parts_q, pieces, 3 * own + 16))
        near = near.astype(F32) + far.astype(F32)
        far = rep_swap(near[height:].astype(BF), 1)
        total = near[:height] + far.astype(F32)
        up_out = jnp.concatenate([total[own * j : own * (j + 1)] for j in range(4)], axis=1)
        out_out = total[4 * own :]
        last = total_of(parts_q)
        qkv_out = last[: 3 * own].reshape(3, own, features)
        sums = last[3 * own :]
        mine = lax.dynamic_slice(sums, (0, index * own), (16, own))
        up_bias_out = lax.dynamic_slice(
            sums, (3 + up_row, index * fan - up_row * features), (1, fan)
        )[0]
        qv_out, out_bias_out, down_bias_out = mine[0:2], mine[2], mine[7]
        gain_out, shift_out = mine[8:10], mine[10:12]
    else:

        def reduced(v, axis):
            return lax.psum_scatter(v.astype(F32), AXES, scatter_dimension=axis, tiled=True)

        grads, qkv_grad, _, _, terms = attend_backward(
            place, table, qkv, gheads, log_total, turned, terms, staged
        )
        input_grad = input_gradient(table, gres, grads, qkv_w)
        down_out = reduced(tn(act, gffn), 0)
        up_out = reduced(nn(nlow_t, gpre), 0)
        out_out = reduced(nn(heads_t, gbranch), 0)
        qkv_out = reduced(qkv_grad, 1)
        qv_out = reduced(terms[0:2], 1)
        out_bias_out = reduced(terms[2], 0)
        up_bias_out = reduced(terms[3:7].reshape(hidden), 0)
        down_bias_out = reduced(terms[7], 0)
        gain_out = reduced(terms[8:10], 1)
        shift_out = reduced(terms[10:12], 1)
        positions = jnp.arange(tokens)
        ends = range_starts + per_pair
        sources = jnp.sum((ends[None, :] <= positions[:, None]).astype(jnp.int32), axis=1)
        opening = jnp.sum(
            jnp.where(jnp.arange(peers)[None, :] == sources[:, None], range_starts[None, :], 0),
            axis=1,
        )
        arrivals = sources * per_peer + positions - opening
        output = moved.reshape(slots, features)[arrivals]

    return (
        output[None],
        input_grad[None],
        qkv_out,
        qv_out,
        out_out,
        out_bias_out,
        up_out,
        up_bias_out,
        down_out,
        down_bias_out,
        gain_out,
        shift_out,
    )


def solution(mesh):
    both = ("seq", "rep")
    in_specs = (
        P("rep", "seq", None),
        P("rep", None),
        P(),
        P(),
        P(None, both, None),
        P(None, both),
        P(both, None),
        P(both),
        P(both, None),
        P(both),
        P(both, None),
        P(both),
        P(None, both),
        P(None, both),
        P("rep", "seq", None),
    )
    out_specs = (
        P("rep", "seq", None),
        P("rep", "seq", None),
        P(None, both, None),
        P(None, both),
        P(both, None),
        P(both),
        P(both, None),
        P(both),
        P(both, None),
        P(both),
        P(None, both),
        P(None, both),
    )
    return jax.shard_map(shards, mesh=mesh, in_specs=in_specs, out_specs=out_specs, check_vma=False)
```

```python
import functools

import jax
import jax.numpy as jnp
from jax import lax
from jax.experimental import pallas as pl
from jax.experimental.pallas import tpu as pltpu
from jax.sharding import PartitionSpec as P

HD = 64
CHUNK = 256
UNIT = 256
EPSILON = 1e-05
BF = jnp.bfloat16
F32 = jnp.float32
AXES = ("seq", "rep")
MIB = 1 << 20
BRIEF = pl.CostEstimate(flops=1000, transcendentals=0, bytes_accessed=1000)


def hbm(x):
    return pltpu.with_memory_space_constraint(x, pltpu.HBM)


def pinned(shape, dtype):
    return pltpu.HBM(shape, dtype)


TAIL_P = 0.4 * 0.7071067811865476
TAIL_C = tuple(
    0.5 * c
    for c in (
        0.23192178895457838,
        0.16182559848968434,
        0.46826879780965075,
        -0.3709009174795544,
        0.7091427810415396,
        -0.20025807634318435,
    )
)
BELL = -0.7213475204444817
RSQRT2PI = 0.3989422804014327


def nn(a, b):
    return lax.dot_general(a, b, (((1,), (0,)), ((), ())), preferred_element_type=F32)


def nt(a, b):
    return lax.dot_general(a, b, (((1,), (1,)), ((), ())), preferred_element_type=F32)


def tn(a, b):
    return lax.dot_general(a, b, (((0,), (0,)), ((), ())), preferred_element_type=F32)


def gelu_parts(x):
    t = 1.0 / (1.0 + TAIL_P * jnp.abs(x))
    poly = TAIL_C[-1] * t + TAIL_C[-2]
    for c in TAIL_C[-3::-1]:
        poly = poly * t + c
    bell = jnp.exp2(x * x * BELL)
    tail = poly * t * bell
    phi = jnp.where(x >= 0, 1.0 - tail, tail)
    return x * phi, phi + x * bell * RSQRT2PI


def start_pieces(place_ref, refs, copies, sem):
    for swap in range(2):
        for plane in range(4):
            device = (place_ref[0] >> 2) ^ (plane * 2 + swap)
            for first, rows, target in copies:
                pltpu.make_async_copy(
                    refs[swap * 4 + plane].at[pl.ds(first, rows), :], target(device), sem
                ).start()


def wait_whole(ref, sem):
    pltpu.make_async_copy(ref, ref, sem).wait()


def attend_forward_kernel(
    staged, place_ref, tab_ref, x_ref, b_ref, *refs
):
    count = 8 if staged else 1
    pieces = refs[:count]
    qkv_ref, heads_ref, turned_ref, total_ref, keep_ref = refs[count : count + 5]
    w_ref, vt_ref, sem, keep_sem = refs[count + 5 :]
    group = pl.program_id(0)
    kind = tab_ref[0]
    slots, width = heads_ref.shape
    features = x_ref.shape[1]
    low = lax.broadcasted_iota(jnp.int32, (UNIT, 2 * HD), 1) < HD
    keep = pltpu.make_async_copy(w_ref, keep_ref, keep_sem)

    @pl.when(group == 0)
    def _():
        if staged:
            rows = features // 8

            def target(n):
                return lambda d: w_ref.at[n, pl.ds(pl.multiple_of(d * rows, 32), rows), :]

            start_pieces(
                place_ref, pieces, [(n * rows, rows, target(n)) for n in range(3)], sem
            )
        else:
            pltpu.make_async_copy(pieces[0], w_ref, sem).start()
        wait_whole(w_ref, sem)
        keep.start()

    @pl.when(group == pl.num_programs(0) - 1)
    def _():
        keep.wait()

    cols = pl.ds(pl.multiple_of(group * width, width), width)

    def project(n, bias, scale):
        weight = w_ref[n, :, cols]
        for r in range(0, slots, UNIT):
            acc = nn(x_ref[r : r + UNIT, :], weight)
            if bias is not None:
                acc = acc + bias
            acc = acc.astype(BF)
            if scale is not None:
                acc = acc * jnp.asarray(scale, BF)
            qkv_ref[n, r : r + UNIT, :] = acc

    project(0, b_ref[0:1, :], HD**-0.5)
    project(1, None, None)
    project(2, b_ref[1:2, :], None)

    for unit in range(4):
        vt_ref[unit] = qkv_ref[2, unit * UNIT : (unit + 1) * UNIT, :].T

    def units(first_unit, count, keys):
        heads = width // HD
        tasks = [(first_unit + u, side) for u in range(count) for side in range(heads)]

        def rows_of(which):
            return pl.ds(pl.multiple_of(which * UNIT, UNIT), UNIT)

        def start_of(which, side):
            return tab_ref[1 + (group * heads + side) * 4 + which]

        def score(which, side):
            lanes = slice(side // 2 * 2 * HD, (side // 2 + 1) * 2 * HD)
            key_rows = pl.ds(pl.multiple_of(start_of(which, side) * UNIT, UNIT), keys)
            mine = low if side % 2 == 0 else ~low
            own = jnp.where(mine, qkv_ref[0, rows_of(which), lanes], jnp.zeros((), BF))
            return nt(qkv_ref[1, key_rows, lanes], own)

        def soften(which, side, scores):
            largest = jnp.max(scores, axis=0, keepdims=True)
            expon = jnp.exp(scores - largest)
            total = jnp.sum(expon, axis=0, keepdims=True)
            total_ref[side, which] = largest + jnp.log(total)
            return expon.astype(BF), 1.0 / total

        def blend(which, side, expon, inverse):
            part = sum(
                nn(
                    vt_ref[start_of(which, side) + j, side * HD : (side + 1) * HD, :],
                    expon[j * UNIT : (j + 1) * UNIT, :],
                )
                for j in range(keys // UNIT)
            )
            part = (part * inverse).astype(BF)
            turned_ref[side * HD : (side + 1) * HD, rows_of(which)] = part
            if side == heads - 1:
                heads_ref[rows_of(which), :] = turned_ref[:, rows_of(which)].T

        ahead, soft = score(*tasks[0]), None
        for i, task in enumerate(tasks):
            now = ahead
            if i + 1 < len(tasks):
                ahead = score(*tasks[i + 1])
            fresh = soften(*task, now)
            if soft is not None:
                blend(*tasks[i - 1], *soft)
            soft = fresh
        blend(*tasks[-1], *soft)

    @pl.when(kind == 2)
    def _():
        lax.fori_loop(0, 1, lambda w, c: (units(w * 4, 4, 2 * UNIT), c)[1], 0)

    @pl.when(kind == 1)
    def _():
        lax.fori_loop(0, 1, lambda w, c: (units(w * 3, 3, UNIT), c)[1], 0)
        heads_ref[3 * UNIT :, :] = jnp.zeros((slots - 3 * UNIT, width), BF)
        turned_ref[:, 3 * UNIT :] = jnp.zeros((width, slots - 3 * UNIT), BF)

    @pl.when(kind == 0)
    def _():
        heads_ref[...] = jnp.zeros_like(heads_ref)
        turned_ref[...] = jnp.zeros_like(turned_ref)


def attend_forward(place, table, x, pieces, vectors):
    slots, features = x.shape
    width = 4 * HD
    staged = len(pieces) == 8
    grid_spec = pltpu.PrefetchScalarGridSpec(
        num_scalar_prefetch=2,
        grid=(features // width,),
        in_specs=[
            pl.BlockSpec((slots, features), lambda g, *_: (0, 0)),
            pl.BlockSpec((16, width), lambda g, *_: (0, g)),
        ]
        + [pl.BlockSpec(memory_space=pl.ANY)] * len(pieces),
        out_specs=[
            pl.BlockSpec((3, slots, width), lambda g, *_: (0, 0, g)),
            pl.BlockSpec((slots, width), lambda g, *_: (0, g)),
            pl.BlockSpec((width, slots), lambda g, *_: (g, 0)),
            pl.BlockSpec((4, 4, 1, UNIT), lambda g, *_: (g, 0, 0, 0)),
            pl.BlockSpec(memory_space=pl.ANY),
        ],
        scratch_shapes=[
            pltpu.VMEM((3, features, features), BF),
            pltpu.VMEM((4, width, UNIT), BF),
            pltpu.SemaphoreType.DMA(()),
            pltpu.SemaphoreType.DMA(()),
        ],
    )
    return pl.pallas_call(
        functools.partial(attend_forward_kernel, staged),
        out_shape=(
            pinned((3, slots, features), BF),
            pinned((slots, features), BF),
            pinned((features, slots), BF),
            pinned((features // HD, 4, 1, UNIT), F32),
            pinned((3, features, features), BF),
        ),
        grid_spec=grid_spec,
        name="attend_forward",
        cost_estimate=BRIEF,
        compiler_params=pltpu.CompilerParams(
            dimension_semantics=("arbitrary",), vmem_limit_bytes=48 * MIB
        ),
    )(place, table, hbm(x), vectors, *map(hbm, pieces))


def norm_forward(z):
    center = z - jnp.mean(z, axis=-1, keepdims=True)
    spread = jnp.mean(center * center, axis=-1, keepdims=True)
    scale = lax.rsqrt(spread + EPSILON)
    return center * scale, scale


def norm_backward(gx, xhat, scale):
    return (
        gx
        - jnp.mean(gx, axis=-1, keepdims=True)
        - xhat * jnp.mean(gx * xhat, axis=-1, keepdims=True)
    ) * scale


def live_tiles(tab_ref):
    kind = tab_ref[0]
    return jnp.where(kind == 2, 4, jnp.where(kind == 1, 3, 0))


def start_weights(staged, place_ref, pieces, down_ref, ow_ref, uw_ref, dw_ref, sems):
    features = ow_ref.shape[0]
    if staged:
        rows = features // 8

        def out_rows(d):
            return ow_ref.at[pl.ds(pl.multiple_of(d * rows, 32), rows), :]

        def up_rows(j):
            lanes = pl.ds(j * features, features)
            return lambda d: uw_ref.at[pl.ds(pl.multiple_of(d * rows, 32), rows), lanes]

        start_pieces(place_ref, pieces, [(0, rows, out_rows)], sems.at[0])
        start_pieces(
            place_ref, pieces, [((1 + j) * rows, rows, up_rows(j)) for j in range(4)], sems.at[1]
        )
    else:
        pltpu.make_async_copy(pieces[0], ow_ref, sems.at[0]).start()
        pltpu.make_async_copy(pieces[1], uw_ref, sems.at[1]).start()
    pltpu.make_async_copy(down_ref, dw_ref, sems.at[2]).start()


def rows_forward_kernel(staged, place_ref, tab_ref, heads_ref, x_ref, vec_ref, down_ref, *refs):
    count = 8 if staged else 2
    pieces = refs[:count]
    written = refs[count : count + 6]
    out_ref, act_ref, slope_ref, nlow_ref, z1_ref, z2_ref = written
    mixed_ref, ow_ref, uw_ref, dw_ref, sems = refs[count + 6 :]
    tile = pl.program_id(0)
    live = live_tiles(tab_ref)
    features = x_ref.shape[1]
    hidden = uw_ref.shape[1]
    peers, levels = out_ref.shape[:2]

    @pl.when(tile >= live)
    def _():
        for ref in written:
            ref[...] = jnp.zeros_like(ref)

    @pl.when((tile == 0) & (live > 0))
    def _():
        start_weights(staged, place_ref, pieces, down_ref, ow_ref, uw_ref, dw_ref, sems)

    @pl.when(tile < live)
    def _():
        def vec(i):
            return vec_ref[i : i + 1, :]

        def arrive(ref, i):
            pl.when(tile == 0)(lambda: wait_whole(ref, sems.at[i]))

        arrive(ow_ref, 0)
        z1 = x_ref[...].astype(F32) + nn(heads_ref[...], ow_ref[...]) + vec(2)
        z1_ref[...] = z1
        normed = norm_forward(z1)[0] * vec(8) + vec(10)
        nlow = normed.astype(BF)
        nlow_ref[...] = nlow.T
        chunks = [slice(c, c + CHUNK) for c in range(0, hidden, CHUNK)]

        def lead(c):
            bias = vec_ref[3 + c.start // features, c.start % features : c.start % features + CHUNK]
            return nn(nlow, uw_ref[:, c]) + bias[None, :]

        arrive(uw_ref, 1)
        arrive(dw_ref, 2)
        ahead, ready, ffn = lead(chunks[0]), None, normed + vec(7)
        for i, c in enumerate(chunks):
            now = ahead
            if i + 1 < len(chunks):
                ahead = lead(chunks[i + 1])
            active, slope = gelu_parts(now)
            active = active.astype(BF)
            act_ref[:, c] = active
            slope_ref[:, c] = slope.astype(BF)
            if ready is not None:
                ffn = ffn + nn(ready, dw_ref[chunks[i - 1], :])
            ready = active
        z2 = ffn + nn(ready, dw_ref[chunks[-1], :])
        z2_ref[...] = z2
        result = norm_forward(z2)[0] * vec(9) + vec(11)
        for j in range(features // 128):
            lanes = slice(j * 128, (j + 1) * 128)
            mixed_ref[j] = result[:, lanes]
            for peer in range(peers):
                out_ref[peer, :, lanes] = mixed_ref[j, pl.ds(peer, levels, stride=peers), :].astype(BF)


def rows_backward_kernel(
    staged, place_ref, tab_ref, z1_ref, z2_ref, cot_ref, slope_ref, vec_ref, down_ref, *refs
):
    count = 8 if staged else 2
    pieces = refs[:count]
    written = refs[count : count + 5]
    gpre_ref, gffn_ref, gres_ref, gbranch_ref, gheads_ref = written
    terms_ref, mixed_ref, ow_ref, uw_ref, dw_ref, sems = refs[count + 5 :]
    tile = pl.program_id(0)
    live = live_tiles(tab_ref)
    features = z1_ref.shape[1]
    hidden = uw_ref.shape[1]
    peers, levels = cot_ref.shape[:2]

    @pl.when(tile == 0)
    def _():
        terms_ref[...] = jnp.zeros_like(terms_ref)

    @pl.when(tile >= live)
    def _():
        for ref in written:
            ref[...] = jnp.zeros_like(ref)

    @pl.when((tile == 0) & (live > 0))
    def _():
        start_weights(staged, place_ref, pieces, down_ref, ow_ref, uw_ref, dw_ref, sems)

    @pl.when(tile < live)
    def _():
        def vec(i):
            return vec_ref[i : i + 1, :]

        def arrive(ref, i):
            pl.when(tile == 0)(lambda: wait_whole(ref, sems.at[i]))

        def add(i, value):
            terms_ref[i : i + 1, :] += jnp.sum(value, axis=0, keepdims=True)

        cot = []
        for j in range(features // 128):
            lanes = slice(j * 128, (j + 1) * 128)
            for peer in range(peers):
                mixed_ref[j, pl.ds(peer, levels, stride=peers), :] = cot_ref[peer, :, lanes].astype(F32)
            cot.append(mixed_ref[j])
        cot = jnp.concatenate(cot, axis=1)
        xhat2, scale2 = norm_forward(z2_ref[...])
        add(9, cot * xhat2)
        add(11, cot)
        gres2 = norm_backward(cot * vec(9), xhat2, scale2)
        gffn = gres2.astype(BF)
        gffn_ref[...] = gffn
        add(7, gffn.astype(F32))
        chunks = [slice(c, c + CHUNK) for c in range(0, hidden, CHUNK)]

        def lead(c):
            return nt(gffn, dw_ref[c, :])

        arrive(dw_ref, 2)
        arrive(uw_ref, 1)
        arrive(ow_ref, 0)
        ahead, ready, gmoved = lead(chunks[0]), None, gres2
        for i, c in enumerate(chunks):
            now = ahead
            if i + 1 < len(chunks):
                ahead = lead(chunks[i + 1])
            gpre = (now * slope_ref[:, c].astype(F32)).astype(BF)
            gpre_ref[:, c] = gpre
            row, lanes = 3 + c.start // features, slice(c.start % features, c.start % features + CHUNK)
            terms_ref[row : row + 1, lanes] += jnp.sum(gpre.astype(F32), axis=0, keepdims=True)
            if ready is not None:
                gmoved = gmoved + nt(ready, uw_ref[:, chunks[i - 1]])
            ready = gpre
        gmoved = gmoved + nt(ready, uw_ref[:, chunks[-1]])
        xhat1, scale1 = norm_forward(z1_ref[...])
        add(8, gmoved * xhat1)
        add(10, gmoved)
        gres1 = norm_backward(gmoved * vec(8), xhat1, scale1)
        gres_ref[...] = gres1
        gbranch = gres1.astype(BF)
        gbranch_ref[...] = gbranch
        add(2, gbranch.astype(F32))
        gheads_ref[...] = nt(gbranch, ow_ref[...]).astype(BF)


def over_rows(kernel, name, place, table, tiles, vectors, down_w, pieces, outs, staged):
    features, hidden = down_w.shape[1], down_w.shape[0]
    slots = tiles[0].shape[0]

    def spec(shape):
        if len(shape) == 3 and shape[0] * shape[1] != slots:
            levels = UNIT // shape[0]
            last = shape[1] // levels - 1
            return pl.BlockSpec(
                (shape[0], levels, features), lambda i, place, tab: (0, jnp.minimum(tab[49] + i, last), 0)
            )
        if len(shape) == 3:
            return pl.BlockSpec((shape[0], UNIT // shape[0], features), lambda i, *_: (0, i, 0))
        if shape[0] == 16:
            return pl.BlockSpec(shape, lambda i, *_: (0, 0))
        if shape[0] == features:
            return pl.BlockSpec((features, UNIT), lambda i, *_: (0, i))
        return pl.BlockSpec((UNIT, shape[1]), lambda i, *_: (i, 0))

    return pl.pallas_call(
        functools.partial(kernel, staged),
        out_shape=[pinned(*o) for o in outs],
        grid_spec=pltpu.PrefetchScalarGridSpec(
            num_scalar_prefetch=2,
            grid=(slots // UNIT,),
            in_specs=[spec(v.shape) for v in tiles]
            + [pl.BlockSpec((16, features), lambda i, *_: (0, 0))]
            + [pl.BlockSpec(memory_space=pl.ANY)] * (1 + len(pieces)),
            out_specs=[spec(o[0]) for o in outs],
            scratch_shapes=[
                pltpu.VMEM((features // 128, UNIT, 128), F32),
                pltpu.VMEM((features, features), BF),
                pltpu.VMEM((features, hidden), BF),
                pltpu.VMEM((hidden, features), BF),
                pltpu.SemaphoreType.DMA((3,)),
            ],
        ),
        name=name,
        cost_estimate=BRIEF,
        compiler_params=pltpu.CompilerParams(
            dimension_semantics=("arbitrary",), vmem_limit_bytes=56 * MIB
        ),
    )(place, table, *map(hbm, tiles), hbm(vectors), hbm(down_w), *map(hbm, pieces))


def rows_forward(place, table, heads, x, pieces, down_w, vectors, peers, staged):
    slots, features = x.shape
    hidden = down_w.shape[0]
    outs = [
        ((peers, slots // peers, features), BF),
        ((slots, hidden), BF),
        ((slots, hidden), BF),
        ((features, slots), BF),
        ((slots, features), F32),
        ((slots, features), F32),
    ]
    return over_rows(
        rows_forward_kernel, "rows_forward", place, table, [heads, x], vectors, down_w, pieces, outs, staged
    )


def rows_backward(place, table, z1, z2, cot, slope, pieces, down_w, vectors, staged):
    slots, features = z1.shape
    hidden = down_w.shape[0]
    outs = [
        ((slots, hidden), BF),
        ((slots, features), BF),
        ((slots, features), F32),
        ((slots, features), BF),
        ((slots, features), BF),
        ((16, features), F32),
    ]
    return over_rows(
        rows_backward_kernel,
        "rows_backward",
        place,
        table,
        [z1, z2, cot, slope],
        vectors,
        down_w,
        pieces,
        outs,
        staged,
    )


def down_grad_kernel(cols_ref, g_ref, out_ref):
    out_ref[...] = tn(cols_ref[...], g_ref[...]).astype(BF)


def down_gradient(act, gffn):
    slots, hidden = act.shape
    features = gffn.shape[1]
    return pl.pallas_call(
        down_grad_kernel,
        out_shape=pinned((hidden, features), BF),
        grid=(hidden // features,),
        in_specs=[
            pl.BlockSpec((slots, features), lambda k: (0, k)),
            pl.BlockSpec((slots, features), lambda k: (0, 0)),
        ],
        out_specs=pl.BlockSpec((features, features), lambda k: (k, 0)),
        name="down_gradient",
        cost_estimate=pl.CostEstimate(
            flops=3 * 10**9, transcendentals=0, bytes_accessed=9 * MIB
        ),
        compiler_params=pltpu.CompilerParams(
            dimension_semantics=("arbitrary",), vmem_limit_bytes=40 * MIB
        ),
    )(hbm(act), hbm(gffn))


def up_grad_kernel(first, place_ref, turned_ref, g_ref, heads_ref, gbranch_ref, keep_ref, send_ref, full_ref):
    step = pl.program_id(0) + first

    @pl.when(step < 4)
    def _():
        full_ref[...] = nn(turned_ref[...], g_ref[...])

    @pl.when(step == 4)
    def _():
        full_ref[...] = nn(heads_ref[...], gbranch_ref[...])

    def put(ref, k, value):
        ref[k, 0] = value

    cut_rows(place_ref, full_ref, keep_ref, send_ref, put)


def up_gradient(place, nlow_t, gpre, heads_t, gbranch, first, blocks):
    features, slots = nlow_t.shape
    rows = features // 8
    cut = pinned((4, blocks, rows, features), BF)

    def whole(shape):
        return pl.BlockSpec(shape, lambda j, *_: (0, 0))

    return pl.pallas_call(
        functools.partial(up_grad_kernel, first),
        out_shape=[cut, cut],
        grid_spec=pltpu.PrefetchScalarGridSpec(
            num_scalar_prefetch=1,
            grid=(blocks,),
            in_specs=[
                whole((features, slots)),
                pl.BlockSpec((slots, features), lambda j, *_: (0, jnp.minimum(j + first, 3))),
                whole((features, slots)),
                whole((slots, features)),
            ],
            out_specs=[pl.BlockSpec((4, 1, rows, features), lambda j, *_: (0, j, 0, 0))] * 2,
            scratch_shapes=[pltpu.VMEM((features, features), F32)],
        ),
        name="up_gradient",
        cost_estimate=BRIEF,
        compiler_params=pltpu.CompilerParams(
            dimension_semantics=("arbitrary",), vmem_limit_bytes=40 * MIB
        ),
    )(place, *map(hbm, (nlow_t, gpre, heads_t, gbranch)))


def cut_rows(place_ref, full_ref, keep_ref, send_ref, at):
    rows = full_ref.shape[0] // 8
    for k in range(4):
        plane = (place_ref[0] >> 3) ^ k
        core = (place_ref[0] >> 2) & 1
        for swap, ref in ((0, keep_ref), (1, send_ref)):
            first = (plane * 2 + (core ^ swap)) * rows
            at(ref, k, full_ref[pl.ds(pl.multiple_of(first, 8), rows), :].astype(BF))


def attend_backward_kernel(
    staged,
    place_ref,
    tab_ref,
    qkv_ref,
    gh_ref,
    total_ref,
    xt_ref,
    terms_in_ref,
    g_ref,
    keep_ref,
    send_a_ref,
    send_b_ref,
    terms_ref,
    dk_ref,
    dv_ref,
    full_ref,
    kt_ref,
    gq_ref,
):
    group = pl.program_id(0)
    kind = tab_ref[0]
    slots, width = gh_ref.shape
    low = lax.broadcasted_iota(jnp.int32, (UNIT, 2 * HD), 1) < HD

    dk_ref[...] = jnp.zeros_like(dk_ref)
    dv_ref[...] = jnp.zeros_like(dv_ref)

    for unit in range(4):
        kt_ref[unit] = qkv_ref[1, unit * UNIT : (unit + 1) * UNIT, :].T

    def units(first_unit, count, keys):
        heads = width // HD
        tasks = [(first_unit + u, side) for u in range(count) for side in range(heads)]

        def places(which, side):
            first = tab_ref[1 + (group * heads + side) * 4 + which]
            return (
                first,
                slice(side // 2 * 2 * HD, (side // 2 + 1) * 2 * HD),
                pl.ds(pl.multiple_of(which * UNIT, UNIT), UNIT),
                pl.ds(pl.multiple_of(first * UNIT, UNIT), keys),
                low if side % 2 == 0 else ~low,
            )

        def lead(which, side):
            first, lanes, rows, key_rows, mine = places(which, side)
            own = jnp.where(mine, qkv_ref[0, rows, lanes], jnp.zeros((), BF))
            gown = jnp.where(mine, gh_ref[rows, lanes], jnp.zeros((), BF))
            return nt(qkv_ref[1, key_rows, lanes], own), nt(qkv_ref[2, key_rows, lanes], gown)

        def middle(which, side, scores, gprobs):
            probs = jnp.exp(scores - total_ref[side, which])
            inner = jnp.sum(gprobs * probs, axis=0, keepdims=True)
            return probs.astype(BF), (probs * (gprobs - inner)).astype(BF)

        def trail(which, side, probs, gscores):
            first, lanes, rows, key_rows, mine = places(which, side)
            own = jnp.where(mine, qkv_ref[0, rows, lanes], jnp.zeros((), BF))
            gown = jnp.where(mine, gh_ref[rows, lanes], jnp.zeros((), BF))
            dv_ref[key_rows, lanes] += nn(probs, gown)
            dk_ref[key_rows, lanes] += nn(gscores, own)
            part = sum(
                nn(
                    kt_ref[first + j, side * HD : (side + 1) * HD, :],
                    gscores[j * UNIT : (j + 1) * UNIT, :],
                )
                for j in range(keys // UNIT)
            )
            gq_ref[side * HD : (side + 1) * HD, :] = (part * HD**-0.5).astype(BF)
            if side == heads - 1:
                g_ref[0, rows, :] = gq_ref[...].T

        ahead, ready = lead(*tasks[0]), None
        for i, task in enumerate(tasks):
            now = ahead
            if i + 1 < len(tasks):
                ahead = lead(*tasks[i + 1])
            fresh = middle(*task, *now)
            if ready is not None:
                trail(*tasks[i - 1], *ready)
            ready = fresh
        trail(*tasks[-1], *ready)

    @pl.when(kind == 2)
    def _():
        lax.fori_loop(0, 1, lambda w, c: (units(w * 4, 4, 2 * UNIT), c)[1], 0)

    @pl.when(kind == 1)
    def _():
        lax.fori_loop(0, 1, lambda w, c: (units(w * 3, 3, UNIT), c)[1], 0)
        g_ref[0, 3 * UNIT :, :] = jnp.zeros((slots - 3 * UNIT, width), BF)

    @pl.when(kind == 0)
    def _():
        g_ref[0] = jnp.zeros((slots, width), BF)

    g_ref[1] = dk_ref[...].astype(BF)
    g_ref[2] = dv_ref[...].astype(BF)
    terms_ref[...] = terms_in_ref[...]
    terms_ref[0:1, :] = jnp.sum(g_ref[0].astype(F32), axis=0, keepdims=True)
    terms_ref[1:2, :] = jnp.sum(g_ref[2].astype(F32), axis=0, keepdims=True)
    for n in range(3):
        if not staged:
            keep_ref[n] = nn(xt_ref[...], g_ref[n]).astype(BF)
            continue
        full_ref[...] = nn(xt_ref[...], g_ref[n])
        rows = full_ref.shape[0] // 8

        def put(ref, k, value):
            if ref is keep_ref:
                keep_ref[k, n] = value
            else:
                at = ((k % 2) * 3 + n) * rows
                (send_a_ref if k < 2 else send_b_ref)[at : at + rows, :] = value

        cut_rows(place_ref, full_ref, keep_ref, None, put)
    if staged:
        send_b_ref[6 * rows :, :] = terms_ref[...].astype(BF)


def attend_backward(place, table, qkv, gheads, log_total, xt, terms, staged):
    _, slots, features = qkv.shape
    width = 4 * HD
    if staged:
        cut = pinned((4, 3, features // 8, features), BF)
        cut_spec = pl.BlockSpec((4, 3, features // 8, width), lambda g, *_: (0, 0, 0, g))
        heights = (6 * features // 8, 6 * features // 8 + 16)
    else:
        heights = (16, 16)
        cut = pinned((3, features, features), BF)
        cut_spec = pl.BlockSpec((3, features, width), lambda g, *_: (0, 0, g))
    grid_spec = pltpu.PrefetchScalarGridSpec(
        num_scalar_prefetch=2,
        grid=(features // width,),
        in_specs=[
            pl.BlockSpec((3, slots, width), lambda g, *_: (0, 0, g)),
            pl.BlockSpec((slots, width), lambda g, *_: (0, g)),
            pl.BlockSpec((4, 4, 1, UNIT), lambda g, *_: (g, 0, 0, 0)),
            pl.BlockSpec((features, slots), lambda g, *_: (0, 0)),
            pl.BlockSpec((16, width), lambda g, *_: (0, g)),
        ],
        out_specs=[
            pl.BlockSpec((3, slots, width), lambda g, *_: (0, 0, g)),
            cut_spec,
            *[pl.BlockSpec((h, width), lambda g, *_: (0, g)) for h in heights],
            pl.BlockSpec((16, width), lambda g, *_: (0, g)),
        ],
        scratch_shapes=[
            pltpu.VMEM((slots, width), F32),
            pltpu.VMEM((slots, width), F32),
            pltpu.VMEM((features, width), F32),
            pltpu.VMEM((4, width, UNIT), BF),
            pltpu.VMEM((width, UNIT), BF),
        ],
    )
    return pl.pallas_call(
        functools.partial(attend_backward_kernel, staged),
        out_shape=(
            pinned((3, slots, features), BF),
            cut,
            *[pinned((h, features), BF) for h in heights],
            pinned((16, features), F32),
        ),
        grid_spec=grid_spec,
        name="attend_backward",
        cost_estimate=BRIEF,
        compiler_params=pltpu.CompilerParams(
            dimension_semantics=("arbitrary",), vmem_limit_bytes=48 * MIB
        ),
    )(place, table, *map(hbm, (qkv, gheads, log_total, xt, terms)))


def chip_sums_kernel(keep_a_ref, got_a_ref, keep_b_ref, got_b_ref, *out_refs):
    for k in range(4):
        at = 0
        for keep_ref, got_ref in ((keep_a_ref, got_a_ref), (keep_b_ref, got_b_ref)):
            rows = keep_ref.shape[2]
            for j in range(keep_ref.shape[1]):

                @pl.when(pl.program_id(0) == k)
                def _():
                    out_refs[k][at : at + rows, :] = (
                        keep_ref[0, j].astype(F32) + got_ref[0, j].astype(F32)
                    ).astype(BF)

                at += rows


def chip_sums(*parts):
    blocks, rows, features = parts[0].shape[1] + parts[2].shape[1], *parts[0].shape[2:]
    return pl.pallas_call(
        chip_sums_kernel,
        out_shape=[pinned((blocks * rows, features), BF)] * 4,
        grid=(4,),
        in_specs=[pl.BlockSpec((1, *p.shape[1:]), lambda k: (k, 0, 0, 0)) for p in parts],
        out_specs=[pl.BlockSpec((blocks * rows, features), lambda k: (0, 0))] * 4,
        name="chip_sums",
        cost_estimate=BRIEF,
        compiler_params=pltpu.CompilerParams(vmem_limit_bytes=24 * MIB),
    )(*map(hbm, parts))


def chip_sums_q_kernel(keep_ref, got_a_ref, got_b_ref, terms_ref, *out_refs):
    rows = keep_ref.shape[2]
    terms = (terms_ref[...] + got_b_ref[6 * rows :, :].astype(F32)).astype(BF)
    for k in range(4):
        got_ref = got_a_ref if k < 2 else got_b_ref
        for n in range(3):
            at = ((k % 2) * 3 + n) * rows
            out_refs[k][n * rows : (n + 1) * rows, :] = (
                keep_ref[k, n].astype(F32) + got_ref[at : at + rows, :].astype(F32)
            ).astype(BF)
        out_refs[k][3 * rows :, :] = terms


def chip_sums_q(keep, got_a, got_b, terms):
    rows, features = keep.shape[2:]
    return pl.pallas_call(
        chip_sums_q_kernel,
        out_shape=[pinned((3 * rows + 16, features), BF)] * 4,
        grid=(1,),
        in_specs=[
            pl.BlockSpec(v.shape, lambda i, n=v.ndim: (0,) * n) for v in (keep, got_a, got_b, terms)
        ],
        out_specs=[pl.BlockSpec((3 * rows + 16, features), lambda i: (0, 0))] * 4,
        name="chip_sums_q",
        cost_estimate=BRIEF,
        compiler_params=pltpu.CompilerParams(vmem_limit_bytes=32 * MIB),
    )(hbm(keep), hbm(got_a), hbm(got_b), hbm(terms))


def plane_sums_kernel(pieces, place_ref, a_ref, b_ref, c_ref, d_ref, *refs):
    out_refs, full_ref = refs[:-1], refs[-1]
    each = 4 // len(out_refs)
    height = out_refs[0].shape[0] // each
    full_ref[...] = (
        a_ref[...].astype(F32)
        + b_ref[...].astype(F32)
        + c_ref[...].astype(F32)
        + d_ref[...].astype(F32)
    )
    rep = place_ref[0] & 3
    for k in range(4):
        for base, rows, at in pieces:
            first = base + (rep ^ k) * rows if rows else base
            rows = rows or 16
            at = at + (k % each) * height
            out_refs[k // each][at : at + rows, :] = full_ref[
                pl.ds(pl.multiple_of(first, 8), rows), :
            ].astype(BF)


def plane_sums(place, parts, pieces, height, arrays=4):
    rows, features = parts[0].shape
    return pl.pallas_call(
        functools.partial(plane_sums_kernel, pieces),
        out_shape=[pinned((height * 4 // arrays, features), BF)] * arrays,
        grid_spec=pltpu.PrefetchScalarGridSpec(
            num_scalar_prefetch=1,
            grid=(1,),
            in_specs=[pl.BlockSpec((rows, features), lambda i, *_: (0, 0))] * 4,
            out_specs=[pl.BlockSpec((height * 4 // arrays, features), lambda i, *_: (0, 0))] * arrays,
            scratch_shapes=[pltpu.VMEM((rows, features), F32)],
        ),
        name="plane_sums",
        cost_estimate=BRIEF,
        compiler_params=pltpu.CompilerParams(vmem_limit_bytes=32 * MIB),
    )(place, *map(hbm, parts))


def input_grad_kernel(tab_ref, gres_ref, g_ref, w_ref, out_ref):
    kind = tab_ref[0]
    live = jnp.where(kind == 2, 4, jnp.where(kind == 1, 3, 0))
    tile = pl.program_id(0)

    @pl.when(tile < live)
    def _():
        total = gres_ref[...]
        for n in range(3):
            total = total + nt(g_ref[n], w_ref[n])
        out_ref[...] = total

    @pl.when(tile >= live)
    def _():
        out_ref[...] = jnp.zeros_like(out_ref)


def input_gradient(table, gres, grads, qkv_w):
    slots, features = gres.shape
    grid_spec = pltpu.PrefetchScalarGridSpec(
        num_scalar_prefetch=1,
        grid=(slots // UNIT,),
        in_specs=[
            pl.BlockSpec((UNIT, features), lambda i, *_: (i, 0)),
            pl.BlockSpec((3, UNIT, features), lambda i, *_: (0, i, 0)),
            pl.BlockSpec((3, features, features), lambda i, *_: (0, 0, 0)),
        ],
        out_specs=pl.BlockSpec((UNIT, features), lambda i, *_: (i, 0)),
    )
    return pl.pallas_call(
        input_grad_kernel,
        out_shape=pinned((slots, features), F32),
        grid_spec=grid_spec,
        name="input_gradient",
        cost_estimate=BRIEF,
        compiler_params=pltpu.CompilerParams(
            dimension_semantics=("arbitrary",), vmem_limit_bytes=40 * MIB
        ),
    )(table, hbm(gres), hbm(grads), hbm(qkv_w))


def gather_line_kernel(place_ref, *refs, blocks):
    full_ref, out_ref = refs[5], refs[4]
    rep = place_ref[0] & 3
    own = refs[0].shape[0] // blocks if refs[0].shape[0] % blocks == 0 else (refs[0].shape[0] - 16) // blocks
    for k in range(4):
        for n in range(blocks):
            full_ref[pl.ds(pl.multiple_of((n * 4 + (rep ^ k)) * own, 8), own), :] = refs[k][
                n * own : (n + 1) * own, :
            ].astype(F32)
    out_ref[: blocks * 4 * own, :] = full_ref[...].astype(BF)
    if out_ref.shape[0] > blocks * 4 * own:
        total = refs[0][blocks * own :, :].astype(F32)
        for k in (1, 2, 3):
            total = total + refs[k][blocks * own :, :].astype(F32)
        out_ref[blocks * 4 * own :, :] = total.astype(BF)


def gather_line(place, parts, blocks, extra):
    rows, features = parts[0].shape
    height = (rows - extra) * 4
    return pl.pallas_call(
        functools.partial(gather_line_kernel, blocks=blocks),
        out_shape=pinned((height + extra, features), BF),
        grid_spec=pltpu.PrefetchScalarGridSpec(
            num_scalar_prefetch=1,
            grid=(1,),
            in_specs=[pl.BlockSpec((rows, features), lambda i, *_: (0, 0))] * 4,
            out_specs=pl.BlockSpec((height + extra, features), lambda i, *_: (0, 0)),
            scratch_shapes=[pltpu.VMEM((height, features), F32)],
        ),
        name="gather_line",
        cost_estimate=BRIEF,
        compiler_params=pltpu.CompilerParams(vmem_limit_bytes=16 * MIB),
    )(place, *parts)


def from_peers_kernel(spans_ref, in_ref, rows_ref):
    peers, per_peer = in_ref.shape[:2]
    some = per_peer * 3 // 4
    for peer in range(peers):
        start = pl.multiple_of(spans_ref[peer], 32)

        @pl.when(spans_ref[peers + peer] == per_peer)
        def _():
            rows_ref[pl.ds(start, per_peer), :] = in_ref[peer]

        @pl.when(spans_ref[peers + peer] == some)
        def _():
            rows_ref[pl.ds(start, some), :] = in_ref[peer, :some, :]


def between_layouts(kernel, name, spans, x, shape):
    return pl.pallas_call(
        kernel,
        out_shape=pinned(shape, BF),
        grid_spec=pltpu.PrefetchScalarGridSpec(
            num_scalar_prefetch=1,
            grid=(1,),
            in_specs=[pl.BlockSpec(x.shape, lambda i, *_: (0,) * x.ndim)],
            out_specs=pl.BlockSpec(shape, lambda i, *_: (0,) * len(shape)),
        ),
        name=name,
        cost_estimate=BRIEF,
        compiler_params=pltpu.CompilerParams(vmem_limit_bytes=16 * MIB),
    )(spans, x)


def seq_swap(x, k):
    n = lax.axis_size("seq")
    return lax.ppermute(x, "seq", [(i, i ^ k) for i in range(n)])


def rep_swap(x, k):
    n = lax.axis_size("rep")
    return lax.ppermute(x, "rep", [(i, i ^ k) for i in range(n)])


def key_table(own_kind, perm_two, perm_three):
    quarters = jnp.arange(4)
    halves = quarters // 2
    pick_two = jnp.sum(
        jnp.where(halves[None, :, None] == jnp.arange(2)[None, None, :], perm_two[:, None, :], 0),
        axis=-1,
    )
    pick_three = jnp.sum(
        jnp.where(
            jnp.minimum(quarters, 2)[None, :, None] == jnp.arange(3)[None, None, :],
            perm_three[:, None, :],
            0,
        ),
        axis=-1,
    )
    first = jnp.where(own_kind == 2, 2 * pick_two, pick_three)
    return jnp.concatenate([own_kind.reshape(1), first.reshape(-1)]).astype(jnp.int32)


def placed(vector, rows, offset, features):
    lane = lax.broadcasted_iota(jnp.int32, (vector.shape[-1], features), 1)
    entry = lax.broadcasted_iota(jnp.int32, (vector.shape[-1], features), 0)
    return jnp.dot(vector, (lane == entry + offset).astype(BF), preferred_element_type=F32)


def shards(
    inputs,
    item_kind,
    perm_two,
    perm_three,
    qkv_weight,
    qv_bias,
    out_weight,
    out_bias,
    up_weight,
    up_bias,
    down_weight,
    down_bias,
    norm_gain,
    norm_bias,
    cotangent,
):
    peers = lax.axis_size("seq")
    copies = lax.axis_size("rep")
    seq = lax.axis_index("seq")
    rep = lax.axis_index("rep")
    x = inputs[0]
    slots, features = x.shape
    tokens = cotangent.shape[1]
    hidden = up_weight.shape[1]
    quarter = slots // 4
    per_peer = slots // peers
    staged = peers == 8 and copies == 4
    own = out_weight.shape[0]

    kind_row = item_kind[0]
    own_kind = jnp.sum(jnp.where(jnp.arange(peers) == seq, kind_row, 0))

    per_pair = (
        jnp.where(kind_row == 2, 4 * quarter, jnp.where(kind_row == 1, 3 * quarter, 0)) // peers
    )
    earlier = jnp.arange(peers)[:, None] < jnp.arange(peers)[None, :]
    range_starts = jnp.sum(jnp.where(earlier, per_pair[:, None], 0), axis=0)
    spans = jnp.concatenate([range_starts, per_pair]).astype(jnp.int32)
    own_start = jnp.sum(jnp.where(jnp.arange(peers) == seq, range_starts, 0))
    table = jnp.concatenate(
        [
            key_table(own_kind, perm_two, perm_three),
            (own_start // (UNIT // peers)).astype(jnp.int32).reshape(1),
        ]
    )

    place = (seq * copies + rep).astype(jnp.int32).reshape(1)
    index = seq * copies + rep
    core, plane = seq & 1, seq >> 1
    fan = 4 * own
    up_row = (index * fan) // features
    together = lax.optimization_barrier

    def swap_rows(rows):
        return lax.all_to_all(rows, "seq", split_axis=0, concat_axis=0, tiled=True)

    turned = x.T
    if staged:
        down_w = lax.all_gather(down_weight, AXES, axis=0, tiled=True)

        def along_rep(piece):
            return [piece] + [rep_swap(piece, k) for k in (1, 2, 3)]

        def along_plane(piece):
            return [piece] + [seq_swap(piece, 2 * k) for k in (1, 2, 3)]

        def both_cores(parts):
            return parts + [seq_swap(p, 1) for p in parts]

        small = jnp.concatenate([qv_bias, out_bias[None], down_bias[None], norm_gain, norm_bias])
        small = placed(small, 8, index * own, features)
        spread = placed(up_bias[None], 1, index * fan - up_row * features, features)
        spread = jnp.where(jnp.arange(4)[:, None] == up_row, spread, 0.0)
        vectors = jnp.concatenate(
            [small[0:3], spread, small[3:8], jnp.zeros((4, features), F32)]
        ).astype(BF)

        first = along_rep(jnp.concatenate([qkv_weight.reshape(3 * own, features), vectors]))
        second = jnp.concatenate(
            [out_weight] + [up_weight[:, c : c + features] for c in range(0, hidden, features)]
        )
        near = rep_swap(second, 1)
        turned, near, table, spans, *first = together((turned, near, table, spans, *first))
        first = gather_line(place, first, 3, 16)
        pair = jnp.concatenate([second, near])
        pair, first = together((pair, first))
        far = rep_swap(pair, 2)
        first = along_plane(first)
        second = gather_line(place, [pair[: 5 * own], pair[5 * own :], far[: 5 * own], far[5 * own :]], 5, 0)
        own_blocks = second
        second = along_plane(second)
        cot, own_blocks, *first = together((cotangent[0], own_blocks, *first))
        cot = lax.all_gather(cot, "seq", axis=0)
        first = both_cores(first)
        vectors = sum(p[12 * own :].astype(F32) for p in first)
        qkv, heads, heads_t, log_total, qkv_w = attend_forward(place, table, x, first, vectors)
        heads, *second = together((heads, *second))
        pieces = both_cores(second)
    else:

        def gathered(v, axis):
            return lax.all_gather(v, AXES, axis=axis, tiled=True)

        qkv_all = gathered(qkv_weight, 1)
        pieces = [gathered(out_weight, 0), gathered(up_weight, 0)]
        down_w = gathered(down_weight, 0)
        vectors = jnp.concatenate(
            [
                gathered(qv_bias, 1),
                gathered(out_bias, 0)[None],
                gathered(up_bias, 0).reshape(4, features),
                gathered(down_bias, 0)[None],
                gathered(norm_gain, 1),
                gathered(norm_bias, 1),
                jnp.zeros((4, features), BF),
            ]
        ).astype(F32)
        cot = lax.all_gather(cotangent[0], "seq", axis=0)
        qkv, heads, heads_t, log_total, qkv_w = attend_forward(place, table, x, [qkv_all], vectors)

    out, act, slope, nlow_t, z1, z2 = rows_forward(
        place, table, heads, x, pieces, down_w, vectors, peers, staged
    )
    moved = swap_rows(out)
    z1, cot = together((z1, cot))
    gpre, gffn, gres, gbranch, gheads, terms = rows_backward(
        place, table, z1, z2, cot, slope, pieces, down_w, vectors, staged
    )
    gffn, moved = together((gffn, moved))

    if staged:

        def over_plane(parts):
            return [parts[0]] + [seq_swap(parts[k], 2 * k) for k in (1, 2, 3)]

        def over_rep(parts):
            return [parts[0]] + [rep_swap(parts[k], k) for k in (1, 2, 3)]

        def total_of(parts):
            total = parts[0].astype(F32)
            for p in parts[1:]:
                total = total + p.astype(F32)
            return total

        down_grad = down_gradient(act, gffn)
        down_out = lax.psum_scatter(down_grad, AXES, scatter_dimension=0, tiled=True).astype(F32)
        gpre, down_grad = together((gpre, down_grad))
        keep_a, send_a = up_gradient(place, nlow_t, gpre, heads_t, gbranch, 0, 3)
        got_a = seq_swap(send_a, 1)
        gbranch, keep_a = together((gbranch, keep_a))
        keep_b, send_b = up_gradient(place, nlow_t, gpre, heads_t, gbranch, 3, 2)
        got_b = seq_swap(send_b, 1)
        output = between_layouts(from_peers_kernel, "from_peers", spans, moved, (tokens, features))
        got_a, got_b, output = together((got_a, got_b, output))
        parts = chip_sums(keep_a, got_a, keep_b, got_b)
        gheads, *parts = together((gheads, *parts))
        parts = over_plane(parts)
        grads, keep_q, send_a, send_b, terms = attend_backward(
            place, table, qkv, gheads, log_total, turned, terms, staged
        )
        send_a, send_b, *parts = together((send_a, send_b, *parts))
        got_a, got_b = seq_swap(send_a, 1), seq_swap(send_b, 1)
        parts_q = chip_sums_q(keep_q, got_a, got_b, terms)
        grads, *parts_q = together((grads, *parts_q))
        parts_q = over_plane(parts_q)
        input_grad = input_gradient(table, gres, grads, qkv_w)
        input_grad, *parts = together((input_grad, *parts))
        pieces = [(4 * own * j, own, own * j) for j in range(5)]
        height = 5 * own
        near, far = plane_sums(place, parts, pieces, height, 2)
        far = rep_swap(far, 2)
        near, *parts_q = together((near, *parts_q))
        pieces = [(4 * own * n, own, own * n) for n in range(3)] + [(12 * own, 0, 3 * own)]
        parts_q = over_rep(plane_sums(place, parts_q, pieces, 3 * own + 16))
        near = near.astype(F32) + far.astype(F32)
        far = rep_swap(near[height:].astype(BF), 1)
        total = near[:height] + far.astype(F32)
        up_out = jnp.concatenate([total[own * j : own * (j + 1)] for j in range(4)], axis=1)
        out_out = total[4 * own :]
        last = total_of(parts_q)
        qkv_out = last[: 3 * own].reshape(3, own, features)
        sums = last[3 * own :]
        mine = lax.dynamic_slice(sums, (0, index * own), (16, own))
        up_bias_out = lax.dynamic_slice(
            sums, (3 + up_row, index * fan - up_row * features), (1, fan)
        )[0]
        qv_out, out_bias_out, down_bias_out = mine[0:2], mine[2], mine[7]
        gain_out, shift_out = mine[8:10], mine[10:12]
    else:

        def reduced(v, axis):
            return lax.psum_scatter(v.astype(F32), AXES, scatter_dimension=axis, tiled=True)

        grads, qkv_grad, _, _, terms = attend_backward(
            place, table, qkv, gheads, log_total, turned, terms, staged
        )
        input_grad = input_gradient(table, gres, grads, qkv_w)
        down_out = reduced(tn(act, gffn), 0)
        up_out = reduced(nn(nlow_t, gpre), 0)
        out_out = reduced(nn(heads_t, gbranch), 0)
        qkv_out = reduced(qkv_grad, 1)
        qv_out = reduced(terms[0:2], 1)
        out_bias_out = reduced(terms[2], 0)
        up_bias_out = reduced(terms[3:7].reshape(hidden), 0)
        down_bias_out = reduced(terms[7], 0)
        gain_out = reduced(terms[8:10], 1)
        shift_out = reduced(terms[10:12], 1)
        positions = jnp.arange(tokens)
        ends = range_starts + per_pair
        sources = jnp.sum((ends[None, :] <= positions[:, None]).astype(jnp.int32), axis=1)
        opening = jnp.sum(
            jnp.where(jnp.arange(peers)[None, :] == sources[:, None], range_starts[None, :], 0),
            axis=1,
        )
        arrivals = sources * per_peer + positions - opening
        output = moved.reshape(slots, features)[arrivals]

    return (
        output[None],
        input_grad[None],
        qkv_out,
        qv_out,
        out_out,
        out_bias_out,
        up_out,
        up_bias_out,
        down_out,
        down_bias_out,
        gain_out,
        shift_out,
    )


def solution(mesh):
    both = ("seq", "rep")
    in_specs = (
        P("rep", "seq", None),
        P("rep", None),
        P(),
        P(),
        P(None, both, None),
        P(None, both),
        P(both, None),
        P(both),
        P(both, None),
        P(both),
        P(both, None),
        P(both),
        P(None, both),
        P(None, both),
        P("rep", "seq", None),
    )
    out_specs = (
        P("rep", "seq", None),
        P("rep", "seq", None),
        P(None, both, None),
        P(None, both),
        P(both, None),
        P(both),
        P(both, None),
        P(both),
        P(both, None),
        P(both),
        P(None, both),
        P(None, both),
    )
    return jax.shard_map(shards, mesh=mesh, in_specs=in_specs, out_specs=out_specs, check_vma=False)
```

```python
import functools

import jax
import jax.numpy as jnp
from jax import lax
from jax.experimental import pallas as pl
from jax.experimental.pallas import tpu as pltpu
from jax.sharding import PartitionSpec as P

HD = 64
CHUNK = 256
UNIT = 256
EPSILON = 1e-05
BF = jnp.bfloat16
F32 = jnp.float32
AXES = ("seq", "rep")
MIB = 1 << 20
BRIEF = pl.CostEstimate(flops=1000, transcendentals=0, bytes_accessed=1000)


def hbm(x):
    return pltpu.with_memory_space_constraint(x, pltpu.HBM)


def pinned(shape, dtype):
    return pltpu.HBM(shape, dtype)


TAIL_P = 0.4 * 0.7071067811865476
TAIL_C = tuple(
    0.5 * c
    for c in (
        0.23192178895457838,
        0.16182559848968434,
        0.46826879780965075,
        -0.3709009174795544,
        0.7091427810415396,
        -0.20025807634318435,
    )
)
BELL = -0.7213475204444817
RSQRT2PI = 0.3989422804014327


def nn(a, b):
    return lax.dot_general(a, b, (((1,), (0,)), ((), ())), preferred_element_type=F32)


def nt(a, b):
    return lax.dot_general(a, b, (((1,), (1,)), ((), ())), preferred_element_type=F32)


def tn(a, b):
    return lax.dot_general(a, b, (((0,), (0,)), ((), ())), preferred_element_type=F32)


def gelu_parts(x):
    t = 1.0 / (1.0 + TAIL_P * jnp.abs(x))
    poly = TAIL_C[-1] * t + TAIL_C[-2]
    for c in TAIL_C[-3::-1]:
        poly = poly * t + c
    bell = jnp.exp2(x * x * BELL)
    tail = poly * t * bell
    phi = jnp.where(x >= 0, 1.0 - tail, tail)
    return x * phi, phi + x * bell * RSQRT2PI


def start_pieces(place_ref, refs, copies, sem):
    for swap in range(2):
        for plane in range(4):
            device = (place_ref[0] >> 2) ^ (plane * 2 + swap)
            for first, rows, target in copies:
                pltpu.make_async_copy(
                    refs[swap * 4 + plane].at[pl.ds(first, rows), :], target(device), sem
                ).start()


def wait_whole(ref, sem):
    pltpu.make_async_copy(ref, ref, sem).wait()


def attend_forward_kernel(
    staged, place_ref, tab_ref, x_ref, b_ref, *refs
):
    count = 8 if staged else 1
    pieces = refs[:count]
    qkv_ref, heads_ref, turned_ref, total_ref, keep_ref = refs[count : count + 5]
    w_ref, vt_ref, sem, keep_sem = refs[count + 5 :]
    group = pl.program_id(0)
    kind = tab_ref[0]
    slots, width = heads_ref.shape
    features = x_ref.shape[1]
    low = lax.broadcasted_iota(jnp.int32, (UNIT, 2 * HD), 1) < HD
    keep = pltpu.make_async_copy(w_ref, keep_ref, keep_sem)

    @pl.when(group == 0)
    def _():
        if staged:
            rows = features // 8

            def target(n):
                return lambda d: w_ref.at[n, pl.ds(pl.multiple_of(d * rows, 32), rows), :]

            start_pieces(
                place_ref, pieces, [(n * rows, rows, target(n)) for n in range(3)], sem
            )
        else:
            pltpu.make_async_copy(pieces[0], w_ref, sem).start()
        wait_whole(w_ref, sem)
        keep.start()

    @pl.when(group == pl.num_programs(0) - 1)
    def _():
        keep.wait()

    cols = pl.ds(pl.multiple_of(group * width, width), width)

    def project(n, bias, scale):
        weight = w_ref[n, :, cols]
        for r in range(0, slots, UNIT):
            acc = nn(x_ref[r : r + UNIT, :], weight)
            if bias is not None:
                acc = acc + bias
            acc = acc.astype(BF)
            if scale is not None:
                acc = acc * jnp.asarray(scale, BF)
            qkv_ref[n, r : r + UNIT, :] = acc

    project(0, b_ref[0:1, :], HD**-0.5)
    project(1, None, None)
    project(2, b_ref[1:2, :], None)

    for unit in range(4):
        vt_ref[unit] = qkv_ref[2, unit * UNIT : (unit + 1) * UNIT, :].T

    def units(first_unit, count, keys):
        heads = width // HD
        tasks = [(first_unit + u, side) for u in range(count) for side in range(heads)]

        def rows_of(which):
            return pl.ds(pl.multiple_of(which * UNIT, UNIT), UNIT)

        def start_of(which, side):
            return tab_ref[1 + (group * heads + side) * 4 + which]

        def score(which, side):
            lanes = slice(side // 2 * 2 * HD, (side // 2 + 1) * 2 * HD)
            key_rows = pl.ds(pl.multiple_of(start_of(which, side) * UNIT, UNIT), keys)
            mine = low if side % 2 == 0 else ~low
            own = jnp.where(mine, qkv_ref[0, rows_of(which), lanes], jnp.zeros((), BF))
            return nt(qkv_ref[1, key_rows, lanes], own)

        def soften(which, side, scores):
            largest = jnp.max(scores, axis=0, keepdims=True)
            expon = jnp.exp(scores - largest)
            total = jnp.sum(expon, axis=0, keepdims=True)
            total_ref[side, which] = largest + jnp.log(total)
            return expon.astype(BF), 1.0 / total

        def blend(which, side, expon, inverse):
            part = sum(
                nn(
                    vt_ref[start_of(which, side) + j, side * HD : (side + 1) * HD, :],
                    expon[j * UNIT : (j + 1) * UNIT, :],
                )
                for j in range(keys // UNIT)
            )
            part = (part * inverse).astype(BF)
            turned_ref[side * HD : (side + 1) * HD, rows_of(which)] = part
            if side == heads - 1:
                heads_ref[rows_of(which), :] = turned_ref[:, rows_of(which)].T

        ahead, soft = score(*tasks[0]), None
        for i, task in enumerate(tasks):
            now = ahead
            if i + 1 < len(tasks):
                ahead = score(*tasks[i + 1])
            fresh = soften(*task, now)
            if soft is not None:
                blend(*tasks[i - 1], *soft)
            soft = fresh
        blend(*tasks[-1], *soft)

    @pl.when(kind == 2)
    def _():
        lax.fori_loop(0, 1, lambda w, c: (units(w * 4, 4, 2 * UNIT), c)[1], 0)

    @pl.when(kind == 1)
    def _():
        lax.fori_loop(0, 1, lambda w, c: (units(w * 3, 3, UNIT), c)[1], 0)
        heads_ref[3 * UNIT :, :] = jnp.zeros((slots - 3 * UNIT, width), BF)
        turned_ref[:, 3 * UNIT :] = jnp.zeros((width, slots - 3 * UNIT), BF)

    @pl.when(kind == 0)
    def _():
        heads_ref[...] = jnp.zeros_like(heads_ref)
        turned_ref[...] = jnp.zeros_like(turned_ref)


def attend_forward(place, table, x, pieces, vectors):
    slots, features = x.shape
    width = 4 * HD
    staged = len(pieces) == 8
    grid_spec = pltpu.PrefetchScalarGridSpec(
        num_scalar_prefetch=2,
        grid=(features // width,),
        in_specs=[
            pl.BlockSpec((slots, features), lambda g, *_: (0, 0)),
            pl.BlockSpec((16, width), lambda g, *_: (0, g)),
        ]
        + [pl.BlockSpec(memory_space=pl.ANY)] * len(pieces),
        out_specs=[
            pl.BlockSpec((3, slots, width), lambda g, *_: (0, 0, g)),
            pl.BlockSpec((slots, width), lambda g, *_: (0, g)),
            pl.BlockSpec((width, slots), lambda g, *_: (g, 0)),
            pl.BlockSpec((4, 4, 1, UNIT), lambda g, *_: (g, 0, 0, 0)),
            pl.BlockSpec(memory_space=pl.ANY),
        ],
        scratch_shapes=[
            pltpu.VMEM((3, features, features), BF),
            pltpu.VMEM((4, width, UNIT), BF),
            pltpu.SemaphoreType.DMA(()),
            pltpu.SemaphoreType.DMA(()),
        ],
    )
    return pl.pallas_call(
        functools.partial(attend_forward_kernel, staged),
        out_shape=(
            pinned((3, slots, features), BF),
            pinned((slots, features), BF),
            pinned((features, slots), BF),
            pinned((features // HD, 4, 1, UNIT), F32),
            pinned((3, features, features), BF),
        ),
        grid_spec=grid_spec,
        name="attend_forward",
        cost_estimate=BRIEF,
        compiler_params=pltpu.CompilerParams(
            dimension_semantics=("arbitrary",), vmem_limit_bytes=48 * MIB
        ),
    )(place, table, hbm(x), vectors, *map(hbm, pieces))


def norm_forward(z):
    center = z - jnp.mean(z, axis=-1, keepdims=True)
    spread = jnp.mean(center * center, axis=-1, keepdims=True)
    scale = lax.rsqrt(spread + EPSILON)
    return center * scale, scale


def norm_backward(gx, xhat, scale):
    return (
        gx
        - jnp.mean(gx, axis=-1, keepdims=True)
        - xhat * jnp.mean(gx * xhat, axis=-1, keepdims=True)
    ) * scale


def live_tiles(tab_ref):
    kind = tab_ref[0]
    return jnp.where(kind == 2, 4, jnp.where(kind == 1, 3, 0))


def start_weights(staged, place_ref, pieces, down_ref, ow_ref, uw_ref, dw_ref, os_ref, sems):
    features = ow_ref.shape[0]
    if staged:
        rows = features // 8
        own, fan = os_ref.shape[1], dw_ref.shape[0] // os_ref.shape[0]

        def up_rows(j):
            lanes = pl.ds(j * features, features)
            return lambda d: uw_ref.at[pl.ds(pl.multiple_of(d * rows, 32), rows), lanes]

        for d in range(os_ref.shape[0]):
            at = d * (fan + own) + fan
            pltpu.make_async_copy(
                down_ref.at[pl.ds(at, own), :], os_ref.at[d], sems.at[3 + d]
            ).start()
        start_pieces(
            place_ref, pieces, [(j * rows, rows, up_rows(j)) for j in range(4)], sems.at[1]
        )
        for d in range(os_ref.shape[0]):
            pltpu.make_async_copy(
                down_ref.at[pl.ds(d * (fan + own), fan), :],
                dw_ref.at[pl.ds(d * fan, fan), :],
                sems.at[2],
            ).start()
    else:
        pltpu.make_async_copy(pieces[0], ow_ref, sems.at[0]).start()
        pltpu.make_async_copy(pieces[1], uw_ref, sems.at[1]).start()
        pltpu.make_async_copy(down_ref, dw_ref, sems.at[2]).start()


def finish_projection(staged, ow_ref, os_ref, sems):
    if not staged:
        wait_whole(ow_ref, sems.at[0])
        return
    own = os_ref.shape[1]
    for d in range(os_ref.shape[0]):
        wait_whole(os_ref.at[d], sems.at[3 + d])
    for d in range(os_ref.shape[0]):
        ow_ref[d * own : (d + 1) * own, :] = os_ref[d]


def rows_forward_kernel(staged, place_ref, tab_ref, heads_ref, x_ref, vec_ref, down_ref, *refs):
    count = 8 if staged else 2
    pieces = refs[:count]
    written = refs[count : count + 6]
    out_ref, act_ref, slope_ref, nlow_ref, z1_ref, z2_ref = written
    mixed_ref, ow_ref, uw_ref, dw_ref, os_ref, sems = refs[count + 6 :]
    tile = pl.program_id(0)
    live = live_tiles(tab_ref)
    features = x_ref.shape[1]
    hidden = uw_ref.shape[1]
    peers, levels = out_ref.shape[:2]

    @pl.when(tile >= live)
    def _():
        for ref in written:
            ref[...] = jnp.zeros_like(ref)

    @pl.when((tile == 0) & (live > 0))
    def _():
        start_weights(staged, place_ref, pieces, down_ref, ow_ref, uw_ref, dw_ref, os_ref, sems)

    @pl.when(tile < live)
    def _():
        def vec(i):
            return vec_ref[i : i + 1, :]

        def arrive(ref, i):
            pl.when(tile == 0)(lambda: wait_whole(ref, sems.at[i]))

        pl.when(tile == 0)(lambda: finish_projection(staged, ow_ref, os_ref, sems))
        z1 = x_ref[...].astype(F32) + nn(heads_ref[...], ow_ref[...]) + vec(2)
        z1_ref[...] = z1
        normed = norm_forward(z1)[0] * vec(8) + vec(10)
        nlow = normed.astype(BF)
        nlow_ref[...] = nlow.T
        chunks = [slice(c, c + CHUNK) for c in range(0, hidden, CHUNK)]

        def lead(c):
            bias = vec_ref[3 + c.start // features, c.start % features : c.start % features + CHUNK]
            return nn(nlow, uw_ref[:, c]) + bias[None, :]

        arrive(uw_ref, 1)
        arrive(dw_ref, 2)
        ahead, ready, ffn = lead(chunks[0]), None, normed + vec(7)
        for i, c in enumerate(chunks):
            now = ahead
            if i + 1 < len(chunks):
                ahead = lead(chunks[i + 1])
            active, slope = gelu_parts(now)
            active = active.astype(BF)
            act_ref[:, c] = active
            slope_ref[:, c] = slope.astype(BF)
            if ready is not None:
                ffn = ffn + nn(ready, dw_ref[chunks[i - 1], :])
            ready = active
        z2 = ffn + nn(ready, dw_ref[chunks[-1], :])
        z2_ref[...] = z2
        result = norm_forward(z2)[0] * vec(9) + vec(11)
        for j in range(features // 128):
            lanes = slice(j * 128, (j + 1) * 128)
            mixed_ref[j] = result[:, lanes]
            for peer in range(peers):
                out_ref[peer, :, lanes] = mixed_ref[j, pl.ds(peer, levels, stride=peers), :].astype(BF)


def rows_backward_kernel(
    staged, place_ref, tab_ref, z1_ref, z2_ref, cot_ref, slope_ref, vec_ref, down_ref, *refs
):
    count = 8 if staged else 2
    pieces = refs[:count]
    written = refs[count : count + 5]
    gpre_ref, gffn_ref, gres_ref, gbranch_ref, gheads_ref = written
    terms_ref, mixed_ref, ow_ref, uw_ref, dw_ref, os_ref, sems = refs[count + 5 :]
    tile = pl.program_id(0)
    live = live_tiles(tab_ref)
    features = z1_ref.shape[1]
    hidden = uw_ref.shape[1]
    peers, levels = cot_ref.shape[:2]

    @pl.when(tile == 0)
    def _():
        terms_ref[...] = jnp.zeros_like(terms_ref)

    @pl.when(tile >= live)
    def _():
        for ref in written:
            ref[...] = jnp.zeros_like(ref)

    @pl.when((tile == 0) & (live > 0))
    def _():
        start_weights(staged, place_ref, pieces, down_ref, ow_ref, uw_ref, dw_ref, os_ref, sems)

    @pl.when(tile < live)
    def _():
        def vec(i):
            return vec_ref[i : i + 1, :]

        def arrive(ref, i):
            pl.when(tile == 0)(lambda: wait_whole(ref, sems.at[i]))

        def add(i, value):
            terms_ref[i : i + 1, :] += jnp.sum(value, axis=0, keepdims=True)

        cot = []
        for j in range(features // 128):
            lanes = slice(j * 128, (j + 1) * 128)
            for peer in range(peers):
                mixed_ref[j, pl.ds(peer, levels, stride=peers), :] = cot_ref[peer, :, lanes].astype(F32)
            cot.append(mixed_ref[j])
        cot = jnp.concatenate(cot, axis=1)
        xhat2, scale2 = norm_forward(z2_ref[...])
        add(9, cot * xhat2)
        add(11, cot)
        gres2 = norm_backward(cot * vec(9), xhat2, scale2)
        gffn = gres2.astype(BF)
        gffn_ref[...] = gffn
        add(7, gffn.astype(F32))
        chunks = [slice(c, c + CHUNK) for c in range(0, hidden, CHUNK)]

        def lead(c):
            return nt(gffn, dw_ref[c, :])

        arrive(dw_ref, 2)
        arrive(uw_ref, 1)
        pl.when(tile == 0)(lambda: finish_projection(staged, ow_ref, os_ref, sems))
        ahead, ready, gmoved = lead(chunks[0]), None, gres2
        for i, c in enumerate(chunks):
            now = ahead
            if i + 1 < len(chunks):
                ahead = lead(chunks[i + 1])
            gpre = (now * slope_ref[:, c].astype(F32)).astype(BF)
            gpre_ref[:, c] = gpre
            row, lanes = 3 + c.start // features, slice(c.start % features, c.start % features + CHUNK)
            terms_ref[row : row + 1, lanes] += jnp.sum(gpre.astype(F32), axis=0, keepdims=True)
            if ready is not None:
                gmoved = gmoved + nt(ready, uw_ref[:, chunks[i - 1]])
            ready = gpre
        gmoved = gmoved + nt(ready, uw_ref[:, chunks[-1]])
        xhat1, scale1 = norm_forward(z1_ref[...])
        add(8, gmoved * xhat1)
        add(10, gmoved)
        gres1 = norm_backward(gmoved * vec(8), xhat1, scale1)
        gres_ref[...] = gres1
        gbranch = gres1.astype(BF)
        gbranch_ref[...] = gbranch
        add(2, gbranch.astype(F32))
        gheads_ref[...] = nt(gbranch, ow_ref[...]).astype(BF)


def over_rows(kernel, name, place, table, tiles, vectors, down_w, pieces, outs, staged, hidden):
    features = down_w.shape[1]
    slots = tiles[0].shape[0]
    own = down_w.shape[0] // 160 if staged else 16

    def spec(shape):
        if len(shape) == 3 and shape[0] * shape[1] != slots:
            levels = UNIT // shape[0]
            last = shape[1] // levels - 1
            return pl.BlockSpec(
                (shape[0], levels, features), lambda i, place, tab: (0, jnp.minimum(tab[49] + i, last), 0)
            )
        if len(shape) == 3:
            return pl.BlockSpec((shape[0], UNIT // shape[0], features), lambda i, *_: (0, i, 0))
        if shape[0] == 16:
            return pl.BlockSpec(shape, lambda i, *_: (0, 0))
        if shape[0] == features:
            return pl.BlockSpec((features, UNIT), lambda i, *_: (0, i))
        return pl.BlockSpec((UNIT, shape[1]), lambda i, *_: (i, 0))

    return pl.pallas_call(
        functools.partial(kernel, staged),
        out_shape=[pinned(*o) for o in outs],
        grid_spec=pltpu.PrefetchScalarGridSpec(
            num_scalar_prefetch=2,
            grid=(slots // UNIT,),
            in_specs=[spec(v.shape) for v in tiles]
            + [pl.BlockSpec((16, features), lambda i, *_: (0, 0))]
            + [pl.BlockSpec(memory_space=pl.ANY)] * (1 + len(pieces)),
            out_specs=[spec(o[0]) for o in outs],
            scratch_shapes=[
                pltpu.VMEM((features // 128, UNIT, 128), F32),
                pltpu.VMEM((features, features), BF),
                pltpu.VMEM((features, hidden), BF),
                pltpu.VMEM((hidden, features), BF),
                pltpu.VMEM((32 if staged else 1, own, features), BF),
                pltpu.SemaphoreType.DMA((3 + 32,)),
            ],
        ),
        name=name,
        cost_estimate=BRIEF,
        compiler_params=pltpu.CompilerParams(
            dimension_semantics=("arbitrary",), vmem_limit_bytes=56 * MIB
        ),
    )(place, table, *map(hbm, tiles), hbm(vectors), hbm(down_w), *map(hbm, pieces))


def rows_forward(place, table, heads, x, pieces, down_w, vectors, peers, hidden, staged):
    slots, features = x.shape
    outs = [
        ((peers, slots // peers, features), BF),
        ((slots, hidden), BF),
        ((slots, hidden), BF),
        ((features, slots), BF),
        ((slots, features), F32),
        ((slots, features), F32),
    ]
    return over_rows(
        rows_forward_kernel, "rows_forward", place, table, [heads, x], vectors, down_w, pieces, outs, staged, hidden
    )


def rows_backward(place, table, z1, z2, cot, slope, pieces, down_w, vectors, staged):
    slots, features = z1.shape
    hidden = slope.shape[1]
    outs = [
        ((slots, hidden), BF),
        ((slots, features), BF),
        ((slots, features), F32),
        ((slots, features), BF),
        ((slots, features), BF),
        ((16, features), F32),
    ]
    return over_rows(
        rows_backward_kernel,
        "rows_backward",
        place,
        table,
        [z1, z2, cot, slope],
        vectors,
        down_w,
        pieces,
        outs,
        staged,
        hidden,
    )


def down_grad_kernel(cols_ref, g_ref, out_ref):
    out_ref[...] = tn(cols_ref[...], g_ref[...]).astype(BF)


def down_gradient(act, gffn):
    slots, hidden = act.shape
    features = gffn.shape[1]
    return pl.pallas_call(
        down_grad_kernel,
        out_shape=pinned((hidden, features), BF),
        grid=(hidden // features,),
        in_specs=[
            pl.BlockSpec((slots, features), lambda k: (0, k)),
            pl.BlockSpec((slots, features), lambda k: (0, 0)),
        ],
        out_specs=pl.BlockSpec((features, features), lambda k: (k, 0)),
        name="down_gradient",
        cost_estimate=pl.CostEstimate(
            flops=3 * 10**9, transcendentals=0, bytes_accessed=9 * MIB
        ),
        compiler_params=pltpu.CompilerParams(
            dimension_semantics=("arbitrary",), vmem_limit_bytes=40 * MIB
        ),
    )(hbm(act), hbm(gffn))


def up_grad_kernel(first, place_ref, turned_ref, g_ref, heads_ref, gbranch_ref, keep_ref, send_ref, full_ref):
    step = pl.program_id(0) + first

    @pl.when(step < 4)
    def _():
        full_ref[...] = nn(turned_ref[...], g_ref[...])

    @pl.when(step == 4)
    def _():
        full_ref[...] = nn(heads_ref[...], gbranch_ref[...])

    def put(ref, k, value):
        ref[k, 0] = value

    cut_rows(place_ref, full_ref, keep_ref, send_ref, put)


def up_gradient(place, nlow_t, gpre, heads_t, gbranch, first, blocks):
    features, slots = nlow_t.shape
    rows = features // 8
    cut = pinned((4, blocks, rows, features), BF)

    def whole(shape):
        return pl.BlockSpec(shape, lambda j, *_: (0, 0))

    return pl.pallas_call(
        functools.partial(up_grad_kernel, first),
        out_shape=[cut, cut],
        grid_spec=pltpu.PrefetchScalarGridSpec(
            num_scalar_prefetch=1,
            grid=(blocks,),
            in_specs=[
                whole((features, slots)),
                pl.BlockSpec((slots, features), lambda j, *_: (0, jnp.minimum(j + first, 3))),
                whole((features, slots)),
                whole((slots, features)),
            ],
            out_specs=[pl.BlockSpec((4, 1, rows, features), lambda j, *_: (0, j, 0, 0))] * 2,
            scratch_shapes=[pltpu.VMEM((features, features), F32)],
        ),
        name="up_gradient",
        cost_estimate=BRIEF,
        compiler_params=pltpu.CompilerParams(
            dimension_semantics=("arbitrary",), vmem_limit_bytes=40 * MIB
        ),
    )(place, *map(hbm, (nlow_t, gpre, heads_t, gbranch)))


def cut_rows(place_ref, full_ref, keep_ref, send_ref, at):
    rows = full_ref.shape[0] // 8
    for k in range(4):
        plane = (place_ref[0] >> 3) ^ k
        core = (place_ref[0] >> 2) & 1
        for swap, ref in ((0, keep_ref), (1, send_ref)):
            first = (plane * 2 + (core ^ swap)) * rows
            at(ref, k, full_ref[pl.ds(pl.multiple_of(first, 8), rows), :].astype(BF))


def attend_backward_kernel(
    staged,
    place_ref,
    tab_ref,
    qkv_ref,
    gh_ref,
    total_ref,
    xt_ref,
    terms_in_ref,
    g_ref,
    keep_ref,
    send_a_ref,
    send_b_ref,
    terms_ref,
    dk_ref,
    dv_ref,
    full_ref,
    kt_ref,
    gq_ref,
):
    group = pl.program_id(0)
    kind = tab_ref[0]
    slots, width = gh_ref.shape
    low = lax.broadcasted_iota(jnp.int32, (UNIT, 2 * HD), 1) < HD

    dk_ref[...] = jnp.zeros_like(dk_ref)
    dv_ref[...] = jnp.zeros_like(dv_ref)

    for unit in range(4):
        kt_ref[unit] = qkv_ref[1, unit * UNIT : (unit + 1) * UNIT, :].T

    def units(first_unit, count, keys):
        heads = width // HD
        tasks = [(first_unit + u, side) for u in range(count) for side in range(heads)]

        def places(which, side):
            first = tab_ref[1 + (group * heads + side) * 4 + which]
            return (
                first,
                slice(side // 2 * 2 * HD, (side // 2 + 1) * 2 * HD),
                pl.ds(pl.multiple_of(which * UNIT, UNIT), UNIT),
                pl.ds(pl.multiple_of(first * UNIT, UNIT), keys),
                low if side % 2 == 0 else ~low,
            )

        def lead(which, side):
            first, lanes, rows, key_rows, mine = places(which, side)
            own = jnp.where(mine, qkv_ref[0, rows, lanes], jnp.zeros((), BF))
            gown = jnp.where(mine, gh_ref[rows, lanes], jnp.zeros((), BF))
            return nt(qkv_ref[1, key_rows, lanes], own), nt(qkv_ref[2, key_rows, lanes], gown)

        def middle(which, side, scores, gprobs):
            probs = jnp.exp(scores - total_ref[side, which])
            inner = jnp.sum(gprobs * probs, axis=0, keepdims=True)
            return probs.astype(BF), (probs * (gprobs - inner)).astype(BF)

        def trail(which, side, probs, gscores):
            first, lanes, rows, key_rows, mine = places(which, side)
            own = jnp.where(mine, qkv_ref[0, rows, lanes], jnp.zeros((), BF))
            gown = jnp.where(mine, gh_ref[rows, lanes], jnp.zeros((), BF))
            dv_ref[key_rows, lanes] += nn(probs, gown)
            dk_ref[key_rows, lanes] += nn(gscores, own)
            part = sum(
                nn(
                    kt_ref[first + j, side * HD : (side + 1) * HD, :],
                    gscores[j * UNIT : (j + 1) * UNIT, :],
                )
                for j in range(keys // UNIT)
            )
            gq_ref[side * HD : (side + 1) * HD, :] = (part * HD**-0.5).astype(BF)
            if side == heads - 1:
                g_ref[0, rows, :] = gq_ref[...].T

        ahead, ready = lead(*tasks[0]), None
        for i, task in enumerate(tasks):
            now = ahead
            if i + 1 < len(tasks):
                ahead = lead(*tasks[i + 1])
            fresh = middle(*task, *now)
            if ready is not None:
                trail(*tasks[i - 1], *ready)
            ready = fresh
        trail(*tasks[-1], *ready)

    @pl.when(kind == 2)
    def _():
        lax.fori_loop(0, 1, lambda w, c: (units(w * 4, 4, 2 * UNIT), c)[1], 0)

    @pl.when(kind == 1)
    def _():
        lax.fori_loop(0, 1, lambda w, c: (units(w * 3, 3, UNIT), c)[1], 0)
        g_ref[0, 3 * UNIT :, :] = jnp.zeros((slots - 3 * UNIT, width), BF)

    @pl.when(kind == 0)
    def _():
        g_ref[0] = jnp.zeros((slots, width), BF)

    g_ref[1] = dk_ref[...].astype(BF)
    g_ref[2] = dv_ref[...].astype(BF)
    terms_ref[...] = terms_in_ref[...]
    terms_ref[0:1, :] = jnp.sum(g_ref[0].astype(F32), axis=0, keepdims=True)
    terms_ref[1:2, :] = jnp.sum(g_ref[2].astype(F32), axis=0, keepdims=True)
    for n in range(3):
        if not staged:
            keep_ref[n] = nn(xt_ref[...], g_ref[n]).astype(BF)
            continue
        full_ref[...] = nn(xt_ref[...], g_ref[n])
        rows = full_ref.shape[0] // 8

        def put(ref, k, value):
            if ref is keep_ref:
                keep_ref[k, n] = value
            else:
                at = ((k % 2) * 3 + n) * rows
                (send_a_ref if k < 2 else send_b_ref)[at : at + rows, :] = value

        cut_rows(place_ref, full_ref, keep_ref, None, put)
    if staged:
        send_b_ref[6 * rows :, :] = terms_ref[...].astype(BF)


def attend_backward(place, table, qkv, gheads, log_total, xt, terms, staged):
    _, slots, features = qkv.shape
    width = 4 * HD
    if staged:
        cut = pinned((4, 3, features // 8, features), BF)
        cut_spec = pl.BlockSpec((4, 3, features // 8, width), lambda g, *_: (0, 0, 0, g))
        heights = (6 * features // 8, 6 * features // 8 + 16)
    else:
        heights = (16, 16)
        cut = pinned((3, features, features), BF)
        cut_spec = pl.BlockSpec((3, features, width), lambda g, *_: (0, 0, g))
    grid_spec = pltpu.PrefetchScalarGridSpec(
        num_scalar_prefetch=2,
        grid=(features // width,),
        in_specs=[
            pl.BlockSpec((3, slots, width), lambda g, *_: (0, 0, g)),
            pl.BlockSpec((slots, width), lambda g, *_: (0, g)),
            pl.BlockSpec((4, 4, 1, UNIT), lambda g, *_: (g, 0, 0, 0)),
            pl.BlockSpec((features, slots), lambda g, *_: (0, 0)),
            pl.BlockSpec((16, width), lambda g, *_: (0, g)),
        ],
        out_specs=[
            pl.BlockSpec((3, slots, width), lambda g, *_: (0, 0, g)),
            cut_spec,
            *[pl.BlockSpec((h, width), lambda g, *_: (0, g)) for h in heights],
            pl.BlockSpec((16, width), lambda g, *_: (0, g)),
        ],
        scratch_shapes=[
            pltpu.VMEM((slots, width), F32),
            pltpu.VMEM((slots, width), F32),
            pltpu.VMEM((features, width), F32),
            pltpu.VMEM((4, width, UNIT), BF),
            pltpu.VMEM((width, UNIT), BF),
        ],
    )
    return pl.pallas_call(
        functools.partial(attend_backward_kernel, staged),
        out_shape=(
            pinned((3, slots, features), BF),
            cut,
            *[pinned((h, features), BF) for h in heights],
            pinned((16, features), F32),
        ),
        grid_spec=grid_spec,
        name="attend_backward",
        cost_estimate=BRIEF,
        compiler_params=pltpu.CompilerParams(
            dimension_semantics=("arbitrary",), vmem_limit_bytes=48 * MIB
        ),
    )(place, table, *map(hbm, (qkv, gheads, log_total, xt, terms)))


def chip_sums_kernel(keep_a_ref, got_a_ref, keep_b_ref, got_b_ref, *out_refs):
    for k in range(4):
        at = 0
        for keep_ref, got_ref in ((keep_a_ref, got_a_ref), (keep_b_ref, got_b_ref)):
            rows = keep_ref.shape[2]
            for j in range(keep_ref.shape[1]):

                @pl.when(pl.program_id(0) == k)
                def _():
                    out_refs[k][at : at + rows, :] = (
                        keep_ref[0, j].astype(F32) + got_ref[0, j].astype(F32)
                    ).astype(BF)

                at += rows


def chip_sums(*parts):
    blocks, rows, features = parts[0].shape[1] + parts[2].shape[1], *parts[0].shape[2:]
    return pl.pallas_call(
        chip_sums_kernel,
        out_shape=[pinned((blocks * rows, features), BF)] * 4,
        grid=(4,),
        in_specs=[pl.BlockSpec((1, *p.shape[1:]), lambda k: (k, 0, 0, 0)) for p in parts],
        out_specs=[pl.BlockSpec((blocks * rows, features), lambda k: (0, 0))] * 4,
        name="chip_sums",
        cost_estimate=BRIEF,
        compiler_params=pltpu.CompilerParams(vmem_limit_bytes=24 * MIB),
    )(*map(hbm, parts))


def chip_sums_q_kernel(keep_ref, got_a_ref, got_b_ref, terms_ref, *out_refs):
    rows = keep_ref.shape[2]
    terms = (terms_ref[...] + got_b_ref[6 * rows :, :].astype(F32)).astype(BF)
    for k in range(4):
        got_ref = got_a_ref if k < 2 else got_b_ref
        for n in range(3):
            at = ((k % 2) * 3 + n) * rows
            out_refs[k][n * rows : (n + 1) * rows, :] = (
                keep_ref[k, n].astype(F32) + got_ref[at : at + rows, :].astype(F32)
            ).astype(BF)
        out_refs[k][3 * rows :, :] = terms


def chip_sums_q(keep, got_a, got_b, terms):
    rows, features = keep.shape[2:]
    return pl.pallas_call(
        chip_sums_q_kernel,
        out_shape=[pinned((3 * rows + 16, features), BF)] * 4,
        grid=(1,),
        in_specs=[
            pl.BlockSpec(v.shape, lambda i, n=v.ndim: (0,) * n) for v in (keep, got_a, got_b, terms)
        ],
        out_specs=[pl.BlockSpec((3 * rows + 16, features), lambda i: (0, 0))] * 4,
        name="chip_sums_q",
        cost_estimate=BRIEF,
        compiler_params=pltpu.CompilerParams(vmem_limit_bytes=32 * MIB),
    )(hbm(keep), hbm(got_a), hbm(got_b), hbm(terms))


def plane_sums_kernel(pieces, place_ref, a_ref, b_ref, c_ref, d_ref, *refs):
    out_refs, full_ref = refs[:-1], refs[-1]
    each = 4 // len(out_refs)
    height = out_refs[0].shape[0] // each
    full_ref[...] = (
        a_ref[...].astype(F32)
        + b_ref[...].astype(F32)
        + c_ref[...].astype(F32)
        + d_ref[...].astype(F32)
    )
    rep = place_ref[0] & 3
    for k in range(4):
        for base, rows, at in pieces:
            first = base + (rep ^ k) * rows if rows else base
            rows = rows or 16
            at = at + (k % each) * height
            out_refs[k // each][at : at + rows, :] = full_ref[
                pl.ds(pl.multiple_of(first, 8), rows), :
            ].astype(BF)


def plane_sums(place, parts, pieces, height, arrays=4):
    rows, features = parts[0].shape
    return pl.pallas_call(
        functools.partial(plane_sums_kernel, pieces),
        out_shape=[pinned((height * 4 // arrays, features), BF)] * arrays,
        grid_spec=pltpu.PrefetchScalarGridSpec(
            num_scalar_prefetch=1,
            grid=(1,),
            in_specs=[pl.BlockSpec((rows, features), lambda i, *_: (0, 0))] * 4,
            out_specs=[pl.BlockSpec((height * 4 // arrays, features), lambda i, *_: (0, 0))] * arrays,
            scratch_shapes=[pltpu.VMEM((rows, features), F32)],
        ),
        name="plane_sums",
        cost_estimate=BRIEF,
        compiler_params=pltpu.CompilerParams(vmem_limit_bytes=32 * MIB),
    )(place, *map(hbm, parts))


def input_grad_kernel(tab_ref, gres_ref, g_ref, w_ref, out_ref):
    kind = tab_ref[0]
    live = jnp.where(kind == 2, 4, jnp.where(kind == 1, 3, 0))
    tile = pl.program_id(0)

    @pl.when(tile < live)
    def _():
        total = gres_ref[...]
        for n in range(3):
            total = total + nt(g_ref[n], w_ref[n])
        out_ref[...] = total

    @pl.when(tile >= live)
    def _():
        out_ref[...] = jnp.zeros_like(out_ref)


def input_gradient(table, gres, grads, qkv_w):
    slots, features = gres.shape
    grid_spec = pltpu.PrefetchScalarGridSpec(
        num_scalar_prefetch=1,
        grid=(slots // UNIT,),
        in_specs=[
            pl.BlockSpec((UNIT, features), lambda i, *_: (i, 0)),
            pl.BlockSpec((3, UNIT, features), lambda i, *_: (0, i, 0)),
            pl.BlockSpec((3, features, features), lambda i, *_: (0, 0, 0)),
        ],
        out_specs=pl.BlockSpec((UNIT, features), lambda i, *_: (i, 0)),
    )
    return pl.pallas_call(
        input_grad_kernel,
        out_shape=pinned((slots, features), F32),
        grid_spec=grid_spec,
        name="input_gradient",
        cost_estimate=BRIEF,
        compiler_params=pltpu.CompilerParams(
            dimension_semantics=("arbitrary",), vmem_limit_bytes=40 * MIB
        ),
    )(table, hbm(gres), hbm(grads), hbm(qkv_w))


def gather_line_kernel(place_ref, *refs, blocks):
    full_ref, out_ref = refs[5], refs[4]
    rep = place_ref[0] & 3
    own = refs[0].shape[0] // blocks if refs[0].shape[0] % blocks == 0 else (refs[0].shape[0] - 16) // blocks
    for k in range(4):
        for n in range(blocks):
            full_ref[pl.ds(pl.multiple_of((n * 4 + (rep ^ k)) * own, 8), own), :] = refs[k][
                n * own : (n + 1) * own, :
            ].astype(F32)
    out_ref[: blocks * 4 * own, :] = full_ref[...].astype(BF)
    if out_ref.shape[0] > blocks * 4 * own:
        total = refs[0][blocks * own :, :].astype(F32)
        for k in (1, 2, 3):
            total = total + refs[k][blocks * own :, :].astype(F32)
        out_ref[blocks * 4 * own :, :] = total.astype(BF)


def gather_line(place, parts, blocks, extra):
    rows, features = parts[0].shape
    height = (rows - extra) * 4
    return pl.pallas_call(
        functools.partial(gather_line_kernel, blocks=blocks),
        out_shape=pinned((height + extra, features), BF),
        grid_spec=pltpu.PrefetchScalarGridSpec(
            num_scalar_prefetch=1,
            grid=(1,),
            in_specs=[pl.BlockSpec((rows, features), lambda i, *_: (0, 0))] * 4,
            out_specs=pl.BlockSpec((height + extra, features), lambda i, *_: (0, 0)),
            scratch_shapes=[pltpu.VMEM((height, features), F32)],
        ),
        name="gather_line",
        cost_estimate=BRIEF,
        compiler_params=pltpu.CompilerParams(vmem_limit_bytes=16 * MIB),
    )(place, *parts)


def to_peers_kernel(spans_ref, rows_ref, out_ref):
    peers, per_peer = out_ref.shape[:2]
    some = per_peer * 3 // 4
    for peer in range(peers):
        start = pl.multiple_of(spans_ref[peer], 32)

        @pl.when(spans_ref[peers + peer] == per_peer)
        def _():
            out_ref[peer] = rows_ref[pl.ds(start, per_peer), :]

        @pl.when(spans_ref[peers + peer] == some)
        def _():
            out_ref[peer, :some, :] = rows_ref[pl.ds(start, some), :]
            out_ref[peer, some:, :] = jnp.zeros_like(out_ref[peer, some:, :])

        @pl.when(spans_ref[peers + peer] == 0)
        def _():
            out_ref[peer] = jnp.zeros_like(out_ref[peer])


def from_peers_kernel(spans_ref, in_ref, rows_ref):
    peers, per_peer = in_ref.shape[:2]
    some = per_peer * 3 // 4
    for peer in range(peers):
        start = pl.multiple_of(spans_ref[peer], 32)

        @pl.when(spans_ref[peers + peer] == per_peer)
        def _():
            rows_ref[pl.ds(start, per_peer), :] = in_ref[peer]

        @pl.when(spans_ref[peers + peer] == some)
        def _():
            rows_ref[pl.ds(start, some), :] = in_ref[peer, :some, :]


def between_layouts(kernel, name, spans, x, shape):
    return pl.pallas_call(
        kernel,
        out_shape=pinned(shape, BF),
        grid_spec=pltpu.PrefetchScalarGridSpec(
            num_scalar_prefetch=1,
            grid=(1,),
            in_specs=[pl.BlockSpec(x.shape, lambda i, *_: (0,) * x.ndim)],
            out_specs=pl.BlockSpec(shape, lambda i, *_: (0,) * len(shape)),
        ),
        name=name,
        cost_estimate=BRIEF,
        compiler_params=pltpu.CompilerParams(vmem_limit_bytes=16 * MIB),
    )(spans, x)


def seq_swap(x, k):
    n = lax.axis_size("seq")
    return lax.ppermute(x, "seq", [(i, i ^ k) for i in range(n)])


def rep_swap(x, k):
    n = lax.axis_size("rep")
    return lax.ppermute(x, "rep", [(i, i ^ k) for i in range(n)])


def key_table(own_kind, perm_two, perm_three):
    quarters = jnp.arange(4)
    halves = quarters // 2
    pick_two = jnp.sum(
        jnp.where(halves[None, :, None] == jnp.arange(2)[None, None, :], perm_two[:, None, :], 0),
        axis=-1,
    )
    pick_three = jnp.sum(
        jnp.where(
            jnp.minimum(quarters, 2)[None, :, None] == jnp.arange(3)[None, None, :],
            perm_three[:, None, :],
            0,
        ),
        axis=-1,
    )
    first = jnp.where(own_kind == 2, 2 * pick_two, pick_three)
    return jnp.concatenate([own_kind.reshape(1), first.reshape(-1)]).astype(jnp.int32)


def placed(vector, rows, offset, features):
    lane = lax.broadcasted_iota(jnp.int32, (vector.shape[-1], features), 1)
    entry = lax.broadcasted_iota(jnp.int32, (vector.shape[-1], features), 0)
    return jnp.dot(vector, (lane == entry + offset).astype(BF), preferred_element_type=F32)


def shards(
    inputs,
    item_kind,
    perm_two,
    perm_three,
    qkv_weight,
    qv_bias,
    out_weight,
    out_bias,
    up_weight,
    up_bias,
    down_weight,
    down_bias,
    norm_gain,
    norm_bias,
    cotangent,
):
    peers = lax.axis_size("seq")
    copies = lax.axis_size("rep")
    seq = lax.axis_index("seq")
    rep = lax.axis_index("rep")
    x = inputs[0]
    slots, features = x.shape
    tokens = cotangent.shape[1]
    hidden = up_weight.shape[1]
    quarter = slots // 4
    per_peer = slots // peers
    staged = peers == 8 and copies == 4
    own = out_weight.shape[0]

    kind_row = item_kind[0]
    own_kind = jnp.sum(jnp.where(jnp.arange(peers) == seq, kind_row, 0))

    per_pair = (
        jnp.where(kind_row == 2, 4 * quarter, jnp.where(kind_row == 1, 3 * quarter, 0)) // peers
    )
    earlier = jnp.arange(peers)[:, None] < jnp.arange(peers)[None, :]
    range_starts = jnp.sum(jnp.where(earlier, per_pair[:, None], 0), axis=0)
    spans = jnp.concatenate([range_starts, per_pair]).astype(jnp.int32)
    own_start = jnp.sum(jnp.where(jnp.arange(peers) == seq, range_starts, 0))
    table = jnp.concatenate(
        [
            key_table(own_kind, perm_two, perm_three),
            (own_start // (UNIT // peers)).astype(jnp.int32).reshape(1),
        ]
    )

    place = (seq * copies + rep).astype(jnp.int32).reshape(1)
    index = seq * copies + rep
    core, plane = seq & 1, seq >> 1
    fan = 4 * own
    up_row = (index * fan) // features
    together = lax.optimization_barrier

    def swap_rows(rows):
        return lax.all_to_all(rows, "seq", split_axis=0, concat_axis=0, tiled=True)

    turned = x.T
    if staged:
        down_w = jnp.concatenate([down_weight, out_weight])
        down_w = lax.all_gather(down_w, AXES, axis=0, tiled=True)

        def along_rep(piece):
            return [piece] + [rep_swap(piece, k) for k in (1, 2, 3)]

        def along_plane(piece):
            return [piece] + [seq_swap(piece, 2 * k) for k in (1, 2, 3)]

        def both_cores(parts):
            return parts + [seq_swap(p, 1) for p in parts]

        small = jnp.concatenate([qv_bias, out_bias[None], down_bias[None], norm_gain, norm_bias])
        small = placed(small, 8, index * own, features)
        spread = placed(up_bias[None], 1, index * fan - up_row * features, features)
        spread = jnp.where(jnp.arange(4)[:, None] == up_row, spread, 0.0)
        vectors = jnp.concatenate(
            [small[0:3], spread, small[3:8], jnp.zeros((4, features), F32)]
        ).astype(BF)

        first = along_rep(jnp.concatenate([qkv_weight.reshape(3 * own, features), vectors]))
        second = jnp.concatenate(
            [up_weight[:, c : c + features] for c in range(0, hidden, features)]
        )
        near = rep_swap(second, 1)
        turned, near, table, spans, *first = together((turned, near, table, spans, *first))
        picked = between_layouts(
            to_peers_kernel, "to_peers", spans, cotangent[0], (peers, per_peer, features)
        )
        first = gather_line(place, first, 3, 16)
        pair = jnp.concatenate([second, near])
        pair, first = together((pair, first))
        far = rep_swap(pair, 2)
        first = along_plane(first)
        second = gather_line(place, [pair[:fan], pair[fan:], far[:fan], far[fan:]], 4, 0)
        own_blocks = second
        second = along_plane(second)
        own_blocks, *first = together((own_blocks, *first))
        first = both_cores(first)
        vectors = sum(p[12 * own :].astype(F32) for p in first)
        qkv, heads, heads_t, log_total, qkv_w = attend_forward(place, table, x, first, vectors)
        heads, picked, *second = together((heads, picked, *second))
        cot = swap_rows(picked)
        pieces = both_cores(second)
    else:

        def gathered(v, axis):
            return lax.all_gather(v, AXES, axis=axis, tiled=True)

        qkv_all = gathered(qkv_weight, 1)
        pieces = [gathered(out_weight, 0), gathered(up_weight, 0)]
        down_w = gathered(down_weight, 0)
        vectors = jnp.concatenate(
            [
                gathered(qv_bias, 1),
                gathered(out_bias, 0)[None],
                gathered(up_bias, 0).reshape(4, features),
                gathered(down_bias, 0)[None],
                gathered(norm_gain, 1),
                gathered(norm_bias, 1),
                jnp.zeros((4, features), BF),
            ]
        ).astype(F32)
        cot = lax.all_gather(cotangent[0], "seq", axis=0)
        qkv, heads, heads_t, log_total, qkv_w = attend_forward(place, table, x, [qkv_all], vectors)

    out, act, slope, nlow_t, z1, z2 = rows_forward(
        place, table, heads, x, pieces, down_w, vectors, peers, hidden, staged
    )
    moved = swap_rows(out)
    z1, cot = together((z1, cot))
    gpre, gffn, gres, gbranch, gheads, terms = rows_backward(
        place, table, z1, z2, cot, slope, pieces, down_w, vectors, staged
    )
    gffn, moved = together((gffn, moved))

    if staged:

        def over_plane(parts):
            return [parts[0]] + [seq_swap(parts[k], 2 * k) for k in (1, 2, 3)]

        def over_rep(parts):
            return [parts[0]] + [rep_swap(parts[k], k) for k in (1, 2, 3)]

        def total_of(parts):
            total = parts[0].astype(F32)
            for p in parts[1:]:
                total = total + p.astype(F32)
            return total

        down_grad = down_gradient(act, gffn)
        down_out = lax.psum_scatter(down_grad, AXES, scatter_dimension=0, tiled=True).astype(F32)
        gpre, down_grad = together((gpre, down_grad))
        keep_a, send_a = up_gradient(place, nlow_t, gpre, heads_t, gbranch, 0, 3)
        got_a = seq_swap(send_a, 1)
        gbranch, keep_a = together((gbranch, keep_a))
        keep_b, send_b = up_gradient(place, nlow_t, gpre, heads_t, gbranch, 3, 2)
        got_b = seq_swap(send_b, 1)
        output = between_layouts(from_peers_kernel, "from_peers", spans, moved, (tokens, features))
        got_a, got_b, output = together((got_a, got_b, output))
        parts = chip_sums(keep_a, got_a, keep_b, got_b)
        gheads, *parts = together((gheads, *parts))
        parts = over_plane(parts)
        grads, keep_q, send_a, send_b, terms = attend_backward(
            place, table, qkv, gheads, log_total, turned, terms, staged
        )
        send_a, send_b, *parts = together((send_a, send_b, *parts))
        got_a, got_b = seq_swap(send_a, 1), seq_swap(send_b, 1)
        parts_q = chip_sums_q(keep_q, got_a, got_b, terms)
        grads, *parts_q = together((grads, *parts_q))
        parts_q = over_plane(parts_q)
        input_grad = input_gradient(table, gres, grads, qkv_w)
        input_grad, *parts = together((input_grad, *parts))
        pieces = [(4 * own * j, own, own * j) for j in range(5)]
        height = 5 * own
        near, far = plane_sums(place, parts, pieces, height, 2)
        far = rep_swap(far, 2)
        near, *parts_q = together((near, *parts_q))
        pieces = [(4 * own * n, own, own * n) for n in range(3)] + [(12 * own, 0, 3 * own)]
        parts_q = over_rep(plane_sums(place, parts_q, pieces, 3 * own + 16))
        near = near.astype(F32) + far.astype(F32)
        far = rep_swap(near[height:].astype(BF), 1)
        total = near[:height] + far.astype(F32)
        up_out = jnp.concatenate([total[own * j : own * (j + 1)] for j in range(4)], axis=1)
        out_out = total[4 * own :]
        last = total_of(parts_q)
        qkv_out = last[: 3 * own].reshape(3, own, features)
        sums = last[3 * own :]
        mine = lax.dynamic_slice(sums, (0, index * own), (16, own))
        up_bias_out = lax.dynamic_slice(
            sums, (3 + up_row, index * fan - up_row * features), (1, fan)
        )[0]
        qv_out, out_bias_out, down_bias_out = mine[0:2], mine[2], mine[7]
        gain_out, shift_out = mine[8:10], mine[10:12]
    else:

        def reduced(v, axis):
            return lax.psum_scatter(v.astype(F32), AXES, scatter_dimension=axis, tiled=True)

        grads, qkv_grad, _, _, terms = attend_backward(
            place, table, qkv, gheads, log_total, turned, terms, staged
        )
        input_grad = input_gradient(table, gres, grads, qkv_w)
        down_out = reduced(tn(act, gffn), 0)
        up_out = reduced(nn(nlow_t, gpre), 0)
        out_out = reduced(nn(heads_t, gbranch), 0)
        qkv_out = reduced(qkv_grad, 1)
        qv_out = reduced(terms[0:2], 1)
        out_bias_out = reduced(terms[2], 0)
        up_bias_out = reduced(terms[3:7].reshape(hidden), 0)
        down_bias_out = reduced(terms[7], 0)
        gain_out = reduced(terms[8:10], 1)
        shift_out = reduced(terms[10:12], 1)
        positions = jnp.arange(tokens)
        ends = range_starts + per_pair
        sources = jnp.sum((ends[None, :] <= positions[:, None]).astype(jnp.int32), axis=1)
        opening = jnp.sum(
            jnp.where(jnp.arange(peers)[None, :] == sources[:, None], range_starts[None, :], 0),
            axis=1,
        )
        arrivals = sources * per_peer + positions - opening
        output = moved.reshape(slots, features)[arrivals]

    return (
        output[None],
        input_grad[None],
        qkv_out,
        qv_out,
        out_out,
        out_bias_out,
        up_out,
        up_bias_out,
        down_out,
        down_bias_out,
        gain_out,
        shift_out,
    )


def solution(mesh):
    both = ("seq", "rep")
    in_specs = (
        P("rep", "seq", None),
        P("rep", None),
        P(),
        P(),
        P(None, both, None),
        P(None, both),
        P(both, None),
        P(both),
        P(both, None),
        P(both),
        P(both, None),
        P(both),
        P(None, both),
        P(None, both),
        P("rep", "seq", None),
    )
    out_specs = (
        P("rep", "seq", None),
        P("rep", "seq", None),
        P(None, both, None),
        P(None, both),
        P(both, None),
        P(both),
        P(both, None),
        P(both),
        P(both, None),
        P(both),
        P(None, both),
        P(None, both),
    )
    return jax.shard_map(shards, mesh=mesh, in_specs=in_specs, out_specs=out_specs, check_vma=False)
```
